128 devices in a mesh: dp: 4 (over z), sy: 8 (over x, core), sx: 4 (over y).
Axes of the slice: x: 4, y: 4, z: 4, core: 2. Of those that a mesh axis runs over, the one named last changes fastest.
Arguments:
- input_gates: bfloat16 [4, 3, 64, 128, 1024], P('dp', None, 'sy', 'sx'), may hold values from -6 to 6
- recur_weight: bfloat16 [2304, 1024], replicated, may hold values from -0.125 to 0.125
- hidden_init: bfloat16 [4, 64, 128, 256], P('dp', 'sy', 'sx'), may hold values from -3 to 3
- cell_init: float32 [4, 64, 128, 256], P('dp', 'sy', 'sx'), may hold values from -5 to 5
- hidden_cot: bfloat16 [4, 3, 64, 128, 256], P('dp', None, 'sy', 'sx'), may hold values from -6 to 6
- frame_count: int32 [4], P('dp'), may hold values from 1 to 3, as said below
Outputs:
- hidden_seq: bfloat16 [4, 3, 64, 128, 256], P('dp', None, 'sy', 'sx')
- weight_grad: float32 [2304, 1024], P(None, ('dp', 'sy', 'sx'))
- gate_grad: bfloat16 [4, 3, 64, 128, 1024], P('dp', None, 'sy', 'sx')
- hidden_grad: bfloat16 [4, 64, 128, 256], P('dp', 'sy', 'sx')
- cell_grad: float32 [4, 64, 128, 256], P('dp', 'sy', 'sx')
The draws below stay inside these ranges and needn't reach their ends.
Inputs may be any that keep to these rules, and one draw needn't show every extreme that they name: `frame_count`: each sample's count of valid frames; some sample has all 3.
All inputs are finite; a program needn't handle non-finite values.
Results may differ from the reference program's by a relative error of at most 0.015.
Values may be sent and summed in bfloat16 or wider, within the bound.
No kernel may reach another device: no remote copies, remote signals or barrier semaphores. Data moves between devices by JAX's collectives and lax.ppermute only.
A program may use at most 64 MiB of HBM per device.

```python
import jax
import jax.numpy as jnp
from jax import lax

C = 256
FRAMES = 3
GY = 64
GX = 128
SAMPLES = 4


def draw_frame_count(key, part):
    counts = jax.random.randint(key, (SAMPLES,), 1, FRAMES + 1).astype(jnp.int32)
    chosen = jax.random.randint(jax.random.fold_in(key, 7), (), 0, SAMPLES)
    places = jnp.arange(SAMPLES, dtype=jnp.int32)
    return jnp.where(places == chosen, jnp.int32(FRAMES), counts).astype(jnp.int32)


def steps_of(rng, shape, shards, low, top_value):
    level, own = 1.0, jax.random.fold_in(rng, 6)
    for position, parts in shards:
        draws = jnp.exp(jax.random.uniform(jax.random.fold_in(own, position), (parts,), jnp.float32, low / len(shards), top_value / len(shards)))
        level = level * jnp.repeat(draws, shape[position] // parts).reshape([-1 if axis == position else 1 for axis in range(len(shape))])
    return level


def bell_draw(rng, extent, deviation, reach, pieces=(), kind=jnp.bfloat16):
    values = deviation * jax.random.normal(rng, extent, jnp.float32)
    if pieces:
        values = values * steps_of(rng, extent, pieces, -0.22, 0.18)
    return jnp.clip(values, -reach, reach).astype(kind)


def setup_inputs(seed: int = 0) -> dict:
    streams_of = jax.random.split(jax.random.key(seed), 7)
    return {
        "input_gates": bell_draw(streams_of[0], (SAMPLES, FRAMES, GY, GX, 4 * C), 1.0, 6.0, ((0, 4), (2, 8), (3, 4))),
        "recur_weight": bell_draw(streams_of[1], (9 * C, 4 * C), (9 * C) ** -0.5, 0.125),
        "hidden_init": bell_draw(streams_of[2], (SAMPLES, GY, GX, C), 0.5, 3.0, ((0, 4), (1, 8), (2, 4))),
        "cell_init": bell_draw(streams_of[3], (SAMPLES, GY, GX, C), 1.0, 5.0, ((0, 4), (1, 8), (2, 4)), jnp.float32),
        "hidden_cot": bell_draw(streams_of[4], (SAMPLES, FRAMES, GY, GX, C), 1.0, 6.0, ((0, 4), (2, 8), (3, 4))),
        "frame_count": draw_frame_count(jax.random.fold_in(streams_of[6], 71), 0),
    }


def patch_rows(padded, rows, cols, width):
    slabs = [padded[row_off:row_off + rows, col_off:col_off + cols] for row_off in range(3) for col_off in range(3)]
    return jnp.concatenate(slabs, axis=-1).reshape(rows * cols, 9 * width)


def back_conv(padded_grad, recur_weight, rows, cols, width):
    total = jnp.zeros((rows * cols, width), jnp.float32)
    for row_off in range(3):
        for col_off in range(3):
            block = row_off * 3 + col_off
            slab = padded_grad[2 - row_off:2 - row_off + rows, 2 - col_off:2 - col_off + cols].reshape(rows * cols, 4 * width)
            weight_block = recur_weight[block * width:(block + 1) * width]
            total = total + lax.dot_general(slab, weight_block, (((1,), (1,)), ((), ())), preferred_element_type=jnp.float32)
    return total


def one_sample(items):
    gates_in, hidden_start, cell_start, cot_seq, count, recur_weight = items
    rows, cols, width = GY, GX, C
    cells = rows * cols
    hidden = hidden_start.reshape(cells, width)
    cell = cell_start.reshape(cells, width)
    saved = []
    outs = []
    for frame in range(FRAMES):
        padded = jnp.pad(hidden.reshape(rows, cols, width), ((1, 1), (1, 1), (0, 0)))
        patches = patch_rows(padded, rows, cols, width)
        gates = gates_in[frame].reshape(cells, 4 * width).astype(jnp.float32) + jnp.dot(patches, recur_weight, preferred_element_type=jnp.float32)
        sig_i = jax.nn.sigmoid(gates[:, :width])
        sig_f = jax.nn.sigmoid(gates[:, width:2 * width])
        tan_g = jnp.tanh(gates[:, 2 * width:3 * width])
        sig_o = jax.nn.sigmoid(gates[:, 3 * width:])
        cell_new = sig_f * cell + sig_i * tan_g
        tan_c = jnp.tanh(cell_new)
        hidden_new = (sig_o * tan_c).astype(jnp.bfloat16)
        valid = frame < count
        saved.append((patches, cell, sig_i, sig_f, tan_g, sig_o, tan_c, valid))
        cell = jnp.where(valid, cell_new, cell)
        hidden = jnp.where(valid, hidden_new, hidden)
        outs.append(hidden.reshape(rows, cols, width))
    grad_h = jnp.zeros((cells, width), jnp.float32)
    grad_c = jnp.zeros((cells, width), jnp.float32)
    w_acc = jnp.zeros((9 * width, 4 * width), jnp.float32)
    gate_list = [None] * FRAMES
    for frame in range(FRAMES - 1, -1, -1):
        patches, cell_prev, sig_i, sig_f, tan_g, sig_o, tan_c, valid = saved[frame]
        grad_h = grad_h + cot_seq[frame].reshape(cells, width).astype(jnp.float32)
        dc_new = grad_c + grad_h * sig_o * (1.0 - tan_c * tan_c)
        d_i = dc_new * tan_g * sig_i * (1.0 - sig_i)
        d_f = dc_new * cell_prev * sig_f * (1.0 - sig_f)
        d_g = dc_new * sig_i * (1.0 - tan_g * tan_g)
        d_o = grad_h * tan_c * sig_o * (1.0 - sig_o)
        dgates = jnp.concatenate([d_i, d_f, d_g, d_o], axis=-1)
        dgates = jnp.where(valid, dgates, 0.0).astype(jnp.bfloat16)
        gate_list[frame] = dgates.reshape(rows, cols, 4 * width)
        w_acc = w_acc + lax.dot_general(patches, dgates, (((0,), (0,)), ((), ())), preferred_element_type=jnp.float32)
        padded_grad = jnp.pad(dgates.reshape(rows, cols, 4 * width), ((1, 1), (1, 1), (0, 0)))
        dh_prev = back_conv(padded_grad, recur_weight, rows, cols, width)
        grad_h = jnp.where(valid, dh_prev, grad_h)
        grad_c = jnp.where(valid, dc_new * sig_f, grad_c)
    return (jnp.stack(outs), w_acc, jnp.stack(gate_list),
            grad_h.astype(jnp.bfloat16).reshape(rows, cols, width), grad_c.reshape(rows, cols, width))


def reference(input_gates, recur_weight, hidden_init, cell_init, hidden_cot, frame_count):
    def wrapped(items):
        return one_sample(items + (recur_weight,))
    hidden_seq, w_parts, gate_grad, hidden_grad, cell_grad = lax.map(
        wrapped, (input_gates, hidden_init, cell_init, hidden_cot, frame_count))
    return hidden_seq, jnp.sum(w_parts, axis=0), gate_grad, hidden_grad, cell_grad
```

```python
import jax
import jax.numpy as jnp
from jax import lax
from jax.sharding import Mesh, PartitionSpec as P


def ring_pairs(size, phase):
    pairs = [(i, (i + 1) % size) for i in range(phase, size, 2)]
    return [edge for a, b in pairs for edge in ((a, b), (b, a))]


def with_halo(value, axis, size, dim):
    me = lax.axis_index(axis)
    odd = me % 2 == 1
    length = value.shape[dim]
    first = lax.slice_in_dim(value, 0, 1, axis=dim)
    last = lax.slice_in_dim(value, length - 1, length, axis=dim)
    near = lax.ppermute(jnp.where(odd, first, last), axis, ring_pairs(size, 0))
    far = lax.ppermute(jnp.where(odd, last, first), axis, ring_pairs(size, 1))
    before = jnp.where(me == 0, 0, jnp.where(odd, near, far))
    after = jnp.where(me == size - 1, 0, jnp.where(odd, far, near))
    return jnp.concatenate([before, value, after], axis=dim)


def patch_rows(padded, rows, cols, width):
    slabs = [
        padded[row_off : row_off + rows, col_off : col_off + cols]
        for row_off in range(3)
        for col_off in range(3)
    ]
    return jnp.concatenate(slabs, axis=-1).reshape(rows * cols, 9 * width)


def state_border(hidden):
    return with_halo(with_halo(hidden, ("x", "core"), 8, 0), "sx", 4, 1)


def gate_border(dgates):
    return with_halo(with_halo(dgates, ("x", "core"), 8, 0), "sx", 4, 1)


def back_conv(padded_grad, recur_weight, rows, cols, width):
    total = jnp.zeros((rows * cols, width), jnp.float32)
    for row_off in range(3):
        for col_off in range(3):
            block = row_off * 3 + col_off
            slab = padded_grad[
                2 - row_off : 2 - row_off + rows, 2 - col_off : 2 - col_off + cols
            ].reshape(rows * cols, 4 * width)
            weight_block = recur_weight[block * width : (block + 1) * width]
            total = total + lax.dot_general(
                slab, weight_block, (((1,), (1,)), ((), ())), preferred_element_type=jnp.float32
            )
    return total


def body(input_gates, recur_weight, hidden_init, cell_init, hidden_cot, frame_count):
    rows, cols, width = (hidden_init.shape[1], hidden_init.shape[2], hidden_init.shape[3])
    frames = input_gates.shape[1]
    cells = rows * cols
    count = frame_count[0]
    hidden = hidden_init[0].reshape(cells, width)
    cell = cell_init[0].reshape(cells, width)
    saved = []
    outs = []
    for frame in range(frames):
        padded = state_border(hidden.reshape(rows, cols, width))
        patches = patch_rows(padded, rows, cols, width)
        gates = input_gates[0, frame].reshape(cells, 4 * width).astype(jnp.float32) + jnp.dot(
            patches, recur_weight, preferred_element_type=jnp.float32
        )
        sig_i = jax.nn.sigmoid(gates[:, :width])
        sig_f = jax.nn.sigmoid(gates[:, width : 2 * width])
        tan_g = jnp.tanh(gates[:, 2 * width : 3 * width])
        sig_o = jax.nn.sigmoid(gates[:, 3 * width :])
        cell_new = sig_f * cell + sig_i * tan_g
        tan_c = jnp.tanh(cell_new)
        hidden_new = (sig_o * tan_c).astype(jnp.bfloat16)
        valid = frame < count
        saved.append((patches, cell, sig_i, sig_f, tan_g, sig_o, tan_c, valid))
        cell = jnp.where(valid, cell_new, cell)
        hidden = jnp.where(valid, hidden_new, hidden)
        outs.append(hidden.reshape(rows, cols, width))
    grad_h = jnp.zeros((cells, width), jnp.float32)
    grad_c = jnp.zeros((cells, width), jnp.float32)
    all_patches, all_grads = ([], [])
    gate_list = [None] * frames
    for frame in range(frames - 1, -1, -1):
        patches, cell_prev, sig_i, sig_f, tan_g, sig_o, tan_c, valid = saved[frame]
        grad_h = grad_h + hidden_cot[0, frame].reshape(cells, width).astype(jnp.float32)
        dc_new = grad_c + grad_h * sig_o * (1.0 - tan_c * tan_c)
        d_i = dc_new * tan_g * sig_i * (1.0 - sig_i)
        d_f = dc_new * cell_prev * sig_f * (1.0 - sig_f)
        d_g = dc_new * sig_i * (1.0 - tan_g * tan_g)
        d_o = grad_h * tan_c * sig_o * (1.0 - sig_o)
        dgates = jnp.concatenate([d_i, d_f, d_g, d_o], axis=-1)
        dgates = jnp.where(valid, dgates, 0.0).astype(jnp.bfloat16)
        gate_list[frame] = dgates.reshape(rows, cols, 4 * width)
        all_patches.append(patches)
        all_grads.append(dgates)
        padded_grad = gate_border(dgates.reshape(rows, cols, 4 * width))
        dh_prev = back_conv(padded_grad, recur_weight, rows, cols, width)
        grad_h = jnp.where(valid, dh_prev, grad_h)
        grad_c = jnp.where(valid, dc_new * sig_f, grad_c)
    weight_t = lax.dot_general(
        jnp.concatenate(all_grads),
        jnp.concatenate(all_patches),
        (((0,), (0,)), ((), ())),
        preferred_element_type=jnp.float32,
    ).reshape(16, 2, 32, 9 * width)
    core = lax.axis_index("core")
    mine = jnp.where(core == 0, weight_t[:, 0], weight_t[:, 1])
    theirs = jnp.where(core == 0, weight_t[:, 1], weight_t[:, 0]).astype(jnp.bfloat16)
    got = lax.ppermute(theirs, "core", [(0, 1), (1, 0)])
    chip_sum = (mine + got.astype(jnp.float32)).astype(jnp.bfloat16).reshape(512, 9 * width)
    parts = lax.all_to_all(chip_sum, ("dp", "x", "sx"), 0, 0, tiled=True)
    weight_grad = jnp.sum(parts.reshape(64, 8, 9 * width).astype(jnp.float32), axis=0).T
    hidden_seq = jnp.stack(outs)[None]
    gate_grad = jnp.stack(gate_list)[None]
    hidden_grad = grad_h.astype(jnp.bfloat16).reshape(1, rows, cols, width)
    cell_grad = grad_c.reshape(1, rows, cols, width)
    return (hidden_seq, weight_grad, gate_grad, hidden_grad, cell_grad)


def solution(mesh):
    split = Mesh(mesh.devices.reshape(4, 4, 2, 4), ("dp", "x", "core", "sx"))
    sy = ("x", "core")
    step = jax.shard_map(
        body,
        mesh=split,
        in_specs=(
            P("dp", None, sy, "sx", None),
            P(),
            P("dp", sy, "sx", None),
            P("dp", sy, "sx", None),
            P("dp", None, sy, "sx", None),
            P("dp"),
        ),
        out_specs=(
            P("dp", None, sy, "sx", None),
            P(None, ("dp", "x", "core", "sx")),
            P("dp", None, sy, "sx", None),
            P("dp", sy, "sx", None),
            P("dp", sy, "sx", None),
        ),
        check_vma=False,
    )
    return step
```

```python
import functools

import jax
import jax.numpy as jnp
from jax import lax
from jax.experimental import pallas as pl
from jax.experimental.pallas import tpu as pltpu
from jax.sharding import Mesh, PartitionSpec as P


def ring_pairs(size, phase):
    pairs = [(i, (i + 1) % size) for i in range(phase, size, 2)]
    return [edge for a, b in pairs for edge in ((a, b), (b, a))]


BF = jnp.bfloat16
F32 = jnp.float32
R, L, C = 8, 32, 256
W = 48
ROWS_A = (("h", 3, 1), ("c", 2, 1), ("x0", 2, 4), ("x1", 1, 4), ("t1", 1, 1))
ROWS_B = (("g", 2, 4), ("q", 1, 1))
ROWS_C = (("g", 1, 4),)


def row_offsets(spec):
    table, at = {}, 0
    for name, width, parts in spec:
        for row in range(width):
            for part in range(parts):
                table[name, row, part] = at
                at += 1
    return table, at


def col_offsets(spec):
    table, at = {}, 0
    for name, width, parts in spec:
        for part in range(parts):
            for row in range(R + 2 * width):
                table[name, row, part] = at
                at += width
    return table, -(-at // 16) * 16


def quarter(part):
    return slice(part * C, (part + 1) * C)


def parities():
    return lax.axis_index("core"), lax.axis_index("sx") % 2


def arranged(odd, near, far, before, after):
    @pl.when(odd == 1)
    def _():
        before[...] = near[...]
        after[...] = far[...]

    @pl.when(odd == 0)
    def _():
        before[...] = far[...]
        after[...] = near[...]


def pack_columns(spec, own, above, below, odd, near, far, left, right):
    rows, _ = row_offsets(spec)
    cols, _ = col_offsets(spec)
    for name, width, parts in spec:
        for row in range(R + 2 * width):
            for part in range(parts):
                at = cols[name, row, part]
                if row < width:
                    unit = rows[name, row, part]
                    first, last = above[unit, 0:8, :], above[unit, 24:32, :]
                elif row >= R + width:
                    unit = rows[name, row - R - width, part]
                    first, last = below[unit, 0:8, :], below[unit, 24:32, :]
                else:
                    first, last = own(name, row - width, slice(0, 8), part), own(name, row - width, slice(24, 32), part)
                left[at : at + width, :] = first.astype(F32)[0:width]
                right[at : at + width, :] = last.astype(F32)[8 - width : 8]

    @pl.when(odd == 1)
    def _():
        near[...] = left[...].astype(BF)
        far[...] = right[...].astype(BF)

    @pl.when(odd == 0)
    def _():
        near[...] = right[...].astype(BF)
        far[...] = left[...].astype(BF)


def rows_a_kernel(h_ref, c_ref, x_ref, t_ref, near, far):
    odd, _ = parities()
    rows, _ = row_offsets(ROWS_A)
    for name, width, parts in ROWS_A:
        first = jnp.where(odd == 1, 0, R - width)
        last = jnp.where(odd == 1, R - width, 0)
        for row in range(width):
            for part in range(parts):
                unit = rows[name, row, part]
                for start, out in ((first, near), (last, far)):
                    at = start + row
                    if name == "h":
                        value = h_ref[0, at]
                    elif name == "c":
                        value = c_ref[0, at].astype(BF)
                    elif name == "t1":
                        value = t_ref[0, 0, at]
                    else:
                        value = x_ref[0, int(name[1]), at, :, quarter(part)]
                    out[unit] = value


def cols_a_kernel(h_ref, c_ref, x_ref, t_ref, near_r, far_r, near, far, above, below, left, right):
    row_odd, col_odd = parities()
    arranged(row_odd, near_r, far_r, above, below)

    def own(name, row, cells, part):
        if name == "h":
            return h_ref[0, row, cells]
        if name == "c":
            return c_ref[0, row, cells]
        if name == "t1":
            return t_ref[0, 0, row, cells]
        return x_ref[0, int(name[1]), row, cells, quarter(part)]

    pack_columns(ROWS_A, own, above, below, col_odd, near, far, left, right)


def cols_b_kernel(g_ref, q_ref, near_r, far_r, near, far, above, below, left, right):
    row_odd, col_odd = parities()
    arranged(row_odd, near_r, far_r, above, below)

    def own(name, row, cells, part):
        if name == "q":
            return q_ref[row, cells]
        return g_ref[row, cells, quarter(part)]

    pack_columns(ROWS_B, own, above, below, col_odd, near, far, left, right)


def cols_c_kernel(g_ref, near_r, far_r, near, far, above, below, left, right):
    row_odd, col_odd = parities()
    arranged(row_odd, near_r, far_r, above, below)

    def own(name, row, cells, part):
        return g_ref[row, cells, quarter(part)]

    pack_columns(ROWS_C, own, above, below, col_odd, near, far, left, right)


def unpack_columns(odd, near, far, left, right):
    @pl.when(odd == 1)
    def _():
        left[...] = near[...].astype(F32)
        right[...] = far[...].astype(F32)

    @pl.when(odd == 0)
    def _():
        left[...] = far[...].astype(F32)
        right[...] = near[...].astype(F32)


def border(at, width, left, right):
    cell = lax.broadcasted_iota(jnp.int32, (16, C), 0)
    out = jnp.zeros((16, C), F32)
    for i in range(width):
        out = jnp.where(cell == i, jnp.broadcast_to(right[at + i : at + i + 1, :], (16, C)), out)
        out = jnp.where(cell == 16 - width + i, jnp.broadcast_to(left[at + i : at + i + 1, :], (16, C)), out)
    return out


def widened_grads(spec, width, g_ref, above, below, left, right, gw):
    rows, _ = row_offsets(spec)
    cols, _ = col_offsets(spec)
    for row in range(R + 2 * width):
        fits = inside(width, row)
        for part in range(4):
            if row < width:
                mid = above[rows["g", row, part]]
            elif row >= R + width:
                mid = below[rows["g", row - R - width, part]]
            else:
                mid = g_ref[row - width, :, quarter(part)]
            full = jnp.concatenate([mid.astype(F32), border(cols["g", row, part], width, left, right)], axis=0)
            gw[row * W : (row + 1) * W, quarter(part)] = jnp.where(fits, full, 0.0).astype(BF)


def back(n, gw, w_ref, z):
    cells = n * W
    for side in range(3):
        total = None
        for up in range(3):
            k = up * 3 + side
            slab = gw[(2 - up) * W : (2 - up) * W + cells, :]
            term = lax.dot_general(
                slab, w_ref[k * C : (k + 1) * C, :], (((1,), (1,)), ((), ())), preferred_element_type=F32
            )
            total = term if total is None else total + term
        z[side, 0:n, 8:56, :] = total.reshape(n, W, C)

    def wrap(row, carry):
        z[0, row, 56:57, :] = z[0, row, 8:9, :]
        z[2, row, 7:8, :] = z[2, row, 55:56, :]
        return carry

    lax.fori_loop(0, n, wrap, 0)


def summed(z, row, cells):
    return z[0, row, 9 : 9 + cells, :] + z[1, row, 8 : 8 + cells, :] + z[2, row, 7 : 7 + cells, :]


def last_kernel(g_ref, w_ref, near_r, far_r, near_c, far_c, dh_ref, above, below, left, right, gw, z):
    row_odd, col_odd = parities()
    arranged(row_odd, near_r, far_r, above, below)
    unpack_columns(col_odd, near_c, far_c, left, right)
    widened_grads(ROWS_C, 1, g_ref, above, below, left, right, gw)
    back(R, gw, w_ref, z)

    def one(row, carry):
        dh_ref[0, row] = summed(z, row, L).astype(BF)
        return carry

    lax.fori_loop(0, R, one, 0)


def theirs_kernel(g0_ref, g1_ref, g2_ref, p_ref, mine_ref, out_ref, turned, theirs):
    other = 1 - lax.axis_index("core")
    for frame, g_ref in enumerate((g0_ref, g1_ref, g2_ref)):
        flat = g_ref[...].reshape(R * L, 4 * C).astype(F32)
        turned[:, quarter(frame)] = jnp.transpose(flat).astype(BF)

    def pick(block, carry):
        at = pl.ds(pl.multiple_of(block * 32, 32), 32)
        theirs[at, :] = turned[pl.ds(pl.multiple_of(block * 64 + other * 32, 32), 32), :]
        mine_ref[at, :] = turned[pl.ds(pl.multiple_of(block * 64 + 32 - other * 32, 32), 32), :]
        return carry

    lax.fori_loop(0, 16, pick, 0)

    def one(n, carry):
        at = pl.ds(pl.multiple_of(n * 3 * C, C), 3 * C)
        out_ref[:, at] = jnp.dot(theirs[...], p_ref[:, at], preferred_element_type=F32).astype(BF)
        return carry

    lax.fori_loop(0, 3, one, 0)


def mine_kernel(mine_ref, p_ref, got_ref, out_ref):
    def one(n, carry):
        at = pl.ds(pl.multiple_of(n * 3 * C, C), 3 * C)
        total = jnp.dot(mine_ref[...], p_ref[:, at], preferred_element_type=F32)
        out_ref[:, at] = (total + got_ref[:, at].astype(F32)).astype(BF)
        return carry

    lax.fori_loop(0, 3, one, 0)


def inside(by, row):
    at_row = (lax.axis_index("x") * 2 + lax.axis_index("core")) * R + row - by
    cell = lax.broadcasted_iota(jnp.int32, (W, C), 0)
    column = jnp.where(cell < 40, cell, cell - W) + lax.axis_index("sx") * L
    fits = (column >= 0) & (column < 4 * L)
    return fits & jnp.broadcast_to((at_row >= 0) & (at_row < 8 * R), (W, C))


def sigmoid(value):
    return 0.5 * jnp.tanh(0.5 * value) + 0.5


def forward_kernel(count_ref, h_ref, c_ref, x_ref, t_ref, w_ref, near_r, far_r, near_c, far_c,
                   seq_ref, patch_ref, m1_ref, m0_ref, t1_ref, g2_ref, q_ref, near_out, far_out,
                   above, below, left, right, hs, cs, gates, shifted, wide):
    row_odd, col_odd = parities()
    count = count_ref[0]
    arranged(row_odd, near_r, far_r, above, below)

    unpack_columns(col_odd, near_c, far_c, left, right)

    rows, _ = row_offsets(ROWS_A)
    cols, _ = col_offsets(ROWS_A)
    widths = {name: width for name, width, _ in ROWS_A}

    def main(name, row, part):
        width = widths[name]
        if row < width:
            return above[rows[name, row, part]].astype(F32)
        if row >= R + width:
            return below[rows[name, row - R - width, part]].astype(F32)
        row -= width
        if name == "h":
            return h_ref[0, row].astype(F32)
        if name == "c":
            return c_ref[0, row]
        if name == "t1":
            return t_ref[0, 1, row].astype(F32)
        return x_ref[0, int(name[1]), row, :, quarter(part)].astype(F32)

    def sides(name, row, part):
        width = widths[name]
        at = cols[name, row, part]
        return right[at : at + width, :], left[at : at + width, :]

    zero16 = jnp.zeros((16, C), F32)
    hs[...] = jnp.zeros_like(hs)
    for row in range(R + 6):
        hs[row, 8:40, :] = main("h", row, 0)
        after, before = sides("h", row, 0)
        hs[row, 40:43, :] = after
        hs[row, 53:56, :] = before
        hs[row, 8:56, :] = jnp.where(inside(3, row), hs[row, 8:56, :], 0.0)
    for row in range(R + 4):
        cs[row, 0:32, :] = main("c", row, 0)
        cs[row, 32:48, :] = zero16
        after, before = sides("c", row, 0)
        cs[row, 32:34, :] = after
        cs[row, 46:48, :] = before

    def load_gates(name, by):
        for row in range(R + 2 * by):
            for part in range(4):
                at = row * W
                gates[at : at + 32, quarter(part)] = main(name, row, part)
                gates[at + 32 : at + W, quarter(part)] = zero16
                after, before = sides(name, row, part)
                gates[at + 32 : at + 32 + by, quarter(part)] = after
                gates[at + W - by : at + W, quarter(part)] = before

    def shift(n_rows):
        def one(row, carry):
            hs[row, 7:8, :] = hs[row, 55:56, :]
            hs[row, 56:57, :] = hs[row, 8:9, :]
            for side in range(3):
                shifted[side, row] = hs[row, 7 + side : 55 + side, :].astype(BF)
            return carry

        lax.fori_loop(0, n_rows, one, 0)

    def own_patches(frame, by):
        for k in range(9):
            up, side = k // 3, k % 3
            patch_ref[frame, :, quarter(k)] = shifted[side, by + up : by + up + R, 0:32, :].reshape(R * L, C)

    for frame in range(3):
        by = 2 - frame
        n = R + 2 * by
        cells = n * W if by else R * L
        valid = frame < count
        wcols = W if by else L
        shift(n + 2)
        own_patches(frame, by)
        if by:
            load_gates("x" + str(frame), by)
            for k in range(9):
                up, side = k // 3, k % 3
                wide[0:cells, quarter(k)] = shifted[side, up : up + n].reshape(cells, C)

            def one(at_n, carry, cells=cells):
                at = pl.ds(pl.multiple_of(at_n * 2 * C, C), 2 * C)
                gates[0:cells, at] = gates[0:cells, at] + jnp.dot(
                    wide[0:cells, :], w_ref[:, at], preferred_element_type=F32
                )
                return carry
        else:

            def one(at_n, carry):
                at = pl.ds(pl.multiple_of(at_n * 2 * C, C), 2 * C)
                gates[0 : R * L, at] = x_ref[0, 2, :, :, at].reshape(R * L, 2 * C).astype(F32) + jnp.dot(
                    patch_ref[2], w_ref[:, at], preferred_element_type=F32
                )
                return carry

        lax.fori_loop(0, 2, one, 0)

        def gating(row, carry, frame=frame, by=by, wcols=wcols, valid=valid):
            start = pl.multiple_of(row * wcols, 16)
            g = gates[pl.ds(start, wcols), :]
            si = sigmoid(g[:, 0:C])
            sf = sigmoid(g[:, C : 2 * C])
            tg = jnp.tanh(g[:, 2 * C : 3 * C])
            so = sigmoid(g[:, 3 * C :])
            cell = cs[row + (0 if frame == 0 else frame), 0:wcols, :]
            cell_new = sf * cell + si * tg
            tc = jnp.tanh(cell_new)
            h_new = (so * tc).astype(BF).astype(F32)
            factors = (
                so * (1.0 - tc * tc),
                tg * si * (1.0 - si),
                cell * sf * (1.0 - sf),
                si * (1.0 - tg * tg),
                tc * so * (1.0 - so),
                sf,
            )
            h_old = hs[row + 1, 8 : 8 + wcols, :]
            keep = jnp.broadcast_to(valid, h_new.shape)
            h_next = jnp.where(keep, h_new, h_old)
            cs[row + frame, 0:wcols, :] = jnp.where(keep, cell_new, cell)
            if by:
                hs[row, 8:56, :] = jnp.where(inside(by, row), h_next, 0.0)
            if frame == 0:

                @pl.when((row >= 2) & (row < 2 + R))
                def _():
                    seq_ref[0, 0, row - 2] = h_next[0:L].astype(BF)
                    for i, factor in enumerate(factors):
                        m0_ref[i, row - 2] = factor[0:L].astype(BF)
            elif frame == 1:
                for i, factor in enumerate(factors):
                    m1_ref[i, row] = factor.astype(BF)

                @pl.when((row >= 1) & (row < 1 + R))
                def _():
                    seq_ref[0, 1, row - 1] = h_next[0:L].astype(BF)
            else:
                seq_ref[0, 2, row] = h_next.astype(BF)
                a, bi, bfg, bg, bo, _ = factors
                grad_h = t_ref[0, 2, row].astype(F32)
                dc_new = grad_h * a
                for part, value in enumerate((dc_new * bi, dc_new * bfg, dc_new * bg, grad_h * bo)):
                    g2_ref[row, :, quarter(part)] = jnp.where(keep, value, 0.0).astype(BF)
                q_ref[row] = jnp.where(keep, dc_new * sf, grad_h)
            return carry

        lax.fori_loop(0, n, gating, 0)
    for row in range(R + 2):
        t1_ref[row, 0:32, :] = main("t1", row, 0).astype(BF)
        after, before = sides("t1", row, 0)
        cell = lax.broadcasted_iota(jnp.int32, (16, C), 0)
        pad = jnp.where(cell == 0, jnp.broadcast_to(after, (16, C)), jnp.where(cell == 15, jnp.broadcast_to(before, (16, C)), 0.0))
        t1_ref[row, 32:48, :] = pad.astype(BF)
    rows_b, _ = row_offsets(ROWS_B)
    for name, width, parts in ROWS_B:
        first = jnp.where(row_odd == 1, 0, R - width)
        last = jnp.where(row_odd == 1, R - width, 0)
        for row in range(width):
            for part in range(parts):
                unit = rows_b[name, row, part]
                for start, out in ((first, near_out), (last, far_out)):
                    if name == "q":
                        out[unit] = q_ref[start + row].astype(BF)
                    else:
                        out[unit] = g2_ref[start + row, :, quarter(part)]


def backward_kernel(count_ref, t0_ref, w_ref, m1_ref, m0_ref, t1_ref, g2_ref, q_ref, near_r, far_r, near_c, far_c,
                    g1_ref, g0_ref, dh_ref, dc_ref, near_out, far_out, above, below, left, right, gw, qs, z):
    row_odd, col_odd = parities()
    count = count_ref[0]
    arranged(row_odd, near_r, far_r, above, below)

    unpack_columns(col_odd, near_c, far_c, left, right)

    rows, _ = row_offsets(ROWS_B)
    cols, _ = col_offsets(ROWS_B)
    valid2, valid1 = 2 < count, 1 < count
    widened_grads(ROWS_B, 2, g2_ref, above, below, left, right, gw)
    for row in range(R + 2):
        if row < 1:
            mid = above[rows["q", 0, 0]].astype(F32)
        elif row >= R + 1:
            mid = below[rows["q", 0, 0]].astype(F32)
        else:
            mid = q_ref[row - 1]
        qs[row, 0:32, :] = mid
        qs[row, 32:48, :] = border(cols["q", row, 0], 1, left, right)

    back(R + 2, gw, w_ref, z)

    def first(row, carry):
        keep2 = jnp.broadcast_to(valid2, (W, C))
        keep1 = jnp.broadcast_to(valid1, (W, C))
        q = qs[row]
        grad_h = jnp.where(keep2, summed(z, row, W), q) + t1_ref[row].astype(F32)
        grad_c = jnp.where(keep2, q, 0.0)
        a, bi, bfg, bg, bo, sf = (m1_ref[i, row].astype(F32) for i in range(6))
        dc_new = grad_c + grad_h * a
        keep = keep1 & inside(1, row)
        at = pl.ds(pl.multiple_of(row * W, W), W)
        for part, value in enumerate((dc_new * bi, dc_new * bfg, dc_new * bg, grad_h * bo)):
            gw[at, quarter(part)] = jnp.where(keep, value, 0.0).astype(BF)

        @pl.when((row >= 1) & (row < 1 + R))
        def _():
            dc_ref[0, row - 1] = jnp.where(keep1, dc_new * sf, grad_c)[0:L]
            dh_ref[0, row - 1] = grad_h[0:L]
            for part in range(4):
                g1_ref[row - 1, :, quarter(part)] = gw[pl.ds(pl.multiple_of(row * W, W), L), quarter(part)]

        return carry

    lax.fori_loop(0, R + 2, first, 0)
    back(R, gw, w_ref, z)

    def second(row, carry):
        keep1 = jnp.broadcast_to(valid1, (L, C))
        grad_h = jnp.where(keep1, summed(z, row, L), dh_ref[0, row]) + t0_ref[0, 0, row].astype(F32)
        a, bi, bfg, bg, bo, sf = (m0_ref[i, row].astype(F32) for i in range(6))
        dc_new = dc_ref[0, row] + grad_h * a
        for part, value in enumerate((dc_new * bi, dc_new * bfg, dc_new * bg, grad_h * bo)):
            g0_ref[row, :, quarter(part)] = value.astype(BF)
        dc_ref[0, row] = dc_new * sf
        return carry

    lax.fori_loop(0, R, second, 0)
    first_row = jnp.where(row_odd == 1, 0, R - 1)
    last_row = jnp.where(row_odd == 1, R - 1, 0)
    for part in range(4):
        near_out[part] = g0_ref[first_row, :, quarter(part)]
        far_out[part] = g0_ref[last_row, :, quarter(part)]


def whole(shape):
    return pl.BlockSpec(shape, lambda _: (0,) * len(shape))


def call(kernel, inputs, outs, scratch, blocks=None, scalar=False, name=None, flops=0, limit=16):
    blocks = blocks or {}
    specs = [whole(blocks.get(i, value.shape)) for i, value in enumerate(inputs)]
    if scalar:
        specs[0] = pl.BlockSpec(memory_space=pltpu.SMEM)
    size = sum(value.size * value.dtype.itemsize for value in inputs)
    return pl.pallas_call(
        kernel,
        grid=(1,),
        in_specs=specs,
        out_specs=[whole(out.shape) for out in outs],
        out_shape=outs,
        scratch_shapes=scratch,
        name=name,
        compiler_params=pltpu.CompilerParams(vmem_limit_bytes=limit << 20),
        cost_estimate=pl.CostEstimate(flops=flops, bytes_accessed=size, transcendentals=0),
    )(*inputs)


def swap_rows(near, far):
    axis = ("x", "core")
    return lax.ppermute(near, axis, ring_pairs(8, 0)), lax.ppermute(far, axis, ring_pairs(8, 1))


def swap_cols(near, far):
    return lax.ppermute(near, "sx", ring_pairs(4, 0)), lax.ppermute(far, "sx", ring_pairs(4, 1))


def body(input_gates, recur_weight, hidden_init, cell_init, hidden_cot, frame_count):
    width = C
    out = jax.ShapeDtypeStruct
    vmem = pltpu.VMEM
    _, row_units = row_offsets(ROWS_A)
    _, col_units = col_offsets(ROWS_A)
    first_two = {2: (1, 2, R, L, 4 * C)}
    middle = hidden_cot[:, 1:2]
    border = out((row_units, L, C), BF)
    near, far = call(
        rows_a_kernel, (hidden_init, cell_init, input_gates, middle), [border] * 2, [], first_two, name="rows_a"
    )
    near_r, far_r = swap_rows(near, far)
    strip = out((col_units, C), BF)
    near, far = call(
        cols_a_kernel,
        (hidden_init, cell_init, input_gates, middle, near_r, far_r),
        [strip] * 2,
        [vmem((row_units, L, C), BF)] * 2 + [vmem((col_units, C), F32)] * 2,
        first_two,
        name="cols_a",
    )
    near_c, far_c = swap_cols(near, far)
    _, row_units_b = row_offsets(ROWS_B)
    _, col_units_b = col_offsets(ROWS_B)
    hidden_seq, patches, m1, m0, t1, g2, q, near, far = call(
        forward_kernel,
        (frame_count, hidden_init, cell_init, input_gates, hidden_cot, recur_weight, near_r, far_r, near_c, far_c),
        [
            out((1, 3, R, L, C), BF),
            out((3, R * L, 9 * C), BF),
            out((6, R + 2, W, C), BF),
            out((6, R, L, C), BF),
            out((R + 2, W, C), BF),
            out((R, L, 4 * C), BF),
            out((R, L, C), F32),
            out((row_units_b, L, C), BF),
            out((row_units_b, L, C), BF),
        ],
        [vmem((row_units, L, C), BF)] * 2
        + [vmem((col_units, C), F32)] * 2
        + [
            vmem((R + 6, 64, C), F32),
            vmem((R + 4, W, C), F32),
            vmem(((R + 4) * W, 4 * C), F32),
            vmem((3, R + 6, W, C), BF),
            vmem(((R + 4) * W, 9 * C), BF),
        ],
        scalar=True,
        name="forward",
        limit=28,
        flops=6 * 10**9,
    )
    near_r, far_r = swap_rows(near, far)
    strip = out((col_units_b, C), BF)
    near, far = call(
        cols_b_kernel,
        (g2, q, near_r, far_r),
        [strip] * 2,
        [vmem((row_units_b, L, C), BF)] * 2 + [vmem((col_units_b, C), F32)] * 2,
        name="cols_b",
    )
    near_c, far_c = swap_cols(near, far)
    g1, g0, _, cell_grad, near_c_rows, far_c_rows = call(
        backward_kernel,
        (frame_count, hidden_cot, recur_weight, m1, m0, t1, g2, q, near_r, far_r, near_c, far_c),
        [out((R, L, 4 * C), BF), out((R, L, 4 * C), BF), out((1, R, L, C), F32), out((1, R, L, C), F32),
         out((4, L, C), BF), out((4, L, C), BF)],
        [vmem((row_units_b, L, C), BF)] * 2
        + [vmem((col_units_b, C), F32)] * 2
        + [vmem(((R + 4) * W, 4 * C), BF), vmem((R + 2, W, C), F32), vmem((3, R + 2, 64, C), F32)],
        {1: (1, 1, R, L, C)},
        scalar=True,
        name="backward",
        limit=24,
        flops=4 * 10**9,
    )
    _, col_units_c = col_offsets(ROWS_C)
    near_r, far_r = swap_rows(near_c_rows, far_c_rows)
    flat_patches = patches.reshape(3 * R * L, 9 * C)
    half = out((512, 9 * C), BF)
    mine, theirs = call(
        theirs_kernel,
        (g0, g1, g2, flat_patches),
        [out((512, 3 * C), BF), half],
        [vmem((4 * C, 3 * C), BF), vmem((512, 3 * C), BF)],
        name="theirs",
        flops=2 * 10**9,
    )
    got = lax.ppermute(theirs, "core", [(0, 1), (1, 0)])
    (chip_sum,) = call(mine_kernel, (mine, flat_patches, got), [half], [], name="mine", flops=2 * 10**9)
    strip = out((col_units_c, C), BF)
    near, far = call(
        cols_c_kernel,
        (g0, near_r, far_r),
        [strip] * 2,
        [vmem((4, L, C), BF)] * 2 + [vmem((col_units_c, C), F32)] * 2,
        name="cols_c",
    )
    near_c, far_c = swap_cols(near, far)
    chip_sum, near_c, far_c = lax.optimization_barrier((chip_sum, near_c, far_c))
    (hidden_grad,) = call(
        last_kernel,
        (g0, recur_weight, near_r, far_r, near_c, far_c),
        [out((1, R, L, C), BF)],
        [vmem((4, L, C), BF)] * 2
        + [vmem((col_units_c, C), F32)] * 2
        + [vmem(((R + 2) * W, 4 * C), BF), vmem((3, R, 64, C), F32)],
        name="last",
        flops=2 * 10**9,
    )
    parts = lax.all_to_all(chip_sum, ("dp", "x", "sx"), 0, 0, tiled=True)
    weight_grad = jnp.sum(parts.reshape(64, 8, 9 * width).astype(jnp.float32), axis=0).T
    gate_grad = jnp.stack([g0, g1, g2])[None]
    return (hidden_seq, weight_grad, gate_grad, hidden_grad, cell_grad)


def solution(mesh):
    split = Mesh(mesh.devices.reshape(4, 4, 2, 4), ("dp", "x", "core", "sx"))
    sy = ("x", "core")
    step = jax.shard_map(
        body,
        mesh=split,
        in_specs=(
            P("dp", None, sy, "sx", None),
            P(),
            P("dp", sy, "sx", None),
            P("dp", sy, "sx", None),
            P("dp", None, sy, "sx", None),
            P("dp"),
        ),
        out_specs=(
            P("dp", None, sy, "sx", None),
            P(None, ("dp", "x", "core", "sx")),
            P("dp", None, sy, "sx", None),
            P("dp", sy, "sx", None),
            P("dp", sy, "sx", None),
        ),
        check_vma=False,
    )
    return step
```

```python
import functools

import jax
import jax.numpy as jnp
from jax import lax
from jax.experimental import pallas as pl
from jax.experimental.pallas import tpu as pltpu
from jax.sharding import Mesh, PartitionSpec as P


def ring_pairs(size, phase):
    pairs = [(i, (i + 1) % size) for i in range(phase, size, 2)]
    return [edge for a, b in pairs for edge in ((a, b), (b, a))]


CORES = [(0, 1), (1, 0)]
AXES = ("dp", "x", "core", "sx")
HALF = 1152
BF = jnp.bfloat16
F32 = jnp.float32
R, L, C = 8, 32, 256
W = 48
ROWS_A = (("h", 3, 1), ("c", 2, 1), ("x0", 2, 4), ("x1", 1, 4), ("t1", 1, 1))
ROWS_B = (("g", 2, 4), ("q", 1, 1))
ROWS_C = (("g", 1, 4),)


def row_offsets(spec):
    table, at = {}, 0
    for name, width, parts in spec:
        for row in range(width):
            for part in range(parts):
                table[name, row, part] = at
                at += 1
    return table, at


def col_offsets(spec):
    table, at = {}, 0
    for name, width, parts in spec:
        for part in range(parts):
            for row in range(R + 2 * width):
                table[name, row, part] = at
                at += width
    return table, -(-at // 16) * 16


def quarter(part):
    return slice(part * C, (part + 1) * C)


def parities():
    return lax.axis_index("core"), lax.axis_index("sx") % 2


def arranged(odd, near, far, before, after):
    @pl.when(odd == 1)
    def _():
        before[...] = near[...]
        after[...] = far[...]

    @pl.when(odd == 0)
    def _():
        before[...] = far[...]
        after[...] = near[...]


def pack_columns(spec, own, above, below, odd, near, far, left, right):
    rows, _ = row_offsets(spec)
    cols, _ = col_offsets(spec)
    for name, width, parts in spec:
        for row in range(R + 2 * width):
            for part in range(parts):
                at = cols[name, row, part]
                if row < width:
                    unit = rows[name, row, part]
                    first, last = above[unit, 0:8, :], above[unit, 24:32, :]
                elif row >= R + width:
                    unit = rows[name, row - R - width, part]
                    first, last = below[unit, 0:8, :], below[unit, 24:32, :]
                else:
                    first, last = own(name, row - width, slice(0, 8), part), own(name, row - width, slice(24, 32), part)
                left[at : at + width, :] = first.astype(F32)[0:width]
                right[at : at + width, :] = last.astype(F32)[8 - width : 8]

    @pl.when(odd == 1)
    def _():
        near[...] = left[...].astype(BF)
        far[...] = right[...].astype(BF)

    @pl.when(odd == 0)
    def _():
        near[...] = right[...].astype(BF)
        far[...] = left[...].astype(BF)


def rows_a_kernel(h_ref, c_ref, x_ref, t_ref, near, far):
    odd, _ = parities()
    rows, _ = row_offsets(ROWS_A)
    for name, width, parts in ROWS_A:
        first = jnp.where(odd == 1, 0, R - width)
        last = jnp.where(odd == 1, R - width, 0)
        for row in range(width):
            for part in range(parts):
                unit = rows[name, row, part]
                for start, out in ((first, near), (last, far)):
                    at = start + row
                    if name == "h":
                        value = h_ref[0, at]
                    elif name == "c":
                        value = c_ref[0, at].astype(BF)
                    elif name == "t1":
                        value = t_ref[0, 0, at]
                    else:
                        value = x_ref[0, int(name[1]), at, :, quarter(part)]
                    out[unit] = value


def cols_a_kernel(h_ref, c_ref, x_ref, t_ref, near_r, far_r, near, far, above, below, left, right):
    row_odd, col_odd = parities()
    arranged(row_odd, near_r, far_r, above, below)

    def own(name, row, cells, part):
        if name == "h":
            return h_ref[0, row, cells]
        if name == "c":
            return c_ref[0, row, cells]
        if name == "t1":
            return t_ref[0, 0, row, cells]
        return x_ref[0, int(name[1]), row, cells, quarter(part)]

    pack_columns(ROWS_A, own, above, below, col_odd, near, far, left, right)


def cols_b_kernel(g_ref, q_ref, near_r, far_r, near, far, above, below, left, right):
    row_odd, col_odd = parities()
    arranged(row_odd, near_r, far_r, above, below)

    def own(name, row, cells, part):
        if name == "q":
            return q_ref[row, cells]
        return g_ref[row, cells, quarter(part)]

    pack_columns(ROWS_B, own, above, below, col_odd, near, far, left, right)


def cols_c_kernel(g_ref, near_r, far_r, near, far, above, below, left, right):
    row_odd, col_odd = parities()
    arranged(row_odd, near_r, far_r, above, below)

    def own(name, row, cells, part):
        return g_ref[row, cells, quarter(part)]

    pack_columns(ROWS_C, own, above, below, col_odd, near, far, left, right)


def unpack_columns(odd, near, far, left, right):
    @pl.when(odd == 1)
    def _():
        left[...] = near[...].astype(F32)
        right[...] = far[...].astype(F32)

    @pl.when(odd == 0)
    def _():
        left[...] = far[...].astype(F32)
        right[...] = near[...].astype(F32)


def border(at, width, left, right):
    cell = lax.broadcasted_iota(jnp.int32, (16, C), 0)
    out = jnp.zeros((16, C), F32)
    for i in range(width):
        out = jnp.where(cell == i, jnp.broadcast_to(right[at + i : at + i + 1, :], (16, C)), out)
        out = jnp.where(cell == 16 - width + i, jnp.broadcast_to(left[at + i : at + i + 1, :], (16, C)), out)
    return out


def widened_grads(spec, width, g_ref, above, below, left, right, gw):
    rows, _ = row_offsets(spec)
    cols, _ = col_offsets(spec)
    for row in range(R + 2 * width):
        fits = inside(width, row)
        for part in range(4):
            if row < width:
                mid = above[rows["g", row, part]]
            elif row >= R + width:
                mid = below[rows["g", row - R - width, part]]
            else:
                mid = g_ref[row - width, :, quarter(part)]
            full = jnp.concatenate([mid.astype(F32), border(cols["g", row, part], width, left, right)], axis=0)
            gw[row * W : (row + 1) * W, quarter(part)] = jnp.where(fits, full, 0.0).astype(BF)


def back(n, gw, w_ref, z):
    cells = n * W
    for side in range(3):
        total = None
        for up in range(3):
            k = up * 3 + side
            slab = gw[(2 - up) * W : (2 - up) * W + cells, :]
            term = lax.dot_general(
                slab, w_ref[k * C : (k + 1) * C, :], (((1,), (1,)), ((), ())), preferred_element_type=F32
            )
            total = term if total is None else total + term
        z[side, 0:n, 8:56, :] = total.reshape(n, W, C)

    def wrap(row, carry):
        z[0, row, 56:57, :] = z[0, row, 8:9, :]
        z[2, row, 7:8, :] = z[2, row, 55:56, :]
        return carry

    lax.fori_loop(0, n, wrap, 0)


def summed(z, row, cells):
    return z[0, row, 9 : 9 + cells, :] + z[1, row, 8 : 8 + cells, :] + z[2, row, 7 : 7 + cells, :]


def last_kernel(g_ref, w_ref, near_r, far_r, near_c, far_c, dh_ref, above, below, left, right, gw, z):
    row_odd, col_odd = parities()
    arranged(row_odd, near_r, far_r, above, below)
    unpack_columns(col_odd, near_c, far_c, left, right)
    widened_grads(ROWS_C, 1, g_ref, above, below, left, right, gw)
    back(R, gw, w_ref, z)

    def one(row, carry):
        dh_ref[0, row] = summed(z, row, L).astype(BF)
        return carry

    lax.fori_loop(0, R, one, 0)


def set_member(core, place, half, j):
    near = jnp.where((place == 1) | (place == 2), 1, 0)
    kind = jnp.where(core == 0, near, place // 2)
    kind = jnp.where(half == 1, 1 - kind, kind)
    return jnp.where(core == 0, kind + j * (3 - 2 * kind), 2 * kind + j)


def turn(grads, turned, mine_ref, theirs_ref):
    core = lax.axis_index("core")
    for frame, g_ref in enumerate(grads):
        flat = g_ref[...].reshape(R * L, 4 * C).astype(F32)
        turned[:, quarter(frame)] = jnp.transpose(flat).astype(BF)

    place = {axis: lax.axis_index(axis) for axis in ("dp", "x")}

    def pick(block, carry):
        at = pl.ds(pl.multiple_of(block * 32, 32), 32)
        outer, inner = block // 4, block % 4
        for who, out in ((core, mine_ref), (1 - core, theirs_ref)):
            d = set_member(who, place["dp"], outer // 2, outer % 2)
            x = set_member(who, place["x"], inner // 2, inner % 2)
            out[at, :] = turned[pl.ds(pl.multiple_of(((d * 4 + x) * 2 + who) * 32, 32), 32), :]
        return carry

    lax.fori_loop(0, 16, pick, 0)


def own_sum_kernel(mine_ref, p_ref, out_ref):
    def one(n, carry):
        at = pl.ds(pl.multiple_of(n * 3 * C, C), 3 * C)
        out_ref[:, at] = jnp.dot(mine_ref[...], p_ref[:, at], preferred_element_type=F32)
        return carry

    lax.fori_loop(0, 3, one, 0)


def parted(rows, total, keep, send):
    for block in range(keep.shape[0] // rows):
        src = block * 2 * rows
        keep[block * rows : (block + 1) * rows, :] = total[src : src + rows].astype(BF)
        send[block * rows : (block + 1) * rows, :] = total[src + rows : src + 2 * rows].astype(BF)


def chip_sum_kernel(got_ref, p_ref, own_ref, keep0, send0, keep1, send1):
    for color, (rows, keep, send) in enumerate(((256, keep0, send0), (64, keep1, send1))):
        at = slice(color * HALF, (color + 1) * HALF)
        total = own_ref[:, at] + jnp.dot(got_ref[...], p_ref[:, at], preferred_element_type=F32)
        parted(rows, total, keep, send)


def halve_kernel(kept0, came0, kept1, came1, keep0, send0, keep1, send1):
    parted(64, kept0[...].astype(F32) + came0[...].astype(F32), keep0, send0)
    parted(128, kept1[...].astype(F32) + came1[...].astype(F32), keep1, send1)


def quarter_kernel(kept0, came0, kept1, came1, out_ref):
    out_ref[:, 0:HALF] = (kept0[...].astype(F32) + came0[...].astype(F32)).astype(BF)
    out_ref[:, HALF:] = (kept1[...].astype(F32) + came1[...].astype(F32)).astype(BF)


def total_kernel(parts_ref, out_ref):
    def one(i, carry):
        out_ref[...] = out_ref[...] + parts_ref[i].astype(F32)
        return carry

    out_ref[...] = jnp.zeros_like(out_ref)
    lax.fori_loop(0, 16, one, 0)


def inside(by, row):
    at_row = (lax.axis_index("x") * 2 + lax.axis_index("core")) * R + row - by
    cell = lax.broadcasted_iota(jnp.int32, (W, C), 0)
    column = jnp.where(cell < 40, cell, cell - W) + lax.axis_index("sx") * L
    fits = (column >= 0) & (column < 4 * L)
    return fits & jnp.broadcast_to((at_row >= 0) & (at_row < 8 * R), (W, C))


def sigmoid(value):
    return 0.5 * jnp.tanh(0.5 * value) + 0.5


def forward_kernel(count_ref, h_ref, c_ref, x_ref, t_ref, w_ref, near_r, far_r, near_c, far_c,
                   seq_ref, patch_ref, m1_ref, m0_ref, t1_ref, g2_ref, q_ref, near_out, far_out,
                   above, below, left, right, hs, cs, gates, shifted, wide):
    row_odd, col_odd = parities()
    count = count_ref[0]
    arranged(row_odd, near_r, far_r, above, below)

    unpack_columns(col_odd, near_c, far_c, left, right)

    rows, _ = row_offsets(ROWS_A)
    cols, _ = col_offsets(ROWS_A)
    widths = {name: width for name, width, _ in ROWS_A}

    def main(name, row, part):
        width = widths[name]
        if row < width:
            return above[rows[name, row, part]].astype(F32)
        if row >= R + width:
            return below[rows[name, row - R - width, part]].astype(F32)
        row -= width
        if name == "h":
            return h_ref[0, row].astype(F32)
        if name == "c":
            return c_ref[0, row]
        if name == "t1":
            return t_ref[0, 1, row].astype(F32)
        return x_ref[0, int(name[1]), row, :, quarter(part)].astype(F32)

    def sides(name, row, part):
        width = widths[name]
        at = cols[name, row, part]
        return right[at : at + width, :], left[at : at + width, :]

    zero16 = jnp.zeros((16, C), F32)
    hs[...] = jnp.zeros_like(hs)
    for row in range(R + 6):
        hs[row, 8:40, :] = main("h", row, 0)
        after, before = sides("h", row, 0)
        hs[row, 40:43, :] = after
        hs[row, 53:56, :] = before
        hs[row, 8:56, :] = jnp.where(inside(3, row), hs[row, 8:56, :], 0.0)
    for row in range(R + 4):
        cs[row, 0:32, :] = main("c", row, 0)
        cs[row, 32:48, :] = zero16
        after, before = sides("c", row, 0)
        cs[row, 32:34, :] = after
        cs[row, 46:48, :] = before

    def load_gates(name, by):
        for row in range(R + 2 * by):
            for part in range(4):
                at = row * W
                gates[at : at + 32, quarter(part)] = main(name, row, part)
                gates[at + 32 : at + W, quarter(part)] = zero16
                after, before = sides(name, row, part)
                gates[at + 32 : at + 32 + by, quarter(part)] = after
                gates[at + W - by : at + W, quarter(part)] = before

    def shift(n_rows):
        def one(row, carry):
            hs[row, 7:8, :] = hs[row, 55:56, :]
            hs[row, 56:57, :] = hs[row, 8:9, :]
            for side in range(3):
                shifted[side, row] = hs[row, 7 + side : 55 + side, :].astype(BF)
            return carry

        lax.fori_loop(0, n_rows, one, 0)

    def own_patches(frame, by):
        for k in range(9):
            up, side = k // 3, k % 3
            patch_ref[frame, :, quarter(k)] = shifted[side, by + up : by + up + R, 0:32, :].reshape(R * L, C)

    for frame in range(3):
        by = 2 - frame
        n = R + 2 * by
        cells = n * W if by else R * L
        valid = frame < count
        wcols = W if by else L
        shift(n + 2)
        own_patches(frame, by)
        if by:
            load_gates("x" + str(frame), by)
            for k in range(9):
                up, side = k // 3, k % 3
                wide[0:cells, quarter(k)] = shifted[side, up : up + n].reshape(cells, C)

            def one(at_n, carry, cells=cells):
                at = pl.ds(pl.multiple_of(at_n * 2 * C, C), 2 * C)
                gates[0:cells, at] = gates[0:cells, at] + jnp.dot(
                    wide[0:cells, :], w_ref[:, at], preferred_element_type=F32
                )
                return carry
        else:

            def one(at_n, carry):
                at = pl.ds(pl.multiple_of(at_n * 2 * C, C), 2 * C)
                gates[0 : R * L, at] = x_ref[0, 2, :, :, at].reshape(R * L, 2 * C).astype(F32) + jnp.dot(
                    patch_ref[2], w_ref[:, at], preferred_element_type=F32
                )
                return carry

        lax.fori_loop(0, 2, one, 0)

        def gating(row, carry, frame=frame, by=by, wcols=wcols, valid=valid):
            start = pl.multiple_of(row * wcols, 16)
            g = gates[pl.ds(start, wcols), :]
            si = sigmoid(g[:, 0:C])
            sf = sigmoid(g[:, C : 2 * C])
            tg = jnp.tanh(g[:, 2 * C : 3 * C])
            so = sigmoid(g[:, 3 * C :])
            cell = cs[row + (0 if frame == 0 else frame), 0:wcols, :]
            cell_new = sf * cell + si * tg
            tc = jnp.tanh(cell_new)
            h_new = (so * tc).astype(BF).astype(F32)
            factors = (
                so * (1.0 - tc * tc),
                tg * si * (1.0 - si),
                cell * sf * (1.0 - sf),
                si * (1.0 - tg * tg),
                tc * so * (1.0 - so),
                sf,
            )
            h_old = hs[row + 1, 8 : 8 + wcols, :]
            keep = jnp.broadcast_to(valid, h_new.shape)
            h_next = jnp.where(keep, h_new, h_old)
            cs[row + frame, 0:wcols, :] = jnp.where(keep, cell_new, cell)
            if by:
                hs[row, 8:56, :] = jnp.where(inside(by, row), h_next, 0.0)
            if frame == 0:

                @pl.when((row >= 2) & (row < 2 + R))
                def _():
                    seq_ref[0, 0, row - 2] = h_next[0:L].astype(BF)
                    for i, factor in enumerate(factors):
                        m0_ref[i, row - 2] = factor[0:L].astype(BF)
            elif frame == 1:
                for i, factor in enumerate(factors):
                    m1_ref[i, row] = factor.astype(BF)

                @pl.when((row >= 1) & (row < 1 + R))
                def _():
                    seq_ref[0, 1, row - 1] = h_next[0:L].astype(BF)
            else:
                seq_ref[0, 2, row] = h_next.astype(BF)
                a, bi, bfg, bg, bo, _ = factors
                grad_h = t_ref[0, 2, row].astype(F32)
                dc_new = grad_h * a
                for part, value in enumerate((dc_new * bi, dc_new * bfg, dc_new * bg, grad_h * bo)):
                    g2_ref[row, :, quarter(part)] = jnp.where(keep, value, 0.0).astype(BF)
                q_ref[row] = jnp.where(keep, dc_new * sf, grad_h)
            return carry

        lax.fori_loop(0, n, gating, 0)
    for row in range(R + 2):
        t1_ref[row, 0:32, :] = main("t1", row, 0).astype(BF)
        after, before = sides("t1", row, 0)
        cell = lax.broadcasted_iota(jnp.int32, (16, C), 0)
        pad = jnp.where(cell == 0, jnp.broadcast_to(after, (16, C)), jnp.where(cell == 15, jnp.broadcast_to(before, (16, C)), 0.0))
        t1_ref[row, 32:48, :] = pad.astype(BF)
    rows_b, _ = row_offsets(ROWS_B)
    for name, width, parts in ROWS_B:
        first = jnp.where(row_odd == 1, 0, R - width)
        last = jnp.where(row_odd == 1, R - width, 0)
        for row in range(width):
            for part in range(parts):
                unit = rows_b[name, row, part]
                for start, out in ((first, near_out), (last, far_out)):
                    if name == "q":
                        out[unit] = q_ref[start + row].astype(BF)
                    else:
                        out[unit] = g2_ref[start + row, :, quarter(part)]


def backward_kernel(count_ref, t0_ref, w_ref, m1_ref, m0_ref, t1_ref, g2_ref, q_ref, near_r, far_r, near_c, far_c,
                    g1_ref, g0_ref, dh_ref, dc_ref, near_out, far_out, mine_ref, theirs_ref, above, below, left, right, gw, qs, z, turned):
    row_odd, col_odd = parities()
    count = count_ref[0]
    arranged(row_odd, near_r, far_r, above, below)

    unpack_columns(col_odd, near_c, far_c, left, right)

    rows, _ = row_offsets(ROWS_B)
    cols, _ = col_offsets(ROWS_B)
    valid2, valid1 = 2 < count, 1 < count
    widened_grads(ROWS_B, 2, g2_ref, above, below, left, right, gw)
    for row in range(R + 2):
        if row < 1:
            mid = above[rows["q", 0, 0]].astype(F32)
        elif row >= R + 1:
            mid = below[rows["q", 0, 0]].astype(F32)
        else:
            mid = q_ref[row - 1]
        qs[row, 0:32, :] = mid
        qs[row, 32:48, :] = border(cols["q", row, 0], 1, left, right)

    back(R + 2, gw, w_ref, z)

    def first(row, carry):
        keep2 = jnp.broadcast_to(valid2, (W, C))
        keep1 = jnp.broadcast_to(valid1, (W, C))
        q = qs[row]
        grad_h = jnp.where(keep2, summed(z, row, W), q) + t1_ref[row].astype(F32)
        grad_c = jnp.where(keep2, q, 0.0)
        a, bi, bfg, bg, bo, sf = (m1_ref[i, row].astype(F32) for i in range(6))
        dc_new = grad_c + grad_h * a
        keep = keep1 & inside(1, row)
        at = pl.ds(pl.multiple_of(row * W, W), W)
        for part, value in enumerate((dc_new * bi, dc_new * bfg, dc_new * bg, grad_h * bo)):
            gw[at, quarter(part)] = jnp.where(keep, value, 0.0).astype(BF)

        @pl.when((row >= 1) & (row < 1 + R))
        def _():
            dc_ref[0, row - 1] = jnp.where(keep1, dc_new * sf, grad_c)[0:L]
            dh_ref[0, row - 1] = grad_h[0:L]
            for part in range(4):
                g1_ref[row - 1, :, quarter(part)] = gw[pl.ds(pl.multiple_of(row * W, W), L), quarter(part)]

        return carry

    lax.fori_loop(0, R + 2, first, 0)
    back(R, gw, w_ref, z)

    def second(row, carry):
        keep1 = jnp.broadcast_to(valid1, (L, C))
        grad_h = jnp.where(keep1, summed(z, row, L), dh_ref[0, row]) + t0_ref[0, 0, row].astype(F32)
        a, bi, bfg, bg, bo, sf = (m0_ref[i, row].astype(F32) for i in range(6))
        dc_new = dc_ref[0, row] + grad_h * a
        for part, value in enumerate((dc_new * bi, dc_new * bfg, dc_new * bg, grad_h * bo)):
            g0_ref[row, :, quarter(part)] = value.astype(BF)
        dc_ref[0, row] = dc_new * sf
        return carry

    lax.fori_loop(0, R, second, 0)
    first_row = jnp.where(row_odd == 1, 0, R - 1)
    last_row = jnp.where(row_odd == 1, R - 1, 0)
    for part in range(4):
        near_out[part] = g0_ref[first_row, :, quarter(part)]
        far_out[part] = g0_ref[last_row, :, quarter(part)]
    turn((g0_ref, g1_ref, g2_ref), turned, mine_ref, theirs_ref)


def whole(shape):
    return pl.BlockSpec(shape, lambda _: (0,) * len(shape))


def call(kernel, inputs, outs, scratch, blocks=None, scalar=False, name=None, flops=0, limit=16):
    blocks = blocks or {}
    specs = [whole(blocks.get(i, value.shape)) for i, value in enumerate(inputs)]
    if scalar:
        specs[0] = pl.BlockSpec(memory_space=pltpu.SMEM)
    size = sum(value.size * value.dtype.itemsize for value in inputs)
    return pl.pallas_call(
        kernel,
        grid=(1,),
        in_specs=specs,
        out_specs=[whole(out.shape) for out in outs],
        out_shape=outs,
        scratch_shapes=scratch,
        name=name,
        compiler_params=pltpu.CompilerParams(vmem_limit_bytes=limit << 20),
        cost_estimate=pl.CostEstimate(flops=flops, bytes_accessed=size, transcendentals=0),
    )(*inputs)


def swap_rows(near, far):
    axis = ("x", "core")
    return lax.ppermute(near, axis, ring_pairs(8, 0)), lax.ppermute(far, axis, ring_pairs(8, 1))


def swap_cols(near, far):
    return lax.ppermute(near, "sx", ring_pairs(4, 0)), lax.ppermute(far, "sx", ring_pairs(4, 1))


def first_partner(value, axis):
    flips = (1, 3)
    pairs = [(i * 2 + c, (i ^ flips[c]) * 2 + c) for i in range(4) for c in range(2)]
    return lax.ppermute(value, (axis, "core"), pairs)


def owner_groups():
    sets = (((0, 3), (1, 2)), ((0, 1), (2, 3)))
    return [
        [((d * 4 + x) * 2 + core) * 4 + y for d in ds for x in xs for y in range(4)]
        for core in range(2)
        for ds in sets[core]
        for xs in sets[core]
    ]


def body(input_gates, recur_weight, hidden_init, cell_init, hidden_cot, frame_count):
    width = C
    out = jax.ShapeDtypeStruct
    vmem = pltpu.VMEM
    _, row_units = row_offsets(ROWS_A)
    _, col_units = col_offsets(ROWS_A)
    first_two = {2: (1, 2, R, L, 4 * C)}
    middle = hidden_cot[:, 1:2]
    border = out((row_units, L, C), BF)
    near, far = call(
        rows_a_kernel, (hidden_init, cell_init, input_gates, middle), [border] * 2, [], first_two, name="rows_a"
    )
    near_r, far_r = swap_rows(near, far)
    strip = out((col_units, C), BF)
    near, far = call(
        cols_a_kernel,
        (hidden_init, cell_init, input_gates, middle, near_r, far_r),
        [strip] * 2,
        [vmem((row_units, L, C), BF)] * 2 + [vmem((col_units, C), F32)] * 2,
        first_two,
        name="cols_a",
    )
    near_c, far_c = swap_cols(near, far)
    _, row_units_b = row_offsets(ROWS_B)
    _, col_units_b = col_offsets(ROWS_B)
    hidden_seq, patches, m1, m0, t1, g2, q, near, far = call(
        forward_kernel,
        (frame_count, hidden_init, cell_init, input_gates, hidden_cot, recur_weight, near_r, far_r, near_c, far_c),
        [
            out((1, 3, R, L, C), BF),
            out((3, R * L, 9 * C), BF),
            out((6, R + 2, W, C), BF),
            out((6, R, L, C), BF),
            out((R + 2, W, C), BF),
            out((R, L, 4 * C), BF),
            out((R, L, C), F32),
            out((row_units_b, L, C), BF),
            out((row_units_b, L, C), BF),
        ],
        [vmem((row_units, L, C), BF)] * 2
        + [vmem((col_units, C), F32)] * 2
        + [
            vmem((R + 6, 64, C), F32),
            vmem((R + 4, W, C), F32),
            vmem(((R + 4) * W, 4 * C), F32),
            vmem((3, R + 6, W, C), BF),
            vmem(((R + 4) * W, 9 * C), BF),
        ],
        scalar=True,
        name="forward",
        limit=28,
        flops=6 * 10**9,
    )
    near_r, far_r = swap_rows(near, far)
    flat_patches = patches.reshape(3 * R * L, 9 * C)
    other_patches = lax.ppermute(flat_patches, "core", CORES)
    strip = out((col_units_b, C), BF)
    near, far = call(
        cols_b_kernel,
        (g2, q, near_r, far_r),
        [strip] * 2,
        [vmem((row_units_b, L, C), BF)] * 2 + [vmem((col_units_b, C), F32)] * 2,
        name="cols_b",
    )
    near_c, far_c = swap_cols(near, far)
    g1, g0, _, cell_grad, near_c_rows, far_c_rows, mine, theirs = call(
        backward_kernel,
        (frame_count, hidden_cot, recur_weight, m1, m0, t1, g2, q, near_r, far_r, near_c, far_c),
        [out((R, L, 4 * C), BF), out((R, L, 4 * C), BF), out((1, R, L, C), F32), out((1, R, L, C), F32),
         out((4, L, C), BF), out((4, L, C), BF), out((512, 3 * C), BF), out((512, 3 * C), BF)],
        [vmem((row_units_b, L, C), BF)] * 2
        + [vmem((col_units_b, C), F32)] * 2
        + [vmem(((R + 4) * W, 4 * C), BF), vmem((R + 2, W, C), F32), vmem((3, R + 2, 64, C), F32), vmem((4 * C, 3 * C), BF)],
        {1: (1, 1, R, L, C)},
        scalar=True,
        name="backward",
        limit=24,
        flops=4 * 10**9,
    )
    _, col_units_c = col_offsets(ROWS_C)
    near_r, far_r = swap_rows(near_c_rows, far_c_rows)
    got = lax.ppermute(theirs, "core", CORES)
    (own_sum,) = call(own_sum_kernel, (mine, flat_patches), [out((512, 9 * C), F32)], [], name="own_sum", flops=2 * 10**9)
    got, near_r, far_r = lax.optimization_barrier((got, near_r, far_r))
    sent = call(
        chip_sum_kernel,
        (got, other_patches, own_sum),
        [out((256, HALF), BF)] * 4,
        [],
        name="chip_sum",
        flops=2 * 10**9,
    )
    strip = out((col_units_c, C), BF)
    near, far = call(
        cols_c_kernel,
        (g0, near_r, far_r),
        [strip] * 2,
        [vmem((4, L, C), BF)] * 2 + [vmem((col_units_c, C), F32)] * 2,
        name="cols_c",
    )
    near_c, far_c = swap_cols(near, far)
    came = first_partner(sent[1], "dp"), first_partner(sent[3], "x")
    *came, near_c, far_c = lax.optimization_barrier((*came, near_c, far_c))
    sent = call(halve_kernel, (sent[0], came[0], sent[2], came[1]), [out((128, HALF), BF)] * 4, [], name="halve")
    came = first_partner(sent[1], "x"), first_partner(sent[3], "dp")
    (hidden_grad,) = call(
        last_kernel,
        (g0, recur_weight, near_r, far_r, near_c, far_c),
        [out((1, R, L, C), BF)],
        [vmem((4, L, C), BF)] * 2
        + [vmem((col_units_c, C), F32)] * 2
        + [vmem(((R + 2) * W, 4 * C), BF), vmem((3, R, 64, C), F32)],
        name="last",
        flops=2 * 10**9,
    )
    *came, hidden_grad = lax.optimization_barrier((*came, hidden_grad))
    (blocks,) = call(
        quarter_kernel, (sent[0], came[0], sent[2], came[1]), [out((128, 9 * C), BF)], [], name="quarter"
    )
    parts = lax.all_to_all(blocks, AXES, 0, 0, tiled=True, axis_index_groups=owner_groups())
    (total,) = call(total_kernel, (parts.reshape(16, 8, 9 * C),), [out((8, 9 * C), F32)], [], name="total")
    weight_grad = total.T
    gate_grad = jnp.stack([g0, g1, g2])[None]
    return (hidden_seq, weight_grad, gate_grad, hidden_grad, cell_grad)


def solution(mesh):
    split = Mesh(mesh.devices.reshape(4, 4, 2, 4), ("dp", "x", "core", "sx"))
    sy = ("x", "core")
    step = jax.shard_map(
        body,
        mesh=split,
        in_specs=(
            P("dp", None, sy, "sx", None),
            P(),
            P("dp", sy, "sx", None),
            P("dp", sy, "sx", None),
            P("dp", None, sy, "sx", None),
            P("dp"),
        ),
        out_specs=(
            P("dp", None, sy, "sx", None),
            P(None, ("dp", "x", "core", "sx")),
            P("dp", None, sy, "sx", None),
            P("dp", sy, "sx", None),
            P("dp", sy, "sx", None),
        ),
        check_vma=False,
    )
    return step
```

```python
import functools

import jax
import jax.numpy as jnp
from jax import lax
from jax.experimental import pallas as pl
from jax.experimental.pallas import tpu as pltpu
from jax.sharding import Mesh, PartitionSpec as P


def ring_pairs(size, phase):
    pairs = [(i, (i + 1) % size) for i in range(phase, size, 2)]
    return [edge for a, b in pairs for edge in ((a, b), (b, a))]


CORES = [(0, 1), (1, 0)]
AXES = ("dp", "x", "core", "sx")
HALF = 1152
BF = jnp.bfloat16
F32 = jnp.float32
R, L, C = 8, 32, 256
W = 48
ROWS_A = (("h", 3, 1), ("c", 2, 1), ("x0", 2, 4), ("x1", 1, 4), ("t1", 1, 1))
ROWS_B = (("g", 2, 4), ("q", 1, 1))
ROWS_C = (("g", 1, 4),)


def row_offsets(spec):
    table, at = {}, 0
    for name, width, parts in spec:
        for row in range(width):
            for part in range(parts):
                table[name, row, part] = at
                at += 1
    return table, at


def col_offsets(spec):
    table, at = {}, 0
    for name, width, parts in spec:
        for part in range(parts):
            for row in range(R + 2 * width):
                table[name, row, part] = at
                at += width
    return table, -(-at // 16) * 16


def quarter(part):
    return slice(part * C, (part + 1) * C)


def parities():
    return lax.axis_index("core"), lax.axis_index("sx") % 2


def arranged(odd, near, far, before, after):
    @pl.when(odd == 1)
    def _():
        before[...] = near[...]
        after[...] = far[...]

    @pl.when(odd == 0)
    def _():
        before[...] = far[...]
        after[...] = near[...]


def pack_columns(spec, own, above, below, odd, near, far, left, right):
    rows, _ = row_offsets(spec)
    cols, _ = col_offsets(spec)
    for name, width, parts in spec:
        for row in range(R + 2 * width):
            for part in range(parts):
                at = cols[name, row, part]
                if row < width:
                    unit = rows[name, row, part]
                    first, last = above[unit, 0:8, :], above[unit, 24:32, :]
                elif row >= R + width:
                    unit = rows[name, row - R - width, part]
                    first, last = below[unit, 0:8, :], below[unit, 24:32, :]
                else:
                    first, last = own(name, row - width, slice(0, 8), part), own(name, row - width, slice(24, 32), part)
                left[at : at + width, :] = first.astype(F32)[0:width]
                right[at : at + width, :] = last.astype(F32)[8 - width : 8]

    @pl.when(odd == 1)
    def _():
        near[...] = left[...].astype(BF)
        far[...] = right[...].astype(BF)

    @pl.when(odd == 0)
    def _():
        near[...] = right[...].astype(BF)
        far[...] = left[...].astype(BF)


def rows_a_kernel(h_ref, c_ref, x_ref, t_ref, near, far, cells, sems):
    odd, _ = parities()
    rows, _ = row_offsets(ROWS_A)
    copies = []

    def start(source, target):
        copy = pltpu.make_async_copy(source, target, sems.at[len(copies)])
        copy.start()
        copies.append(copy)

    for side, out in enumerate((near, far)):
        top = odd == 1 if side == 0 else odd == 0
        for name, width, parts in ROWS_A:
            first = jnp.where(top, 0, R - width)
            at = pl.ds(first, width)
            unit = rows[name, 0, 0]
            if name == "h":
                start(h_ref.at[0, at], out.at[unit : unit + width])
            elif name == "c":
                start(c_ref.at[0, at], cells.at[side])
            elif name == "t1":
                start(t_ref.at[0, 1, at], out.at[unit : unit + width])
            else:
                for row in range(width):
                    for part in range(parts):
                        start(x_ref.at[0, int(name[1]), first + row, :, quarter(part)], out.at[rows[name, row, part]])
    for copy in copies:
        copy.wait()
    for side, out in enumerate((near, far)):
        for row in range(2):
            out[rows["c", row, 0]] = cells[side, row].astype(BF)


def cols_a_kernel(h_ref, c_ref, x_ref, t_ref, near_r, far_r, near, far, above, below, left, right):
    row_odd, col_odd = parities()
    arranged(row_odd, near_r, far_r, above, below)

    def own(name, row, cells, part):
        if name == "h":
            return h_ref[0, row, cells]
        if name == "c":
            return c_ref[0, row, cells]
        if name == "t1":
            return t_ref[0, 1, row, cells]
        return x_ref[0, int(name[1]), row, cells, quarter(part)]

    pack_columns(ROWS_A, own, above, below, col_odd, near, far, left, right)


def cols_b_kernel(g_ref, q_ref, near_r, far_r, near, far, above, below, left, right):
    row_odd, col_odd = parities()
    arranged(row_odd, near_r, far_r, above, below)

    def own(name, row, cells, part):
        if name == "q":
            return q_ref[row, cells]
        return g_ref[row, cells, quarter(part)]

    pack_columns(ROWS_B, own, above, below, col_odd, near, far, left, right)


def cols_c_kernel(g_ref, near_r, far_r, near, far, above, below, left, right):
    row_odd, col_odd = parities()
    arranged(row_odd, near_r, far_r, above, below)

    def own(name, row, cells, part):
        return g_ref[row, cells, quarter(part)]

    pack_columns(ROWS_C, own, above, below, col_odd, near, far, left, right)


def unpack_columns(odd, near, far, left, right):
    @pl.when(odd == 1)
    def _():
        left[...] = near[...].astype(F32)
        right[...] = far[...].astype(F32)

    @pl.when(odd == 0)
    def _():
        left[...] = far[...].astype(F32)
        right[...] = near[...].astype(F32)


def border(at, width, left, right):
    cell = lax.broadcasted_iota(jnp.int32, (16, C), 0)
    out = jnp.zeros((16, C), F32)
    for i in range(width):
        out = jnp.where(cell == i, jnp.broadcast_to(right[at + i : at + i + 1, :], (16, C)), out)
        out = jnp.where(cell == 16 - width + i, jnp.broadcast_to(left[at + i : at + i + 1, :], (16, C)), out)
    return out


def widened_grads(spec, width, g_ref, above, below, left, right, gw):
    rows, _ = row_offsets(spec)
    cols, _ = col_offsets(spec)
    for row in range(R + 2 * width):
        fits = inside(width, row)
        for part in range(4):
            if row < width:
                mid = above[rows["g", row, part]]
            elif row >= R + width:
                mid = below[rows["g", row - R - width, part]]
            else:
                mid = g_ref[row - width, :, quarter(part)]
            full = jnp.concatenate([mid.astype(F32), border(cols["g", row, part], width, left, right)], axis=0)
            gw[row * W : (row + 1) * W, quarter(part)] = jnp.where(fits, full, 0.0).astype(BF)


def back(n, gw, w_ref, z):
    cells = n * W
    for side in range(3):
        total = None
        for up in range(3):
            k = up * 3 + side
            slab = gw[(2 - up) * W : (2 - up) * W + cells, :]
            term = lax.dot_general(
                slab, w_ref[k * C : (k + 1) * C, :], (((1,), (1,)), ((), ())), preferred_element_type=F32
            )
            total = term if total is None else total + term
        z[side, 0:n, 8:56, :] = total.reshape(n, W, C)

    def wrap(row, carry):
        z[0, row, 56:57, :] = z[0, row, 8:9, :]
        z[2, row, 7:8, :] = z[2, row, 55:56, :]
        return carry

    lax.fori_loop(0, n, wrap, 0)


def summed(z, row, cells):
    return z[0, row, 9 : 9 + cells, :] + z[1, row, 8 : 8 + cells, :] + z[2, row, 7 : 7 + cells, :]


def last_kernel(g_ref, w_ref, near_r, far_r, near_c, far_c, dh_ref, above, below, left, right, gw, z):
    row_odd, col_odd = parities()
    arranged(row_odd, near_r, far_r, above, below)
    unpack_columns(col_odd, near_c, far_c, left, right)
    widened_grads(ROWS_C, 1, g_ref, above, below, left, right, gw)
    back(R, gw, w_ref, z)

    def one(row, carry):
        dh_ref[0, row] = summed(z, row, L).astype(BF)
        return carry

    lax.fori_loop(0, R, one, 0)


def set_member(core, place, half, j):
    near = jnp.where((place == 1) | (place == 2), 1, 0)
    kind = jnp.where(core == 0, near, place // 2)
    kind = jnp.where(half == 1, 1 - kind, kind)
    return jnp.where(core == 0, kind + j * (3 - 2 * kind), 2 * kind + j)


def turn(grads, turned, mine_ref, theirs_ref):
    core = lax.axis_index("core")
    for frame, g_ref in enumerate(grads):
        flat = g_ref[...].reshape(R * L, 4 * C).astype(F32)
        turned[:, quarter(frame)] = jnp.transpose(flat).astype(BF)

    place = {axis: lax.axis_index(axis) for axis in ("dp", "x")}

    def pick(block, carry):
        at = pl.ds(pl.multiple_of(block * 32, 32), 32)
        outer, inner = block // 4, block % 4
        for who, out in ((core, mine_ref), (1 - core, theirs_ref)):
            d = set_member(who, place["dp"], outer // 2, outer % 2)
            x = set_member(who, place["x"], inner // 2, inner % 2)
            out[at, :] = turned[pl.ds(pl.multiple_of(((d * 4 + x) * 2 + who) * 32, 32), 32), :]
        return carry

    lax.fori_loop(0, 16, pick, 0)


def own_sum_kernel(mine_ref, p_ref, out_ref):
    def one(n, carry):
        at = pl.ds(pl.multiple_of(n * 3 * C, C), 3 * C)
        out_ref[:, at] = jnp.dot(mine_ref[...], p_ref[:, at], preferred_element_type=F32)
        return carry

    lax.fori_loop(0, 3, one, 0)


def parted(rows, total, keep, send):
    for block in range(keep.shape[0] // rows):
        src = block * 2 * rows
        keep[block * rows : (block + 1) * rows, :] = total[src : src + rows].astype(BF)
        send[block * rows : (block + 1) * rows, :] = total[src + rows : src + 2 * rows].astype(BF)


def chip_sum_kernel(got_ref, p_ref, own_ref, keep0, send0, keep1, send1):
    for color, (rows, keep, send) in enumerate(((256, keep0, send0), (64, keep1, send1))):
        at = slice(color * HALF, (color + 1) * HALF)
        total = own_ref[:, at] + jnp.dot(got_ref[...], p_ref[:, at], preferred_element_type=F32)
        parted(rows, total, keep, send)


def halve_kernel(kept0, came0, kept1, came1, keep0, send0, keep1, send1):
    parted(64, kept0[...].astype(F32) + came0[...].astype(F32), keep0, send0)
    parted(128, kept1[...].astype(F32) + came1[...].astype(F32), keep1, send1)


def quarter_kernel(kept0, came0, kept1, came1, out_ref):
    out_ref[:, 0:HALF] = (kept0[...].astype(F32) + came0[...].astype(F32)).astype(BF)
    out_ref[:, HALF:] = (kept1[...].astype(F32) + came1[...].astype(F32)).astype(BF)


def total_kernel(parts_ref, out_ref):
    def one(i, carry):
        out_ref[...] = out_ref[...] + parts_ref[i].astype(F32)
        return carry

    out_ref[...] = jnp.zeros_like(out_ref)
    lax.fori_loop(0, 16, one, 0)


def inside(by, row):
    at_row = (lax.axis_index("x") * 2 + lax.axis_index("core")) * R + row - by
    cell = lax.broadcasted_iota(jnp.int32, (W, C), 0)
    column = jnp.where(cell < 40, cell, cell - W) + lax.axis_index("sx") * L
    fits = (column >= 0) & (column < 4 * L)
    return fits & jnp.broadcast_to((at_row >= 0) & (at_row < 8 * R), (W, C))


def sigmoid(value):
    return 0.5 * jnp.tanh(0.5 * value) + 0.5


def load_kernel(w_hbm, w_ref, sems):
    copies = [
        pltpu.make_async_copy(w_hbm.at[quarter(i)], w_ref.at[quarter(i)], sems.at[i]) for i in range(9)
    ]
    for copy in copies:
        copy.start()
    for copy in copies:
        copy.wait()


def forward_kernel(count_ref, h_ref, c_ref, x_ref, t_ref, w_ref, near_r, far_r, near_c, far_c,
                   seq_ref, patch_ref, m1_ref, m0_ref, t1_ref, g2_ref, q_ref, near_out, far_out,
                   above, below, left, right, hs, cs, gates, shifted, wide):
    row_odd, col_odd = parities()
    count = count_ref[0]
    arranged(row_odd, near_r, far_r, above, below)

    unpack_columns(col_odd, near_c, far_c, left, right)

    rows, _ = row_offsets(ROWS_A)
    cols, _ = col_offsets(ROWS_A)
    widths = {name: width for name, width, _ in ROWS_A}

    def main(name, row, part):
        width = widths[name]
        if row < width:
            return above[rows[name, row, part]].astype(F32)
        if row >= R + width:
            return below[rows[name, row - R - width, part]].astype(F32)
        row -= width
        if name == "h":
            return h_ref[0, row].astype(F32)
        if name == "c":
            return c_ref[0, row]
        if name == "t1":
            return t_ref[0, 1, row].astype(F32)
        return x_ref[0, int(name[1]), row, :, quarter(part)].astype(F32)

    def sides(name, row, part):
        width = widths[name]
        at = cols[name, row, part]
        return right[at : at + width, :], left[at : at + width, :]

    zero16 = jnp.zeros((16, C), F32)
    hs[...] = jnp.zeros_like(hs)
    for row in range(R + 6):
        hs[row, 8:40, :] = main("h", row, 0)
        after, before = sides("h", row, 0)
        hs[row, 40:43, :] = after
        hs[row, 53:56, :] = before
        hs[row, 8:56, :] = jnp.where(inside(3, row), hs[row, 8:56, :], 0.0)
    for row in range(R + 4):
        cs[row, 0:32, :] = main("c", row, 0)
        cs[row, 32:48, :] = zero16
        after, before = sides("c", row, 0)
        cs[row, 32:34, :] = after
        cs[row, 46:48, :] = before

    def load_gates(name, by):
        for row in range(R + 2 * by):
            for part in range(4):
                at = row * W
                gates[at : at + 32, quarter(part)] = main(name, row, part)
                gates[at + 32 : at + W, quarter(part)] = zero16
                after, before = sides(name, row, part)
                gates[at + 32 : at + 32 + by, quarter(part)] = after
                gates[at + W - by : at + W, quarter(part)] = before

    def shift(n_rows):
        def one(row, carry):
            hs[row, 7:8, :] = hs[row, 55:56, :]
            hs[row, 56:57, :] = hs[row, 8:9, :]
            for side in range(3):
                shifted[side, row] = hs[row, 7 + side : 55 + side, :].astype(BF)
            return carry

        lax.fori_loop(0, n_rows, one, 0)

    def own_patches(frame, by):
        for k in range(9):
            up, side = k // 3, k % 3
            patch_ref[frame, :, quarter(k)] = shifted[side, by + up : by + up + R, 0:32, :].reshape(R * L, C)

    for frame in range(3):
        by = 2 - frame
        n = R + 2 * by
        cells = n * W if by else R * L
        valid = frame < count
        wcols = W if by else L
        shift(n + 2)
        own_patches(frame, by)
        if by:
            load_gates("x" + str(frame), by)
            for k in range(9):
                up, side = k // 3, k % 3
                wide[0:cells, quarter(k)] = shifted[side, up : up + n].reshape(cells, C)

            def one(at_n, carry, cells=cells):
                at = pl.ds(pl.multiple_of(at_n * 2 * C, C), 2 * C)
                gates[0:cells, at] = gates[0:cells, at] + jnp.dot(
                    wide[0:cells, :], w_ref[:, at], preferred_element_type=F32
                )
                return carry
        else:

            def one(at_n, carry):
                at = pl.ds(pl.multiple_of(at_n * 2 * C, C), 2 * C)
                gates[0 : R * L, at] = x_ref[0, 2, :, :, at].reshape(R * L, 2 * C).astype(F32) + jnp.dot(
                    patch_ref[2], w_ref[:, at], preferred_element_type=F32
                )
                return carry

        lax.fori_loop(0, 2, one, 0)

        def gating(row, carry, frame=frame, by=by, wcols=wcols, valid=valid):
            start = pl.multiple_of(row * wcols, 16)
            g = gates[pl.ds(start, wcols), :]
            si = sigmoid(g[:, 0:C])
            sf = sigmoid(g[:, C : 2 * C])
            tg = jnp.tanh(g[:, 2 * C : 3 * C])
            so = sigmoid(g[:, 3 * C :])
            cell = cs[row + (0 if frame == 0 else frame), 0:wcols, :]
            cell_new = sf * cell + si * tg
            tc = jnp.tanh(cell_new)
            h_new = (so * tc).astype(BF).astype(F32)
            factors = (
                so * (1.0 - tc * tc),
                tg * si * (1.0 - si),
                cell * sf * (1.0 - sf),
                si * (1.0 - tg * tg),
                tc * so * (1.0 - so),
                sf,
            )
            h_old = hs[row + 1, 8 : 8 + wcols, :]
            keep = jnp.broadcast_to(valid, h_new.shape)
            h_next = jnp.where(keep, h_new, h_old)
            cs[row + frame, 0:wcols, :] = jnp.where(keep, cell_new, cell)
            if by:
                hs[row, 8:56, :] = jnp.where(inside(by, row), h_next, 0.0)
            if frame == 0:

                @pl.when((row >= 2) & (row < 2 + R))
                def _():
                    seq_ref[0, 0, row - 2] = h_next[0:L].astype(BF)
                    for i, factor in enumerate(factors):
                        m0_ref[i, row - 2] = factor[0:L].astype(BF)
            elif frame == 1:
                for i, factor in enumerate(factors):
                    m1_ref[i, row] = factor.astype(BF)

                @pl.when((row >= 1) & (row < 1 + R))
                def _():
                    seq_ref[0, 1, row - 1] = h_next[0:L].astype(BF)
            else:
                seq_ref[0, 2, row] = h_next.astype(BF)
                a, bi, bfg, bg, bo, _ = factors
                grad_h = t_ref[0, 2, row].astype(F32)
                dc_new = grad_h * a
                for part, value in enumerate((dc_new * bi, dc_new * bfg, dc_new * bg, grad_h * bo)):
                    g2_ref[row, :, quarter(part)] = jnp.where(keep, value, 0.0).astype(BF)
                q_ref[row] = jnp.where(keep, dc_new * sf, grad_h)
            return carry

        lax.fori_loop(0, n, gating, 0)
    for row in range(R + 2):
        t1_ref[row, 0:32, :] = main("t1", row, 0).astype(BF)
        after, before = sides("t1", row, 0)
        cell = lax.broadcasted_iota(jnp.int32, (16, C), 0)
        pad = jnp.where(cell == 0, jnp.broadcast_to(after, (16, C)), jnp.where(cell == 15, jnp.broadcast_to(before, (16, C)), 0.0))
        t1_ref[row, 32:48, :] = pad.astype(BF)
    rows_b, _ = row_offsets(ROWS_B)
    for name, width, parts in ROWS_B:
        first = jnp.where(row_odd == 1, 0, R - width)
        last = jnp.where(row_odd == 1, R - width, 0)
        for row in range(width):
            for part in range(parts):
                unit = rows_b[name, row, part]
                for start, out in ((first, near_out), (last, far_out)):
                    if name == "q":
                        out[unit] = q_ref[start + row].astype(BF)
                    else:
                        out[unit] = g2_ref[start + row, :, quarter(part)]


def backward_kernel(count_ref, t0_ref, w_ref, m1_ref, m0_ref, t1_ref, g2_ref, q_ref, near_r, far_r, near_c, far_c,
                    g1_ref, g0_ref, dh_ref, dc_ref, near_out, far_out, mine_ref, theirs_ref, above, below, left, right, gw, qs, z, turned):
    row_odd, col_odd = parities()
    count = count_ref[0]
    arranged(row_odd, near_r, far_r, above, below)

    unpack_columns(col_odd, near_c, far_c, left, right)

    rows, _ = row_offsets(ROWS_B)
    cols, _ = col_offsets(ROWS_B)
    valid2, valid1 = 2 < count, 1 < count
    widened_grads(ROWS_B, 2, g2_ref, above, below, left, right, gw)
    for row in range(R + 2):
        if row < 1:
            mid = above[rows["q", 0, 0]].astype(F32)
        elif row >= R + 1:
            mid = below[rows["q", 0, 0]].astype(F32)
        else:
            mid = q_ref[row - 1]
        qs[row, 0:32, :] = mid
        qs[row, 32:48, :] = border(cols["q", row, 0], 1, left, right)

    back(R + 2, gw, w_ref, z)

    def first(row, carry):
        keep2 = jnp.broadcast_to(valid2, (W, C))
        keep1 = jnp.broadcast_to(valid1, (W, C))
        q = qs[row]
        grad_h = jnp.where(keep2, summed(z, row, W), q) + t1_ref[row].astype(F32)
        grad_c = jnp.where(keep2, q, 0.0)
        a, bi, bfg, bg, bo, sf = (m1_ref[i, row].astype(F32) for i in range(6))
        dc_new = grad_c + grad_h * a
        keep = keep1 & inside(1, row)
        at = pl.ds(pl.multiple_of(row * W, W), W)
        for part, value in enumerate((dc_new * bi, dc_new * bfg, dc_new * bg, grad_h * bo)):
            gw[at, quarter(part)] = jnp.where(keep, value, 0.0).astype(BF)

        @pl.when((row >= 1) & (row < 1 + R))
        def _():
            dc_ref[0, row - 1] = jnp.where(keep1, dc_new * sf, grad_c)[0:L]
            dh_ref[0, row - 1] = grad_h[0:L]
            for part in range(4):
                g1_ref[row - 1, :, quarter(part)] = gw[pl.ds(pl.multiple_of(row * W, W), L), quarter(part)]

        return carry

    lax.fori_loop(0, R + 2, first, 0)
    back(R, gw, w_ref, z)

    def second(row, carry):
        keep1 = jnp.broadcast_to(valid1, (L, C))
        grad_h = jnp.where(keep1, summed(z, row, L), dh_ref[0, row]) + t0_ref[0, 0, row].astype(F32)
        a, bi, bfg, bg, bo, sf = (m0_ref[i, row].astype(F32) for i in range(6))
        dc_new = dc_ref[0, row] + grad_h * a
        for part, value in enumerate((dc_new * bi, dc_new * bfg, dc_new * bg, grad_h * bo)):
            g0_ref[row, :, quarter(part)] = value.astype(BF)
        dc_ref[0, row] = dc_new * sf
        return carry

    lax.fori_loop(0, R, second, 0)
    first_row = jnp.where(row_odd == 1, 0, R - 1)
    last_row = jnp.where(row_odd == 1, R - 1, 0)
    for part in range(4):
        near_out[part] = g0_ref[first_row, :, quarter(part)]
        far_out[part] = g0_ref[last_row, :, quarter(part)]
    turn((g0_ref, g1_ref, g2_ref), turned, mine_ref, theirs_ref)


def whole(shape):
    return pl.BlockSpec(shape, lambda _: (0,) * len(shape))


def call(kernel, inputs, outs, scratch, blocks=None, scalar=False, name=None, flops=0, limit=16, outside=()):
    blocks = blocks or {}
    specs = [whole(blocks.get(i, value.shape)) for i, value in enumerate(inputs)]
    inputs = list(inputs)
    for i in outside:
        specs[i] = pl.BlockSpec(memory_space=pltpu.HBM)
        inputs[i] = pltpu.with_memory_space_constraint(inputs[i], pltpu.HBM)
    if scalar:
        specs[0] = pl.BlockSpec(memory_space=pltpu.SMEM)
    size = sum(value.size * value.dtype.itemsize for value in inputs)
    return pl.pallas_call(
        kernel,
        grid=(1,),
        in_specs=specs,
        out_specs=[whole(out.shape) for out in outs],
        out_shape=outs,
        scratch_shapes=scratch,
        name=name,
        compiler_params=pltpu.CompilerParams(vmem_limit_bytes=limit << 20),
        cost_estimate=pl.CostEstimate(flops=flops, bytes_accessed=size, transcendentals=0),
    )(*inputs)


def swap_rows(near, far):
    axis = ("x", "core")
    return lax.ppermute(near, axis, ring_pairs(8, 0)), lax.ppermute(far, axis, ring_pairs(8, 1))


def swap_cols(near, far):
    return lax.ppermute(near, "sx", ring_pairs(4, 0)), lax.ppermute(far, "sx", ring_pairs(4, 1))


def first_partner(value, axis):
    flips = (1, 3)
    pairs = [(i * 2 + c, (i ^ flips[c]) * 2 + c) for i in range(4) for c in range(2)]
    return lax.ppermute(value, (axis, "core"), pairs)


def owner_groups():
    sets = (((0, 3), (1, 2)), ((0, 1), (2, 3)))
    return [
        [((d * 4 + x) * 2 + core) * 4 + y for d in ds for x in xs for y in range(4)]
        for core in range(2)
        for ds in sets[core]
        for xs in sets[core]
    ]


def body(input_gates, recur_weight, hidden_init, cell_init, hidden_cot, frame_count):
    width = C
    out = jax.ShapeDtypeStruct
    vmem = pltpu.VMEM
    _, row_units = row_offsets(ROWS_A)
    _, col_units = col_offsets(ROWS_A)
    first_two = {2: (1, 2, R, L, 4 * C)}
    border = out((row_units, L, C), BF)
    near, far = call(
        rows_a_kernel,
        (hidden_init, cell_init, input_gates, hidden_cot),
        [border] * 2,
        [vmem((2, 2, L, C), F32), pltpu.SemaphoreType.DMA((30,))],
        name="rows_a",
        outside=(0, 1, 2, 3),
    )
    near_r, far_r = swap_rows(near, far)
    strip = out((col_units, C), BF)
    near, far = call(
        cols_a_kernel,
        (hidden_init, cell_init, input_gates, hidden_cot, near_r, far_r),
        [strip] * 2,
        [vmem((row_units, L, C), BF)] * 2 + [vmem((col_units, C), F32)] * 2,
        first_two,
        name="cols_a",
    )
    near_c, far_c = swap_cols(near, far)
    weight_in, _ = lax.optimization_barrier((recur_weight, near))
    (recur_weight,) = call(
        load_kernel,
        (weight_in,),
        [out((9 * C, 4 * C), BF)],
        [pltpu.SemaphoreType.DMA((9,))],
        name="load",
        outside=(0,),
    )
    _, row_units_b = row_offsets(ROWS_B)
    _, col_units_b = col_offsets(ROWS_B)
    hidden_seq, patches, m1, m0, t1, g2, q, near, far = call(
        forward_kernel,
        (frame_count, hidden_init, cell_init, input_gates, hidden_cot, recur_weight, near_r, far_r, near_c, far_c),
        [
            out((1, 3, R, L, C), BF),
            out((3, R * L, 9 * C), BF),
            out((6, R + 2, W, C), BF),
            out((6, R, L, C), BF),
            out((R + 2, W, C), BF),
            out((R, L, 4 * C), BF),
            out((R, L, C), F32),
            out((row_units_b, L, C), BF),
            out((row_units_b, L, C), BF),
        ],
        [vmem((row_units, L, C), BF)] * 2
        + [vmem((col_units, C), F32)] * 2
        + [
            vmem((R + 6, 64, C), F32),
            vmem((R + 4, W, C), F32),
            vmem(((R + 4) * W, 4 * C), F32),
            vmem((3, R + 6, W, C), BF),
            vmem(((R + 4) * W, 9 * C), BF),
        ],
        scalar=True,
        name="forward",
        limit=28,
        flops=6 * 10**9,
    )
    near_r, far_r = swap_rows(near, far)
    flat_patches = patches.reshape(3 * R * L, 9 * C)
    other_patches = lax.ppermute(flat_patches, "core", CORES)
    strip = out((col_units_b, C), BF)
    near, far = call(
        cols_b_kernel,
        (g2, q, near_r, far_r),
        [strip] * 2,
        [vmem((row_units_b, L, C), BF)] * 2 + [vmem((col_units_b, C), F32)] * 2,
        name="cols_b",
    )
    near_c, far_c = swap_cols(near, far)
    g1, g0, _, cell_grad, near_c_rows, far_c_rows, mine, theirs = call(
        backward_kernel,
        (frame_count, hidden_cot, recur_weight, m1, m0, t1, g2, q, near_r, far_r, near_c, far_c),
        [out((R, L, 4 * C), BF), out((R, L, 4 * C), BF), out((1, R, L, C), F32), out((1, R, L, C), F32),
         out((4, L, C), BF), out((4, L, C), BF), out((512, 3 * C), BF), out((512, 3 * C), BF)],
        [vmem((row_units_b, L, C), BF)] * 2
        + [vmem((col_units_b, C), F32)] * 2
        + [vmem(((R + 4) * W, 4 * C), BF), vmem((R + 2, W, C), F32), vmem((3, R + 2, 64, C), F32), vmem((4 * C, 3 * C), BF)],
        {1: (1, 1, R, L, C)},
        scalar=True,
        name="backward",
        limit=24,
        flops=4 * 10**9,
    )
    _, col_units_c = col_offsets(ROWS_C)
    near_r, far_r = swap_rows(near_c_rows, far_c_rows)
    got = lax.ppermute(theirs, "core", CORES)
    (own_sum,) = call(own_sum_kernel, (mine, flat_patches), [out((512, 9 * C), F32)], [], name="own_sum", flops=2 * 10**9)
    got, near_r, far_r = lax.optimization_barrier((got, near_r, far_r))
    sent = call(
        chip_sum_kernel,
        (got, other_patches, own_sum),
        [out((256, HALF), BF)] * 4,
        [],
        name="chip_sum",
        flops=2 * 10**9,
    )
    strip = out((col_units_c, C), BF)
    near, far = call(
        cols_c_kernel,
        (g0, near_r, far_r),
        [strip] * 2,
        [vmem((4, L, C), BF)] * 2 + [vmem((col_units_c, C), F32)] * 2,
        name="cols_c",
    )
    near_c, far_c = swap_cols(near, far)
    came = first_partner(sent[1], "dp"), first_partner(sent[3], "x")
    *came, near_c, far_c = lax.optimization_barrier((*came, near_c, far_c))
    sent = call(halve_kernel, (sent[0], came[0], sent[2], came[1]), [out((128, HALF), BF)] * 4, [], name="halve")
    came = first_partner(sent[1], "x"), first_partner(sent[3], "dp")
    (hidden_grad,) = call(
        last_kernel,
        (g0, recur_weight, near_r, far_r, near_c, far_c),
        [out((1, R, L, C), BF)],
        [vmem((4, L, C), BF)] * 2
        + [vmem((col_units_c, C), F32)] * 2
        + [vmem(((R + 2) * W, 4 * C), BF), vmem((3, R, 64, C), F32)],
        name="last",
        flops=2 * 10**9,
    )
    *came, hidden_grad = lax.optimization_barrier((*came, hidden_grad))
    (blocks,) = call(
        quarter_kernel, (sent[0], came[0], sent[2], came[1]), [out((128, 9 * C), BF)], [], name="quarter"
    )
    parts = lax.all_to_all(blocks, AXES, 0, 0, tiled=True, axis_index_groups=owner_groups())
    (total,) = call(total_kernel, (parts.reshape(16, 8, 9 * C),), [out((8, 9 * C), F32)], [], name="total")
    weight_grad = total.T
    gate_grad = jnp.stack([g0, g1, g2])[None]
    return (hidden_seq, weight_grad, gate_grad, hidden_grad, cell_grad)


def solution(mesh):
    split = Mesh(mesh.devices.reshape(4, 4, 2, 4), ("dp", "x", "core", "sx"))
    sy = ("x", "core")
    step = jax.shard_map(
        body,
        mesh=split,
        in_specs=(
            P("dp", None, sy, "sx", None),
            P(),
            P("dp", sy, "sx", None),
            P("dp", sy, "sx", None),
            P("dp", None, sy, "sx", None),
            P("dp"),
        ),
        out_specs=(
            P("dp", None, sy, "sx", None),
            P(None, ("dp", "x", "core", "sx")),
            P("dp", None, sy, "sx", None),
            P("dp", sy, "sx", None),
            P("dp", sy, "sx", None),
        ),
        check_vma=False,
    )
    return step
```

```python
import functools

import jax
import jax.numpy as jnp
from jax import lax
from jax.experimental import pallas as pl
from jax.experimental.pallas import tpu as pltpu
from jax.sharding import Mesh, PartitionSpec as P


def ring_pairs(size, phase):
    pairs = [(i, (i + 1) % size) for i in range(phase, size, 2)]
    return [edge for a, b in pairs for edge in ((a, b), (b, a))]


CORES = [(0, 1), (1, 0)]
AXES = ("dp", "x", "core", "sx")
HALF = 1152
BF = jnp.bfloat16
F32 = jnp.float32
R, L, C = 8, 32, 256
W = 48
ROWS_A = (("h", 3, 1), ("c", 2, 1), ("x0", 2, 4), ("x1", 1, 4), ("t1", 1, 1))
ROWS_B = (("g", 2, 4), ("q", 1, 1))
ROWS_C = (("g", 1, 4),)


def row_offsets(spec):
    table, at = {}, 0
    for name, width, parts in spec:
        for row in range(width):
            for part in range(parts):
                table[name, row, part] = at
                at += 1
    return table, at


def col_offsets(spec):
    table, at = {}, 0
    for name, width, parts in spec:
        for part in range(parts):
            for row in range(R + 2 * width):
                table[name, row, part] = at
                at += width
    return table, -(-at // 16) * 16


def quarter(part):
    return slice(part * C, (part + 1) * C)


def parities():
    return lax.axis_index("core"), lax.axis_index("sx") % 2


def arranged(odd, near, far, before, after):
    @pl.when(odd == 1)
    def _():
        before[...] = near[...]
        after[...] = far[...]

    @pl.when(odd == 0)
    def _():
        before[...] = far[...]
        after[...] = near[...]


def pack_columns(spec, own, above, below, odd, near, far, left, right):
    rows, _ = row_offsets(spec)
    cols, _ = col_offsets(spec)
    for name, width, parts in spec:
        for row in range(R + 2 * width):
            for part in range(parts):
                at = cols[name, row, part]
                if row < width:
                    unit = rows[name, row, part]
                    first, last = above[unit, 0:8, :], above[unit, 24:32, :]
                elif row >= R + width:
                    unit = rows[name, row - R - width, part]
                    first, last = below[unit, 0:8, :], below[unit, 24:32, :]
                else:
                    first, last = own(name, row - width, slice(0, 8), part), own(name, row - width, slice(24, 32), part)
                left[at : at + width, :] = first.astype(F32)[0:width]
                right[at : at + width, :] = last.astype(F32)[8 - width : 8]

    @pl.when(odd == 1)
    def _():
        near[...] = left[...].astype(BF)
        far[...] = right[...].astype(BF)

    @pl.when(odd == 0)
    def _():
        near[...] = right[...].astype(BF)
        far[...] = left[...].astype(BF)


def rows_a_kernel(h_ref, c_ref, x_ref, t_ref, near, far, cells, sems):
    odd, _ = parities()
    rows, _ = row_offsets(ROWS_A)
    copies = []

    def start(source, target):
        copy = pltpu.make_async_copy(source, target, sems.at[len(copies)])
        copy.start()
        copies.append(copy)

    for side, out in enumerate((near, far)):
        top = odd == 1 if side == 0 else odd == 0
        for name, width, parts in ROWS_A:
            first = jnp.where(top, 0, R - width)
            at = pl.ds(first, width)
            unit = rows[name, 0, 0]
            if name == "h":
                start(h_ref.at[0, at], out.at[unit : unit + width])
            elif name == "c":
                start(c_ref.at[0, at], cells.at[side])
            elif name == "t1":
                start(t_ref.at[0, 1, at], out.at[unit : unit + width])
            else:
                for row in range(width):
                    for part in range(parts):
                        start(x_ref.at[0, int(name[1]), first + row, :, quarter(part)], out.at[rows[name, row, part]])
    for copy in copies:
        copy.wait()
    for side, out in enumerate((near, far)):
        for row in range(2):
            out[rows["c", row, 0]] = cells[side, row].astype(BF)


def cols_a_kernel(h_ref, c_ref, x_ref, t_ref, near_r, far_r, near, far, above, below, left, right):
    row_odd, col_odd = parities()
    arranged(row_odd, near_r, far_r, above, below)

    def own(name, row, cells, part):
        if name == "h":
            return h_ref[0, row, cells]
        if name == "c":
            return c_ref[0, row, cells]
        if name == "t1":
            return t_ref[0, 1, row, cells]
        return x_ref[0, int(name[1]), row, cells, quarter(part)]

    pack_columns(ROWS_A, own, above, below, col_odd, near, far, left, right)


def cols_b_kernel(g_ref, q_ref, near_r, far_r, near, far, above, below, left, right):
    row_odd, col_odd = parities()
    arranged(row_odd, near_r, far_r, above, below)

    def own(name, row, cells, part):
        if name == "q":
            return q_ref[row, cells]
        return g_ref[row, cells, quarter(part)]

    pack_columns(ROWS_B, own, above, below, col_odd, near, far, left, right)


def cols_c_kernel(g_ref, near_r, far_r, near, far, above, below, left, right):
    row_odd, col_odd = parities()
    arranged(row_odd, near_r, far_r, above, below)

    def own(name, row, cells, part):
        return g_ref[row, cells, quarter(part)]

    pack_columns(ROWS_C, own, above, below, col_odd, near, far, left, right)


def unpack_columns(odd, near, far, left, right):
    @pl.when(odd == 1)
    def _():
        left[...] = near[...].astype(F32)
        right[...] = far[...].astype(F32)

    @pl.when(odd == 0)
    def _():
        left[...] = far[...].astype(F32)
        right[...] = near[...].astype(F32)


def border(at, width, left, right):
    cell = lax.broadcasted_iota(jnp.int32, (16, C), 0)
    out = jnp.zeros((16, C), F32)
    for i in range(width):
        out = jnp.where(cell == i, jnp.broadcast_to(right[at + i : at + i + 1, :], (16, C)), out)
        out = jnp.where(cell == 16 - width + i, jnp.broadcast_to(left[at + i : at + i + 1, :], (16, C)), out)
    return out


def widened_grads(spec, width, g_ref, above, below, left, right, gw):
    rows, _ = row_offsets(spec)
    cols, _ = col_offsets(spec)
    for row in range(R + 2 * width):
        fits = inside(width, row)
        for part in range(4):
            if row < width:
                mid = above[rows["g", row, part]]
            elif row >= R + width:
                mid = below[rows["g", row - R - width, part]]
            else:
                mid = g_ref[row - width, :, quarter(part)]
            full = jnp.concatenate([mid.astype(F32), border(cols["g", row, part], width, left, right)], axis=0)
            gw[row * W : (row + 1) * W, quarter(part)] = jnp.where(fits, full, 0.0).astype(BF)


def back(n, gw, w_ref, z):
    cells = n * W
    for side in range(3):
        total = None
        for up in range(3):
            k = up * 3 + side
            slab = gw[(2 - up) * W : (2 - up) * W + cells, :]
            term = lax.dot_general(
                slab, w_ref[k * C : (k + 1) * C, :], (((1,), (1,)), ((), ())), preferred_element_type=F32
            )
            total = term if total is None else total + term
        z[side, 0:n, 8:56, :] = total.reshape(n, W, C)

    def wrap(row, carry):
        z[0, row, 56:57, :] = z[0, row, 8:9, :]
        z[2, row, 7:8, :] = z[2, row, 55:56, :]
        return carry

    lax.fori_loop(0, n, wrap, 0)


def summed(z, row, cells):
    return z[0, row, 9 : 9 + cells, :] + z[1, row, 8 : 8 + cells, :] + z[2, row, 7 : 7 + cells, :]


def last_kernel(g_ref, w_ref, near_r, far_r, near_c, far_c, dh_ref, above, below, left, right, gw, z):
    row_odd, col_odd = parities()
    arranged(row_odd, near_r, far_r, above, below)
    unpack_columns(col_odd, near_c, far_c, left, right)
    widened_grads(ROWS_C, 1, g_ref, above, below, left, right, gw)
    back(R, gw, w_ref, z)

    def one(row, carry):
        dh_ref[0, row] = summed(z, row, L).astype(BF)
        return carry

    lax.fori_loop(0, R, one, 0)


def set_member(core, place, half, j):
    near = jnp.where((place == 1) | (place == 2), 1, 0)
    kind = jnp.where(core == 0, near, place // 2)
    kind = jnp.where(half == 1, 1 - kind, kind)
    return jnp.where(core == 0, kind + j * (3 - 2 * kind), 2 * kind + j)


def turn(grads, turned, mine_ref, theirs_ref):
    core = lax.axis_index("core")
    for frame, g_ref in enumerate(grads):
        flat = g_ref[...].reshape(R * L, 4 * C).astype(F32)
        turned[:, quarter(frame)] = jnp.transpose(flat).astype(BF)

    place = {axis: lax.axis_index(axis) for axis in ("dp", "x")}

    def pick(block, carry):
        at = pl.ds(pl.multiple_of(block * 32, 32), 32)
        outer, inner = block // 4, block % 4
        for who, out in ((core, mine_ref), (1 - core, theirs_ref)):
            d = set_member(who, place["dp"], outer // 2, outer % 2)
            x = set_member(who, place["x"], inner // 2, inner % 2)
            out[at, :] = turned[pl.ds(pl.multiple_of(((d * 4 + x) * 2 + who) * 32, 32), 32), :]
        return carry

    lax.fori_loop(0, 16, pick, 0)


def own_sum_kernel(mine_ref, p_ref, out_ref):
    def one(n, carry):
        at = pl.ds(pl.multiple_of(n * 3 * C, C), 3 * C)
        out_ref[:, at] = jnp.dot(mine_ref[...], p_ref[:, at], preferred_element_type=F32)
        return carry

    lax.fori_loop(0, 3, one, 0)


def parted(rows, total, keep, send):
    for block in range(keep.shape[0] // rows):
        src = block * 2 * rows
        keep[block * rows : (block + 1) * rows, :] = total[src : src + rows].astype(BF)
        send[block * rows : (block + 1) * rows, :] = total[src + rows : src + 2 * rows].astype(BF)


def chip_sum_kernel(got_ref, p_ref, own_ref, keep0, send0, keep1, send1):
    for color, (rows, keep, send) in enumerate(((256, keep0, send0), (64, keep1, send1))):
        at = slice(color * HALF, (color + 1) * HALF)
        total = own_ref[:, at] + jnp.dot(got_ref[...], p_ref[:, at], preferred_element_type=F32)
        parted(rows, total, keep, send)


def halve_kernel(kept0, came0, kept1, came1, keep0, send0, keep1, send1):
    parted(64, kept0[...].astype(F32) + came0[...].astype(F32), keep0, send0)
    parted(128, kept1[...].astype(F32) + came1[...].astype(F32), keep1, send1)


def quarter_kernel(kept0, came0, kept1, came1, out_ref):
    out_ref[:, 0:HALF] = (kept0[...].astype(F32) + came0[...].astype(F32)).astype(BF)
    out_ref[:, HALF:] = (kept1[...].astype(F32) + came1[...].astype(F32)).astype(BF)


def total_kernel(parts_ref, out_ref):
    def one(i, carry):
        out_ref[...] = out_ref[...] + parts_ref[i].astype(F32)
        return carry

    out_ref[...] = jnp.zeros_like(out_ref)
    lax.fori_loop(0, 16, one, 0)


def inside(by, row):
    at_row = (lax.axis_index("x") * 2 + lax.axis_index("core")) * R + row - by
    cell = lax.broadcasted_iota(jnp.int32, (W, C), 0)
    column = jnp.where(cell < 40, cell, cell - W) + lax.axis_index("sx") * L
    fits = (column >= 0) & (column < 4 * L)
    return fits & jnp.broadcast_to((at_row >= 0) & (at_row < 8 * R), (W, C))


def sigmoid(value):
    return 0.5 * jnp.tanh(0.5 * value) + 0.5


def load_kernel(w_hbm, w_ref, sems):
    copies = [
        pltpu.make_async_copy(w_hbm.at[quarter(i)], w_ref.at[quarter(i)], sems.at[i]) for i in range(9)
    ]
    for copy in copies:
        copy.start()
    for copy in copies:
        copy.wait()


def ahead_kernel(h_ref, w_ref, near_r, far_r, out_ref, above, below, hs, shifted, wide):
    row_odd, _ = parities()
    arranged(row_odd, near_r, far_r, above, below)
    rows, _ = row_offsets(ROWS_A)
    n = R + 4
    hs[...] = jnp.zeros_like(hs)
    for row in range(R + 6):
        if row < 3:
            mid = above[rows["h", row, 0]]
        elif row >= R + 3:
            mid = below[rows["h", row - R - 3, 0]]
        else:
            mid = h_ref[0, row - 3]
        hs[row, 8:40, :] = jnp.where(inside(3, row)[0:L], mid.astype(F32), 0.0)
        for side in range(3):
            shifted[side, row] = hs[row, 7 + side : 39 + side, :].astype(BF)
    for k in range(9):
        up, side = k // 3, k % 3
        wide[:, quarter(k)] = shifted[side, up : up + n].reshape(n * L, C)

    def one(at_n, carry):
        at = pl.ds(pl.multiple_of(at_n * 2 * C, C), 2 * C)
        out_ref[:, at] = jnp.dot(wide[...], w_ref[:, at], preferred_element_type=F32)
        return carry

    lax.fori_loop(0, 2, one, 0)


def forward_kernel(count_ref, h_ref, c_ref, x_ref, t_ref, w_ref, main_ref, near_r, far_r, near_c, far_c,
                   seq_ref, patch_ref, m1_ref, m0_ref, t1_ref, g2_ref, q_ref, near_out, far_out,
                   above, below, left, right, hs, cs, gates, shifted, wide, edge, edge_gates):
    row_odd, col_odd = parities()
    count = count_ref[0]
    arranged(row_odd, near_r, far_r, above, below)

    unpack_columns(col_odd, near_c, far_c, left, right)

    rows, _ = row_offsets(ROWS_A)
    cols, _ = col_offsets(ROWS_A)
    widths = {name: width for name, width, _ in ROWS_A}

    def main(name, row, part):
        width = widths[name]
        if row < width:
            return above[rows[name, row, part]].astype(F32)
        if row >= R + width:
            return below[rows[name, row - R - width, part]].astype(F32)
        row -= width
        if name == "h":
            return h_ref[0, row].astype(F32)
        if name == "c":
            return c_ref[0, row]
        if name == "t1":
            return t_ref[0, 1, row].astype(F32)
        return x_ref[0, int(name[1]), row, :, quarter(part)].astype(F32)

    def sides(name, row, part):
        width = widths[name]
        at = cols[name, row, part]
        return right[at : at + width, :], left[at : at + width, :]

    zero16 = jnp.zeros((16, C), F32)
    hs[...] = jnp.zeros_like(hs)
    for row in range(R + 6):
        hs[row, 8:40, :] = main("h", row, 0)
        after, before = sides("h", row, 0)
        hs[row, 40:43, :] = after
        hs[row, 53:56, :] = before
        hs[row, 8:56, :] = jnp.where(inside(3, row), hs[row, 8:56, :], 0.0)
    for row in range(R + 4):
        cs[row, 0:32, :] = main("c", row, 0)
        cs[row, 32:48, :] = zero16
        after, before = sides("c", row, 0)
        cs[row, 32:34, :] = after
        cs[row, 46:48, :] = before

    def load_gates(name, by):
        for row in range(R + 2 * by):
            for part in range(4):
                at = row * W
                gates[at : at + 32, quarter(part)] = main(name, row, part)
                gates[at + 32 : at + W, quarter(part)] = zero16
                after, before = sides(name, row, part)
                gates[at + 32 : at + 32 + by, quarter(part)] = after
                gates[at + W - by : at + W, quarter(part)] = before

    def shift(n_rows):
        def one(row, carry):
            hs[row, 7:8, :] = hs[row, 55:56, :]
            hs[row, 56:58, :] = hs[row, 8:10, :]
            for side in range(3):
                shifted[side, row] = hs[row, 7 + side : 55 + side, :].astype(BF)
            return carry

        lax.fori_loop(0, n_rows, one, 0)

    def own_patches(frame, by):
        for k in range(9):
            up, side = k // 3, k % 3
            patch_ref[frame, :, quarter(k)] = shifted[side, by + up : by + up + R, 0:32, :].reshape(R * L, C)

    def merge(row, carry):
        cell = lax.broadcasted_iota(jnp.int32, (16, C), 0)
        at = pl.multiple_of(row * W, 16)
        for part in range(4):
            main = main_ref[pl.ds(pl.multiple_of(row * L, 16), L), quarter(part)]
            side = edge_gates[pl.ds(pl.multiple_of(row * 16, 16), 16), quarter(part)]

            def put(value, slot, source):
                return jnp.where(cell == slot, jnp.broadcast_to(side[source : source + 1], (16, C)), value)

            low = put(main[0:16], 0, 15)
            high = put(main[16:32], 15, 0)
            out = jnp.zeros((16, C), F32)
            for slot, source in ((0, 1), (1, 2), (14, 13), (15, 14)):
                out = put(out, slot, source)
            for i, value in enumerate((low, high, out)):
                cells = pl.ds(at + 16 * i, 16)
                gates[cells, quarter(part)] = gates[cells, quarter(part)] + value
        return carry

    for frame in range(3):
        by = 2 - frame
        n = R + 2 * by
        cells = n * W if by else R * L
        valid = frame < count
        wcols = W if by else L
        shift(n + 2)
        own_patches(frame, by)
        if frame == 0:
            load_gates("x0", by)
            for row in range(n + 2):
                for side in range(3):
                    near = hs[row, 38 + side : 46 + side, :]
                    far = hs[row, 48 + side : 56 + side, :]
                    edge[side, row] = jnp.concatenate([near, far], axis=0).astype(BF)
            for k in range(9):
                up, side = k // 3, k % 3
                wide[0 : n * 16, quarter(k)] = edge[side, up : up + n].reshape(n * 16, C)

            def one(at_n, carry):
                at = pl.ds(pl.multiple_of(at_n * 2 * C, C), 2 * C)
                edge_gates[:, at] = jnp.dot(wide[0 : 12 * 16, :], w_ref[:, at], preferred_element_type=F32)
                return carry

        elif by:
            load_gates("x1", by)
            for k in range(9):
                up, side = k // 3, k % 3
                wide[0:cells, quarter(k)] = shifted[side, up : up + n].reshape(cells, C)

            def one(at_n, carry, cells=cells):
                at = pl.ds(pl.multiple_of(at_n * 2 * C, C), 2 * C)
                gates[0:cells, at] = gates[0:cells, at] + jnp.dot(
                    wide[0:cells, :], w_ref[:, at], preferred_element_type=F32
                )
                return carry
        else:

            def one(at_n, carry):
                at = pl.ds(pl.multiple_of(at_n * 2 * C, C), 2 * C)
                gates[0 : R * L, at] = x_ref[0, 2, :, :, at].reshape(R * L, 2 * C).astype(F32) + jnp.dot(
                    patch_ref[2], w_ref[:, at], preferred_element_type=F32
                )
                return carry

        lax.fori_loop(0, 2, one, 0)
        if frame == 0:
            lax.fori_loop(0, n, merge, 0)

        def gating(row, carry, frame=frame, by=by, wcols=wcols, valid=valid):
            start = pl.multiple_of(row * wcols, 16)
            g = gates[pl.ds(start, wcols), :]
            si = sigmoid(g[:, 0:C])
            sf = sigmoid(g[:, C : 2 * C])
            tg = jnp.tanh(g[:, 2 * C : 3 * C])
            so = sigmoid(g[:, 3 * C :])
            cell = cs[row + (0 if frame == 0 else frame), 0:wcols, :]
            cell_new = sf * cell + si * tg
            tc = jnp.tanh(cell_new)
            h_new = (so * tc).astype(BF).astype(F32)
            factors = (
                so * (1.0 - tc * tc),
                tg * si * (1.0 - si),
                cell * sf * (1.0 - sf),
                si * (1.0 - tg * tg),
                tc * so * (1.0 - so),
                sf,
            )
            h_old = hs[row + 1, 8 : 8 + wcols, :]
            keep = jnp.broadcast_to(valid, h_new.shape)
            h_next = jnp.where(keep, h_new, h_old)
            cs[row + frame, 0:wcols, :] = jnp.where(keep, cell_new, cell)
            if by:
                hs[row, 8:56, :] = jnp.where(inside(by, row), h_next, 0.0)
            if frame == 0:

                @pl.when((row >= 2) & (row < 2 + R))
                def _():
                    seq_ref[0, 0, row - 2] = h_next[0:L].astype(BF)
                    for i, factor in enumerate(factors):
                        m0_ref[i, row - 2] = factor[0:L].astype(BF)
            elif frame == 1:
                for i, factor in enumerate(factors):
                    m1_ref[i, row] = factor.astype(BF)

                @pl.when((row >= 1) & (row < 1 + R))
                def _():
                    seq_ref[0, 1, row - 1] = h_next[0:L].astype(BF)
            else:
                seq_ref[0, 2, row] = h_next.astype(BF)
                a, bi, bfg, bg, bo, _ = factors
                grad_h = t_ref[0, 2, row].astype(F32)
                dc_new = grad_h * a
                for part, value in enumerate((dc_new * bi, dc_new * bfg, dc_new * bg, grad_h * bo)):
                    g2_ref[row, :, quarter(part)] = jnp.where(keep, value, 0.0).astype(BF)
                q_ref[row] = jnp.where(keep, dc_new * sf, grad_h)
            return carry

        lax.fori_loop(0, n, gating, 0)
    for row in range(R + 2):
        t1_ref[row, 0:32, :] = main("t1", row, 0).astype(BF)
        after, before = sides("t1", row, 0)
        cell = lax.broadcasted_iota(jnp.int32, (16, C), 0)
        pad = jnp.where(cell == 0, jnp.broadcast_to(after, (16, C)), jnp.where(cell == 15, jnp.broadcast_to(before, (16, C)), 0.0))
        t1_ref[row, 32:48, :] = pad.astype(BF)
    rows_b, _ = row_offsets(ROWS_B)
    for name, width, parts in ROWS_B:
        first = jnp.where(row_odd == 1, 0, R - width)
        last = jnp.where(row_odd == 1, R - width, 0)
        for row in range(width):
            for part in range(parts):
                unit = rows_b[name, row, part]
                for start, out in ((first, near_out), (last, far_out)):
                    if name == "q":
                        out[unit] = q_ref[start + row].astype(BF)
                    else:
                        out[unit] = g2_ref[start + row, :, quarter(part)]


def backward_kernel(count_ref, t0_ref, w_ref, m1_ref, m0_ref, t1_ref, g2_ref, q_ref, near_r, far_r, near_c, far_c,
                    g1_ref, g0_ref, dh_ref, dc_ref, near_out, far_out, mine_ref, theirs_ref, above, below, left, right, gw, qs, z, turned):
    row_odd, col_odd = parities()
    count = count_ref[0]
    arranged(row_odd, near_r, far_r, above, below)

    unpack_columns(col_odd, near_c, far_c, left, right)

    rows, _ = row_offsets(ROWS_B)
    cols, _ = col_offsets(ROWS_B)
    valid2, valid1 = 2 < count, 1 < count
    widened_grads(ROWS_B, 2, g2_ref, above, below, left, right, gw)
    for row in range(R + 2):
        if row < 1:
            mid = above[rows["q", 0, 0]].astype(F32)
        elif row >= R + 1:
            mid = below[rows["q", 0, 0]].astype(F32)
        else:
            mid = q_ref[row - 1]
        qs[row, 0:32, :] = mid
        qs[row, 32:48, :] = border(cols["q", row, 0], 1, left, right)

    back(R + 2, gw, w_ref, z)

    def first(row, carry):
        keep2 = jnp.broadcast_to(valid2, (W, C))
        keep1 = jnp.broadcast_to(valid1, (W, C))
        q = qs[row]
        grad_h = jnp.where(keep2, summed(z, row, W), q) + t1_ref[row].astype(F32)
        grad_c = jnp.where(keep2, q, 0.0)
        a, bi, bfg, bg, bo, sf = (m1_ref[i, row].astype(F32) for i in range(6))
        dc_new = grad_c + grad_h * a
        keep = keep1 & inside(1, row)
        at = pl.ds(pl.multiple_of(row * W, W), W)
        for part, value in enumerate((dc_new * bi, dc_new * bfg, dc_new * bg, grad_h * bo)):
            gw[at, quarter(part)] = jnp.where(keep, value, 0.0).astype(BF)

        @pl.when((row >= 1) & (row < 1 + R))
        def _():
            dc_ref[0, row - 1] = jnp.where(keep1, dc_new * sf, grad_c)[0:L]
            dh_ref[0, row - 1] = grad_h[0:L]
            for part in range(4):
                g1_ref[row - 1, :, quarter(part)] = gw[pl.ds(pl.multiple_of(row * W, W), L), quarter(part)]

        return carry

    lax.fori_loop(0, R + 2, first, 0)
    back(R, gw, w_ref, z)

    def second(row, carry):
        keep1 = jnp.broadcast_to(valid1, (L, C))
        grad_h = jnp.where(keep1, summed(z, row, L), dh_ref[0, row]) + t0_ref[0, 0, row].astype(F32)
        a, bi, bfg, bg, bo, sf = (m0_ref[i, row].astype(F32) for i in range(6))
        dc_new = dc_ref[0, row] + grad_h * a
        for part, value in enumerate((dc_new * bi, dc_new * bfg, dc_new * bg, grad_h * bo)):
            g0_ref[row, :, quarter(part)] = value.astype(BF)
        dc_ref[0, row] = dc_new * sf
        return carry

    lax.fori_loop(0, R, second, 0)
    first_row = jnp.where(row_odd == 1, 0, R - 1)
    last_row = jnp.where(row_odd == 1, R - 1, 0)
    for part in range(4):
        near_out[part] = g0_ref[first_row, :, quarter(part)]
        far_out[part] = g0_ref[last_row, :, quarter(part)]
    turn((g0_ref, g1_ref, g2_ref), turned, mine_ref, theirs_ref)


def whole(shape):
    return pl.BlockSpec(shape, lambda _: (0,) * len(shape))


def call(kernel, inputs, outs, scratch, blocks=None, scalar=False, name=None, flops=0, limit=16, outside=()):
    blocks = blocks or {}
    specs = [whole(blocks.get(i, value.shape)) for i, value in enumerate(inputs)]
    inputs = list(inputs)
    for i in outside:
        specs[i] = pl.BlockSpec(memory_space=pltpu.HBM)
        inputs[i] = pltpu.with_memory_space_constraint(inputs[i], pltpu.HBM)
    if scalar:
        specs[0] = pl.BlockSpec(memory_space=pltpu.SMEM)
    size = sum(value.size * value.dtype.itemsize for value in inputs)
    return pl.pallas_call(
        kernel,
        grid=(1,),
        in_specs=specs,
        out_specs=[whole(out.shape) for out in outs],
        out_shape=outs,
        scratch_shapes=scratch,
        name=name,
        compiler_params=pltpu.CompilerParams(vmem_limit_bytes=limit << 20),
        cost_estimate=pl.CostEstimate(flops=flops, bytes_accessed=size, transcendentals=0),
    )(*inputs)


def swap_rows(near, far):
    axis = ("x", "core")
    return lax.ppermute(near, axis, ring_pairs(8, 0)), lax.ppermute(far, axis, ring_pairs(8, 1))


def swap_cols(near, far):
    return lax.ppermute(near, "sx", ring_pairs(4, 0)), lax.ppermute(far, "sx", ring_pairs(4, 1))


def first_partner(value, axis):
    flips = (1, 3)
    pairs = [(i * 2 + c, (i ^ flips[c]) * 2 + c) for i in range(4) for c in range(2)]
    return lax.ppermute(value, (axis, "core"), pairs)


def owner_groups():
    sets = (((0, 3), (1, 2)), ((0, 1), (2, 3)))
    return [
        [((d * 4 + x) * 2 + core) * 4 + y for d in ds for x in xs for y in range(4)]
        for core in range(2)
        for ds in sets[core]
        for xs in sets[core]
    ]


def body(input_gates, recur_weight, hidden_init, cell_init, hidden_cot, frame_count):
    width = C
    out = jax.ShapeDtypeStruct
    vmem = pltpu.VMEM
    _, row_units = row_offsets(ROWS_A)
    _, col_units = col_offsets(ROWS_A)
    first_two = {2: (1, 2, R, L, 4 * C)}
    border = out((row_units, L, C), BF)
    near, far = call(
        rows_a_kernel,
        (hidden_init, cell_init, input_gates, hidden_cot),
        [border] * 2,
        [vmem((2, 2, L, C), F32), pltpu.SemaphoreType.DMA((30,))],
        name="rows_a",
        outside=(0, 1, 2, 3),
    )
    near_r, far_r = swap_rows(near, far)
    weight_in, _ = lax.optimization_barrier((recur_weight, near))
    (recur_weight,) = call(
        load_kernel,
        (weight_in,),
        [out((9 * C, 4 * C), BF)],
        [pltpu.SemaphoreType.DMA((9,))],
        name="load",
        outside=(0,),
    )
    (own_gates,) = call(
        ahead_kernel,
        (hidden_init, recur_weight, near_r, far_r),
        [out(((R + 4) * L, 4 * C), F32)],
        [vmem((row_units, L, C), BF)] * 2
        + [vmem((R + 6, 64, C), F32), vmem((3, R + 6, L, C), BF), vmem(((R + 4) * L, 9 * C), BF)],
        name="ahead",
        flops=2 * 10**9,
    )
    strip = out((col_units, C), BF)
    near, far = call(
        cols_a_kernel,
        (hidden_init, cell_init, input_gates, hidden_cot, near_r, far_r),
        [strip] * 2,
        [vmem((row_units, L, C), BF)] * 2 + [vmem((col_units, C), F32)] * 2,
        first_two,
        name="cols_a",
    )
    near_c, far_c = swap_cols(near, far)
    _, row_units_b = row_offsets(ROWS_B)
    _, col_units_b = col_offsets(ROWS_B)
    hidden_seq, patches, m1, m0, t1, g2, q, near, far = call(
        forward_kernel,
        (frame_count, hidden_init, cell_init, input_gates, hidden_cot, recur_weight, own_gates, near_r, far_r, near_c, far_c),
        [
            out((1, 3, R, L, C), BF),
            out((3, R * L, 9 * C), BF),
            out((6, R + 2, W, C), BF),
            out((6, R, L, C), BF),
            out((R + 2, W, C), BF),
            out((R, L, 4 * C), BF),
            out((R, L, C), F32),
            out((row_units_b, L, C), BF),
            out((row_units_b, L, C), BF),
        ],
        [vmem((row_units, L, C), BF)] * 2
        + [vmem((col_units, C), F32)] * 2
        + [
            vmem((R + 6, 64, C), F32),
            vmem((R + 4, W, C), F32),
            vmem(((R + 4) * W, 4 * C), F32),
            vmem((3, R + 6, W, C), BF),
            vmem(((R + 4) * W, 9 * C), BF),
            vmem((3, R + 6, 16, C), BF),
            vmem(((R + 4) * 16, 4 * C), F32),
        ],
        scalar=True,
        name="forward",
        limit=30,
        flops=6 * 10**9,
    )
    near_r, far_r = swap_rows(near, far)
    flat_patches = patches.reshape(3 * R * L, 9 * C)
    other_patches = lax.ppermute(flat_patches, "core", CORES)
    strip = out((col_units_b, C), BF)
    near, far = call(
        cols_b_kernel,
        (g2, q, near_r, far_r),
        [strip] * 2,
        [vmem((row_units_b, L, C), BF)] * 2 + [vmem((col_units_b, C), F32)] * 2,
        name="cols_b",
    )
    near_c, far_c = swap_cols(near, far)
    g1, g0, _, cell_grad, near_c_rows, far_c_rows, mine, theirs = call(
        backward_kernel,
        (frame_count, hidden_cot, recur_weight, m1, m0, t1, g2, q, near_r, far_r, near_c, far_c),
        [out((R, L, 4 * C), BF), out((R, L, 4 * C), BF), out((1, R, L, C), F32), out((1, R, L, C), F32),
         out((4, L, C), BF), out((4, L, C), BF), out((512, 3 * C), BF), out((512, 3 * C), BF)],
        [vmem((row_units_b, L, C), BF)] * 2
        + [vmem((col_units_b, C), F32)] * 2
        + [vmem(((R + 4) * W, 4 * C), BF), vmem((R + 2, W, C), F32), vmem((3, R + 2, 64, C), F32), vmem((4 * C, 3 * C), BF)],
        {1: (1, 1, R, L, C)},
        scalar=True,
        name="backward",
        limit=24,
        flops=4 * 10**9,
    )
    _, col_units_c = col_offsets(ROWS_C)
    near_r, far_r = swap_rows(near_c_rows, far_c_rows)
    got = lax.ppermute(theirs, "core", CORES)
    (own_sum,) = call(own_sum_kernel, (mine, flat_patches), [out((512, 9 * C), F32)], [], name="own_sum", flops=2 * 10**9)
    got, near_r, far_r = lax.optimization_barrier((got, near_r, far_r))
    sent = call(
        chip_sum_kernel,
        (got, other_patches, own_sum),
        [out((256, HALF), BF)] * 4,
        [],
        name="chip_sum",
        flops=2 * 10**9,
    )
    strip = out((col_units_c, C), BF)
    near, far = call(
        cols_c_kernel,
        (g0, near_r, far_r),
        [strip] * 2,
        [vmem((4, L, C), BF)] * 2 + [vmem((col_units_c, C), F32)] * 2,
        name="cols_c",
    )
    near_c, far_c = swap_cols(near, far)
    came = first_partner(sent[1], "dp"), first_partner(sent[3], "x")
    *came, near_c, far_c = lax.optimization_barrier((*came, near_c, far_c))
    sent = call(halve_kernel, (sent[0], came[0], sent[2], came[1]), [out((128, HALF), BF)] * 4, [], name="halve")
    came = first_partner(sent[1], "x"), first_partner(sent[3], "dp")
    (hidden_grad,) = call(
        last_kernel,
        (g0, recur_weight, near_r, far_r, near_c, far_c),
        [out((1, R, L, C), BF)],
        [vmem((4, L, C), BF)] * 2
        + [vmem((col_units_c, C), F32)] * 2
        + [vmem(((R + 2) * W, 4 * C), BF), vmem((3, R, 64, C), F32)],
        name="last",
        flops=2 * 10**9,
    )
    *came, hidden_grad = lax.optimization_barrier((*came, hidden_grad))
    (blocks,) = call(
        quarter_kernel, (sent[0], came[0], sent[2], came[1]), [out((128, 9 * C), BF)], [], name="quarter"
    )
    parts = lax.all_to_all(blocks, AXES, 0, 0, tiled=True, axis_index_groups=owner_groups())
    (total,) = call(total_kernel, (parts.reshape(16, 8, 9 * C),), [out((8, 9 * C), F32)], [], name="total")
    weight_grad = total.T
    gate_grad = jnp.stack([g0, g1, g2])[None]
    return (hidden_seq, weight_grad, gate_grad, hidden_grad, cell_grad)


def solution(mesh):
    split = Mesh(mesh.devices.reshape(4, 4, 2, 4), ("dp", "x", "core", "sx"))
    sy = ("x", "core")
    step = jax.shard_map(
        body,
        mesh=split,
        in_specs=(
            P("dp", None, sy, "sx", None),
            P(),
            P("dp", sy, "sx", None),
            P("dp", sy, "sx", None),
            P("dp", None, sy, "sx", None),
            P("dp"),
        ),
        out_specs=(
            P("dp", None, sy, "sx", None),
            P(None, ("dp", "x", "core", "sx")),
            P("dp", None, sy, "sx", None),
            P("dp", sy, "sx", None),
            P("dp", sy, "sx", None),
        ),
        check_vma=False,
    )
    return step
```

```python
import functools

import jax
import jax.numpy as jnp
from jax import lax
from jax.experimental import pallas as pl
from jax.experimental.pallas import tpu as pltpu
from jax.sharding import Mesh, PartitionSpec as P


def ring_pairs(size, phase):
    pairs = [(i, (i + 1) % size) for i in range(phase, size, 2)]
    return [edge for a, b in pairs for edge in ((a, b), (b, a))]


CORES = [(0, 1), (1, 0)]
AXES = ("dp", "x", "core", "sx")
HALF = 1152
BF = jnp.bfloat16
F32 = jnp.float32
R, L, C = 8, 32, 256
W = 48
ROWS_A = (("h", 3, 1), ("c", 2, 1), ("x0", 2, 4), ("x1", 1, 4), ("t1", 1, 1))
ROWS_B = (("g", 2, 4), ("q", 1, 1))
ROWS_C = (("g", 1, 4),)


def row_offsets(spec):
    table, at = {}, 0
    for name, width, parts in spec:
        for row in range(width):
            for part in range(parts):
                table[name, row, part] = at
                at += 1
    return table, at


def col_offsets(spec):
    table, at = {}, 0
    for name, width, parts in spec:
        for part in range(parts):
            for row in range(R + 2 * width):
                table[name, row, part] = at
                at += width
    return table, -(-at // 16) * 16


def quarter(part):
    return slice(part * C, (part + 1) * C)


def parities():
    return lax.axis_index("core"), lax.axis_index("sx") % 2


def arranged(odd, near, far, before, after):
    @pl.when(odd == 1)
    def _():
        before[...] = near[...]
        after[...] = far[...]

    @pl.when(odd == 0)
    def _():
        before[...] = far[...]
        after[...] = near[...]


def pack_columns(spec, own, above, below, odd, near, far, left, right):
    rows, _ = row_offsets(spec)
    cols, _ = col_offsets(spec)
    for name, width, parts in spec:
        for row in range(R + 2 * width):
            for part in range(parts):
                at = cols[name, row, part]
                if row < width:
                    unit = rows[name, row, part]
                    first, last = above[unit, 0:8, :], above[unit, 24:32, :]
                elif row >= R + width:
                    unit = rows[name, row - R - width, part]
                    first, last = below[unit, 0:8, :], below[unit, 24:32, :]
                else:
                    first, last = own(name, row - width, slice(0, 8), part), own(name, row - width, slice(24, 32), part)
                left[at : at + width, :] = first.astype(F32)[0:width]
                right[at : at + width, :] = last.astype(F32)[8 - width : 8]

    @pl.when(odd == 1)
    def _():
        near[...] = left[...].astype(BF)
        far[...] = right[...].astype(BF)

    @pl.when(odd == 0)
    def _():
        near[...] = right[...].astype(BF)
        far[...] = left[...].astype(BF)


def rows_a_kernel(h_ref, c_ref, x_ref, t_ref, near, far, cells, sems):
    odd, _ = parities()
    rows, _ = row_offsets(ROWS_A)
    copies = []

    def start(source, target):
        copy = pltpu.make_async_copy(source, target, sems.at[len(copies)])
        copy.start()
        copies.append(copy)

    for side, out in enumerate((near, far)):
        top = odd == 1 if side == 0 else odd == 0
        for name, width, parts in ROWS_A:
            first = jnp.where(top, 0, R - width)
            at = pl.ds(first, width)
            unit = rows[name, 0, 0]
            if name == "h":
                start(h_ref.at[0, at], out.at[unit : unit + width])
            elif name == "c":
                start(c_ref.at[0, at], cells.at[side])
            elif name == "t1":
                start(t_ref.at[0, 1, at], out.at[unit : unit + width])
            else:
                for row in range(width):
                    for part in range(parts):
                        start(x_ref.at[0, int(name[1]), first + row, :, quarter(part)], out.at[rows[name, row, part]])
    for copy in copies:
        copy.wait()
    for side, out in enumerate((near, far)):
        for row in range(2):
            out[rows["c", row, 0]] = cells[side, row].astype(BF)


def cols_a_kernel(h_ref, c_ref, x_ref, t_ref, near_r, far_r, near, far, above, below, left, right):
    row_odd, col_odd = parities()
    arranged(row_odd, near_r, far_r, above, below)

    def own(name, row, cells, part):
        if name == "h":
            return h_ref[0, row, cells]
        if name == "c":
            return c_ref[0, row, cells]
        if name == "t1":
            return t_ref[0, 1, row, cells]
        return x_ref[0, int(name[1]), row, cells, quarter(part)]

    pack_columns(ROWS_A, own, above, below, col_odd, near, far, left, right)


def cols_b_kernel(g_ref, q_ref, near_r, far_r, near, far, above, below, left, right):
    row_odd, col_odd = parities()
    arranged(row_odd, near_r, far_r, above, below)

    def own(name, row, cells, part):
        if name == "q":
            return q_ref[row, cells]
        return g_ref[row, cells, quarter(part)]

    pack_columns(ROWS_B, own, above, below, col_odd, near, far, left, right)


def cols_c_kernel(g_ref, near_r, far_r, near, far, above, below, left, right):
    row_odd, col_odd = parities()
    arranged(row_odd, near_r, far_r, above, below)

    def own(name, row, cells, part):
        return g_ref[row, cells, quarter(part)]

    pack_columns(ROWS_C, own, above, below, col_odd, near, far, left, right)


def unpack_columns(odd, near, far, left, right):
    @pl.when(odd == 1)
    def _():
        left[...] = near[...].astype(F32)
        right[...] = far[...].astype(F32)

    @pl.when(odd == 0)
    def _():
        left[...] = far[...].astype(F32)
        right[...] = near[...].astype(F32)


def border(at, width, left, right):
    cell = lax.broadcasted_iota(jnp.int32, (16, C), 0)
    out = jnp.zeros((16, C), F32)
    for i in range(width):
        out = jnp.where(cell == i, jnp.broadcast_to(right[at + i : at + i + 1, :], (16, C)), out)
        out = jnp.where(cell == 16 - width + i, jnp.broadcast_to(left[at + i : at + i + 1, :], (16, C)), out)
    return out


def widened_grads(spec, width, g_ref, above, below, left, right, gw):
    rows, _ = row_offsets(spec)
    cols, _ = col_offsets(spec)
    for row in range(R + 2 * width):
        fits = inside(width, row)
        for part in range(4):
            if row < width:
                mid = above[rows["g", row, part]]
            elif row >= R + width:
                mid = below[rows["g", row - R - width, part]]
            else:
                mid = g_ref[row - width, :, quarter(part)]
            full = jnp.concatenate([mid.astype(F32), border(cols["g", row, part], width, left, right)], axis=0)
            gw[row * W : (row + 1) * W, quarter(part)] = jnp.where(fits, full, 0.0).astype(BF)


def wrapped(n, z):
    def wrap(row, carry):
        z[0, row, 56:57, :] = z[0, row, 8:9, :]
        z[2, row, 7:8, :] = z[2, row, 55:56, :]
        return carry

    lax.fori_loop(0, n, wrap, 0)


def back(n, gw, w_ref, z):
    for side in range(3):
        z[side, 0:n, 8:56, :] = products(gw, w_ref, side, n, W).reshape(n, W, C)
    wrapped(n, z)


def summed(z, row, cells):
    return z[0, row, 9 : 9 + cells, :] + z[1, row, 8 : 8 + cells, :] + z[2, row, 7 : 7 + cells, :]


def last_kernel(g_ref, w_ref, near_r, far_r, near_c, far_c, dh_ref, above, below, left, right, gw, z):
    row_odd, col_odd = parities()
    arranged(row_odd, near_r, far_r, above, below)
    unpack_columns(col_odd, near_c, far_c, left, right)
    widened_grads(ROWS_C, 1, g_ref, above, below, left, right, gw)
    back(R, gw, w_ref, z)

    def one(row, carry):
        dh_ref[0, row] = summed(z, row, L).astype(BF)
        return carry

    lax.fori_loop(0, R, one, 0)


def set_member(core, place, half, j):
    near = jnp.where((place == 1) | (place == 2), 1, 0)
    kind = jnp.where(core == 0, near, place // 2)
    kind = jnp.where(half == 1, 1 - kind, kind)
    return jnp.where(core == 0, kind + j * (3 - 2 * kind), 2 * kind + j)


def turn(grads, turned, mine_ref, theirs_ref):
    core = lax.axis_index("core")
    for frame, g_ref in enumerate(grads):
        flat = g_ref[...].reshape(R * L, 4 * C).astype(F32)
        turned[:, quarter(frame)] = jnp.transpose(flat).astype(BF)

    place = {axis: lax.axis_index(axis) for axis in ("dp", "x")}

    def pick(block, carry):
        at = pl.ds(pl.multiple_of(block * 32, 32), 32)
        outer, inner = block // 4, block % 4
        for who, out in ((core, mine_ref), (1 - core, theirs_ref)):
            d = set_member(who, place["dp"], outer // 2, outer % 2)
            x = set_member(who, place["x"], inner // 2, inner % 2)
            out[at, :] = turned[pl.ds(pl.multiple_of(((d * 4 + x) * 2 + who) * 32, 32), 32), :]
        return carry

    lax.fori_loop(0, 16, pick, 0)


def own_sum_kernel(mine_ref, p_ref, out_ref):
    def one(n, carry):
        at = pl.ds(pl.multiple_of(n * 3 * C, C), 3 * C)
        out_ref[:, at] = jnp.dot(mine_ref[...], p_ref[:, at], preferred_element_type=F32)
        return carry

    lax.fori_loop(0, 3, one, 0)


def parted(rows, total, keep, send):
    for block in range(keep.shape[0] // rows):
        src = block * 2 * rows
        keep[block * rows : (block + 1) * rows, :] = total[src : src + rows].astype(BF)
        send[block * rows : (block + 1) * rows, :] = total[src + rows : src + 2 * rows].astype(BF)


def chip_sum_kernel(got_ref, p_ref, own_ref, keep0, send0, keep1, send1):
    for color, (rows, keep, send) in enumerate(((256, keep0, send0), (64, keep1, send1))):
        at = slice(color * HALF, (color + 1) * HALF)
        total = own_ref[:, at] + jnp.dot(got_ref[...], p_ref[:, at], preferred_element_type=F32)
        parted(rows, total, keep, send)


def halve_kernel(kept0, came0, kept1, came1, keep0, send0, keep1, send1):
    parted(64, kept0[...].astype(F32) + came0[...].astype(F32), keep0, send0)
    parted(128, kept1[...].astype(F32) + came1[...].astype(F32), keep1, send1)


def quarter_kernel(kept0, came0, kept1, came1, out_ref):
    out_ref[:, 0:HALF] = (kept0[...].astype(F32) + came0[...].astype(F32)).astype(BF)
    out_ref[:, HALF:] = (kept1[...].astype(F32) + came1[...].astype(F32)).astype(BF)


def total_kernel(parts_ref, out_ref):
    def one(i, carry):
        out_ref[...] = out_ref[...] + parts_ref[i].astype(F32)
        return carry

    out_ref[...] = jnp.zeros_like(out_ref)
    lax.fori_loop(0, 16, one, 0)


def inside(by, row):
    at_row = (lax.axis_index("x") * 2 + lax.axis_index("core")) * R + row - by
    cell = lax.broadcasted_iota(jnp.int32, (W, C), 0)
    column = jnp.where(cell < 40, cell, cell - W) + lax.axis_index("sx") * L
    fits = (column >= 0) & (column < 4 * L)
    return fits & jnp.broadcast_to((at_row >= 0) & (at_row < 8 * R), (W, C))


def sigmoid(value):
    return 0.5 * jnp.tanh(0.5 * value) + 0.5


def load_kernel(w_hbm, w_ref, sems):
    copies = [
        pltpu.make_async_copy(w_hbm.at[quarter(i)], w_ref.at[quarter(i)], sems.at[i]) for i in range(9)
    ]
    for copy in copies:
        copy.start()
    for copy in copies:
        copy.wait()


def ahead_kernel(h_ref, w_ref, near_r, far_r, out_ref, above, below, hs, shifted, wide):
    row_odd, _ = parities()
    arranged(row_odd, near_r, far_r, above, below)
    rows, _ = row_offsets(ROWS_A)
    n = R + 4
    hs[...] = jnp.zeros_like(hs)
    for row in range(R + 6):
        if row < 3:
            mid = above[rows["h", row, 0]]
        elif row >= R + 3:
            mid = below[rows["h", row - R - 3, 0]]
        else:
            mid = h_ref[0, row - 3]
        hs[row, 8:40, :] = jnp.where(inside(3, row)[0:L], mid.astype(F32), 0.0)
        for side in range(3):
            shifted[side, row] = hs[row, 7 + side : 39 + side, :].astype(BF)
    for k in range(9):
        up, side = k // 3, k % 3
        wide[:, quarter(k)] = shifted[side, up : up + n].reshape(n * L, C)

    def one(at_n, carry):
        at = pl.ds(pl.multiple_of(at_n * 2 * C, C), 2 * C)
        out_ref[:, at] = jnp.dot(wide[...], w_ref[:, at], preferred_element_type=F32)
        return carry

    lax.fori_loop(0, 2, one, 0)


def forward_kernel(count_ref, h_ref, c_ref, x_ref, t_ref, w_ref, main_ref, near_r, far_r, near_c, far_c,
                   seq_ref, patch_ref, m1_ref, m0_ref, t1_ref, g2_ref, q_ref, near_out, far_out,
                   above, below, left, right, hs, cs, gates, shifted, wide, edge, edge_gates):
    row_odd, col_odd = parities()
    count = count_ref[0]
    arranged(row_odd, near_r, far_r, above, below)

    unpack_columns(col_odd, near_c, far_c, left, right)

    rows, _ = row_offsets(ROWS_A)
    cols, _ = col_offsets(ROWS_A)
    widths = {name: width for name, width, _ in ROWS_A}

    def main(name, row, part):
        width = widths[name]
        if row < width:
            return above[rows[name, row, part]].astype(F32)
        if row >= R + width:
            return below[rows[name, row - R - width, part]].astype(F32)
        row -= width
        if name == "h":
            return h_ref[0, row].astype(F32)
        if name == "c":
            return c_ref[0, row]
        if name == "t1":
            return t_ref[0, 1, row].astype(F32)
        return x_ref[0, int(name[1]), row, :, quarter(part)].astype(F32)

    def sides(name, row, part):
        width = widths[name]
        at = cols[name, row, part]
        return right[at : at + width, :], left[at : at + width, :]

    zero16 = jnp.zeros((16, C), F32)
    hs[...] = jnp.zeros_like(hs)
    for row in range(R + 6):
        hs[row, 8:40, :] = main("h", row, 0)
        after, before = sides("h", row, 0)
        hs[row, 40:43, :] = after
        hs[row, 53:56, :] = before
        hs[row, 8:56, :] = jnp.where(inside(3, row), hs[row, 8:56, :], 0.0)
    for row in range(R + 4):
        cs[row, 0:32, :] = main("c", row, 0)
        cs[row, 32:48, :] = zero16
        after, before = sides("c", row, 0)
        cs[row, 32:34, :] = after
        cs[row, 46:48, :] = before

    def load_gates(name, by):
        for row in range(R + 2 * by):
            for part in range(4):
                at = row * W
                gates[at : at + 32, quarter(part)] = main(name, row, part)
                gates[at + 32 : at + W, quarter(part)] = zero16
                after, before = sides(name, row, part)
                gates[at + 32 : at + 32 + by, quarter(part)] = after
                gates[at + W - by : at + W, quarter(part)] = before

    def shift(n_rows):
        def one(row, carry):
            hs[row, 7:8, :] = hs[row, 55:56, :]
            hs[row, 56:58, :] = hs[row, 8:10, :]
            for side in range(3):
                shifted[side, row] = hs[row, 7 + side : 55 + side, :].astype(BF)
            return carry

        lax.fori_loop(0, n_rows, one, 0)

    def own_patches(frame, by):
        for k in range(9):
            up, side = k // 3, k % 3
            patch_ref[frame, :, quarter(k)] = shifted[side, by + up : by + up + R, 0:32, :].reshape(R * L, C)

    def merge(row, carry):
        cell = lax.broadcasted_iota(jnp.int32, (16, C), 0)
        at = pl.multiple_of(row * W, 16)
        for part in range(4):
            main = main_ref[pl.ds(pl.multiple_of(row * L, 16), L), quarter(part)]
            side = edge_gates[pl.ds(pl.multiple_of(row * 16, 16), 16), quarter(part)]

            def put(value, slot, source):
                return jnp.where(cell == slot, jnp.broadcast_to(side[source : source + 1], (16, C)), value)

            low = put(main[0:16], 0, 15)
            high = put(main[16:32], 15, 0)
            out = jnp.zeros((16, C), F32)
            for slot, source in ((0, 1), (1, 2), (14, 13), (15, 14)):
                out = put(out, slot, source)
            for i, value in enumerate((low, high, out)):
                cells = pl.ds(at + 16 * i, 16)
                gates[cells, quarter(part)] = gates[cells, quarter(part)] + value
        return carry

    for frame in range(3):
        by = 2 - frame
        n = R + 2 * by
        cells = n * W if by else R * L
        valid = frame < count
        wcols = W if by else L
        shift(n + 2)
        own_patches(frame, by)
        if frame == 0:
            load_gates("x0", by)
            for row in range(n + 2):
                for side in range(3):
                    near = hs[row, 38 + side : 46 + side, :]
                    far = hs[row, 48 + side : 56 + side, :]
                    edge[side, row] = jnp.concatenate([near, far], axis=0).astype(BF)
            for k in range(9):
                up, side = k // 3, k % 3
                wide[0 : n * 16, quarter(k)] = edge[side, up : up + n].reshape(n * 16, C)

            def one(at_n, carry):
                at = pl.ds(pl.multiple_of(at_n * 2 * C, C), 2 * C)
                edge_gates[:, at] = jnp.dot(wide[0 : 12 * 16, :], w_ref[:, at], preferred_element_type=F32)
                return carry

        elif by:
            load_gates("x1", by)
            for k in range(9):
                up, side = k // 3, k % 3
                wide[0:cells, quarter(k)] = shifted[side, up : up + n].reshape(cells, C)

            def one(at_n, carry, cells=cells):
                at = pl.ds(pl.multiple_of(at_n * 2 * C, C), 2 * C)
                gates[0:cells, at] = gates[0:cells, at] + jnp.dot(
                    wide[0:cells, :], w_ref[:, at], preferred_element_type=F32
                )
                return carry
        else:

            def one(at_n, carry):
                at = pl.ds(pl.multiple_of(at_n * 2 * C, C), 2 * C)
                gates[0 : R * L, at] = x_ref[0, 2, :, :, at].reshape(R * L, 2 * C).astype(F32) + jnp.dot(
                    patch_ref[2], w_ref[:, at], preferred_element_type=F32
                )
                return carry

        lax.fori_loop(0, 2, one, 0)
        if frame == 0:
            lax.fori_loop(0, n, merge, 0)

        def gating(row, carry, frame=frame, by=by, wcols=wcols, valid=valid):
            start = pl.multiple_of(row * wcols, 16)
            g = gates[pl.ds(start, wcols), :]
            si = sigmoid(g[:, 0:C])
            sf = sigmoid(g[:, C : 2 * C])
            tg = jnp.tanh(g[:, 2 * C : 3 * C])
            so = sigmoid(g[:, 3 * C :])
            cell = cs[row + (0 if frame == 0 else frame), 0:wcols, :]
            cell_new = sf * cell + si * tg
            tc = jnp.tanh(cell_new)
            h_new = (so * tc).astype(BF).astype(F32)
            factors = (
                so * (1.0 - tc * tc),
                tg * si * (1.0 - si),
                cell * sf * (1.0 - sf),
                si * (1.0 - tg * tg),
                tc * so * (1.0 - so),
                sf,
            )
            h_old = hs[row + 1, 8 : 8 + wcols, :]
            keep = jnp.broadcast_to(valid, h_new.shape)
            h_next = jnp.where(keep, h_new, h_old)
            cs[row + frame, 0:wcols, :] = jnp.where(keep, cell_new, cell)
            if by:
                hs[row, 8:56, :] = jnp.where(inside(by, row), h_next, 0.0)
            if frame == 0:

                @pl.when((row >= 2) & (row < 2 + R))
                def _():
                    seq_ref[0, 0, row - 2] = h_next[0:L].astype(BF)
                    for i, factor in enumerate(factors):
                        m0_ref[i, row - 2] = factor[0:L].astype(BF)
            elif frame == 1:
                for i, factor in enumerate(factors):
                    m1_ref[i, row] = factor.astype(BF)

                @pl.when((row >= 1) & (row < 1 + R))
                def _():
                    seq_ref[0, 1, row - 1] = h_next[0:L].astype(BF)
            else:
                seq_ref[0, 2, row] = h_next.astype(BF)
                a, bi, bfg, bg, bo, _ = factors
                grad_h = t_ref[0, 2, row].astype(F32)
                dc_new = grad_h * a
                for part, value in enumerate((dc_new * bi, dc_new * bfg, dc_new * bg, grad_h * bo)):
                    g2_ref[row, :, quarter(part)] = jnp.where(keep, value, 0.0).astype(BF)
                q_ref[row] = jnp.where(keep, dc_new * sf, grad_h)
            return carry

        lax.fori_loop(0, n, gating, 0)
    for row in range(R + 2):
        t1_ref[row, 0:32, :] = main("t1", row, 0).astype(BF)
        after, before = sides("t1", row, 0)
        cell = lax.broadcasted_iota(jnp.int32, (16, C), 0)
        pad = jnp.where(cell == 0, jnp.broadcast_to(after, (16, C)), jnp.where(cell == 15, jnp.broadcast_to(before, (16, C)), 0.0))
        t1_ref[row, 32:48, :] = pad.astype(BF)
    rows_b, _ = row_offsets(ROWS_B)
    for name, width, parts in ROWS_B:
        first = jnp.where(row_odd == 1, 0, R - width)
        last = jnp.where(row_odd == 1, R - width, 0)
        for row in range(width):
            for part in range(parts):
                unit = rows_b[name, row, part]
                for start, out in ((first, near_out), (last, far_out)):
                    if name == "q":
                        out[unit] = q_ref[start + row].astype(BF)
                    else:
                        out[unit] = g2_ref[start + row, :, quarter(part)]


def ahead_back_kernel(g_ref, w_ref, near_r, far_r, z_ref, above, below, gm):
    row_odd, _ = parities()
    arranged(row_odd, near_r, far_r, above, below)
    rows, _ = row_offsets(ROWS_B)
    for row in range(R + 4):
        fits = inside(2, row)[0:L]
        for part in range(4):
            if row < 2:
                mid = above[rows["g", row, part]]
            elif row >= R + 2:
                mid = below[rows["g", row - R - 2, part]]
            else:
                mid = g_ref[row - 2, :, quarter(part)]
            gm[row * L : (row + 1) * L, quarter(part)] = jnp.where(fits, mid.astype(F32), 0.0).astype(BF)
    n = R + 2
    for side in range(3):
        z_ref[side] = products(gm, w_ref, side, n, L).reshape(n, L, C)


def products(grads, w_ref, side, n, cells):
    total = None
    for up in range(3):
        k = up * 3 + side
        term = lax.dot_general(
            grads[(2 - up) * cells : (2 - up + n) * cells, :],
            w_ref[k * C : (k + 1) * C, :],
            (((1,), (1,)), ((), ())),
            preferred_element_type=F32,
        )
        total = term if total is None else total + term
    return total


def backward_kernel(count_ref, t0_ref, w_ref, zmain_ref, m1_ref, m0_ref, t1_ref, g2_ref, q_ref, near_r, far_r, near_c, far_c,
                    g1_ref, g0_ref, dh_ref, dc_ref, near_out, far_out, mine_ref, theirs_ref, above, below, left, right, gw, qs, z, turned, gb):
    row_odd, col_odd = parities()
    count = count_ref[0]
    arranged(row_odd, near_r, far_r, above, below)

    unpack_columns(col_odd, near_c, far_c, left, right)

    rows, _ = row_offsets(ROWS_B)
    cols, _ = col_offsets(ROWS_B)
    valid2, valid1 = 2 < count, 1 < count
    for row in range(R + 4):
        fits = inside(2, row)[L:W]
        for part in range(4):
            value = border(cols["g", row, part], 2, left, right)
            gb[row * 16 : (row + 1) * 16, quarter(part)] = jnp.where(fits, value, 0.0).astype(BF)
    for row in range(R + 2):
        if row < 1:
            mid = above[rows["q", 0, 0]].astype(F32)
        elif row >= R + 1:
            mid = below[rows["q", 0, 0]].astype(F32)
        else:
            mid = q_ref[row - 1]
        qs[row, 0:32, :] = mid
        qs[row, 32:48, :] = border(cols["q", row, 0], 1, left, right)

    for side in range(3):
        z[side, 0 : R + 2, 8:40, :] = zmain_ref[side]
        z[side, 0 : R + 2, 40:56, :] = products(gb, w_ref, side, R + 2, 16).reshape(R + 2, 16, C)
    wrapped(R + 2, z)

    def first(row, carry):
        keep2 = jnp.broadcast_to(valid2, (W, C))
        keep1 = jnp.broadcast_to(valid1, (W, C))
        q = qs[row]
        grad_h = jnp.where(keep2, summed(z, row, W), q) + t1_ref[row].astype(F32)
        grad_c = jnp.where(keep2, q, 0.0)
        a, bi, bfg, bg, bo, sf = (m1_ref[i, row].astype(F32) for i in range(6))
        dc_new = grad_c + grad_h * a
        keep = keep1 & inside(1, row)
        at = pl.ds(pl.multiple_of(row * W, W), W)
        for part, value in enumerate((dc_new * bi, dc_new * bfg, dc_new * bg, grad_h * bo)):
            gw[at, quarter(part)] = jnp.where(keep, value, 0.0).astype(BF)

        @pl.when((row >= 1) & (row < 1 + R))
        def _():
            dc_ref[0, row - 1] = jnp.where(keep1, dc_new * sf, grad_c)[0:L]
            dh_ref[0, row - 1] = grad_h[0:L]
            for part in range(4):
                g1_ref[row - 1, :, quarter(part)] = gw[pl.ds(pl.multiple_of(row * W, W), L), quarter(part)]

        return carry

    lax.fori_loop(0, R + 2, first, 0)
    back(R, gw, w_ref, z)

    def second(row, carry):
        keep1 = jnp.broadcast_to(valid1, (L, C))
        grad_h = jnp.where(keep1, summed(z, row, L), dh_ref[0, row]) + t0_ref[0, 0, row].astype(F32)
        a, bi, bfg, bg, bo, sf = (m0_ref[i, row].astype(F32) for i in range(6))
        dc_new = dc_ref[0, row] + grad_h * a
        for part, value in enumerate((dc_new * bi, dc_new * bfg, dc_new * bg, grad_h * bo)):
            g0_ref[row, :, quarter(part)] = value.astype(BF)
        dc_ref[0, row] = dc_new * sf
        return carry

    lax.fori_loop(0, R, second, 0)
    first_row = jnp.where(row_odd == 1, 0, R - 1)
    last_row = jnp.where(row_odd == 1, R - 1, 0)
    for part in range(4):
        near_out[part] = g0_ref[first_row, :, quarter(part)]
        far_out[part] = g0_ref[last_row, :, quarter(part)]
    turn((g0_ref, g1_ref, g2_ref), turned, mine_ref, theirs_ref)


def whole(shape):
    return pl.BlockSpec(shape, lambda _: (0,) * len(shape))


def call(kernel, inputs, outs, scratch, blocks=None, scalar=False, name=None, flops=0, limit=16, outside=()):
    blocks = blocks or {}
    specs = [whole(blocks.get(i, value.shape)) for i, value in enumerate(inputs)]
    inputs = list(inputs)
    for i in outside:
        specs[i] = pl.BlockSpec(memory_space=pltpu.HBM)
        inputs[i] = pltpu.with_memory_space_constraint(inputs[i], pltpu.HBM)
    if scalar:
        specs[0] = pl.BlockSpec(memory_space=pltpu.SMEM)
    size = sum(value.size * value.dtype.itemsize for value in inputs)
    return pl.pallas_call(
        kernel,
        grid=(1,),
        in_specs=specs,
        out_specs=[whole(out.shape) for out in outs],
        out_shape=outs,
        scratch_shapes=scratch,
        name=name,
        compiler_params=pltpu.CompilerParams(vmem_limit_bytes=limit << 20),
        cost_estimate=pl.CostEstimate(flops=flops, bytes_accessed=size, transcendentals=0),
    )(*inputs)


def swap_rows(near, far):
    axis = ("x", "core")
    return lax.ppermute(near, axis, ring_pairs(8, 0)), lax.ppermute(far, axis, ring_pairs(8, 1))


def swap_cols(near, far):
    return lax.ppermute(near, "sx", ring_pairs(4, 0)), lax.ppermute(far, "sx", ring_pairs(4, 1))


def first_partner(value, axis):
    flips = (1, 3)
    pairs = [(i * 2 + c, (i ^ flips[c]) * 2 + c) for i in range(4) for c in range(2)]
    return lax.ppermute(value, (axis, "core"), pairs)


def owner_groups():
    sets = (((0, 3), (1, 2)), ((0, 1), (2, 3)))
    return [
        [((d * 4 + x) * 2 + core) * 4 + y for d in ds for x in xs for y in range(4)]
        for core in range(2)
        for ds in sets[core]
        for xs in sets[core]
    ]


def body(input_gates, recur_weight, hidden_init, cell_init, hidden_cot, frame_count):
    width = C
    out = jax.ShapeDtypeStruct
    vmem = pltpu.VMEM
    _, row_units = row_offsets(ROWS_A)
    _, col_units = col_offsets(ROWS_A)
    first_two = {2: (1, 2, R, L, 4 * C)}
    border = out((row_units, L, C), BF)
    near, far = call(
        rows_a_kernel,
        (hidden_init, cell_init, input_gates, hidden_cot),
        [border] * 2,
        [vmem((2, 2, L, C), F32), pltpu.SemaphoreType.DMA((30,))],
        name="rows_a",
        outside=(0, 1, 2, 3),
    )
    near_r, far_r = swap_rows(near, far)
    weight_in, _ = lax.optimization_barrier((recur_weight, near))
    (recur_weight,) = call(
        load_kernel,
        (weight_in,),
        [out((9 * C, 4 * C), BF)],
        [pltpu.SemaphoreType.DMA((9,))],
        name="load",
        outside=(0,),
    )
    (own_gates,) = call(
        ahead_kernel,
        (hidden_init, recur_weight, near_r, far_r),
        [out(((R + 4) * L, 4 * C), F32)],
        [vmem((row_units, L, C), BF)] * 2
        + [vmem((R + 6, 64, C), F32), vmem((3, R + 6, L, C), BF), vmem(((R + 4) * L, 9 * C), BF)],
        name="ahead",
        flops=2 * 10**9,
    )
    strip = out((col_units, C), BF)
    near, far = call(
        cols_a_kernel,
        (hidden_init, cell_init, input_gates, hidden_cot, near_r, far_r),
        [strip] * 2,
        [vmem((row_units, L, C), BF)] * 2 + [vmem((col_units, C), F32)] * 2,
        first_two,
        name="cols_a",
    )
    near_c, far_c = swap_cols(near, far)
    _, row_units_b = row_offsets(ROWS_B)
    _, col_units_b = col_offsets(ROWS_B)
    hidden_seq, patches, m1, m0, t1, g2, q, near, far = call(
        forward_kernel,
        (frame_count, hidden_init, cell_init, input_gates, hidden_cot, recur_weight, own_gates, near_r, far_r, near_c, far_c),
        [
            out((1, 3, R, L, C), BF),
            out((3, R * L, 9 * C), BF),
            out((6, R + 2, W, C), BF),
            out((6, R, L, C), BF),
            out((R + 2, W, C), BF),
            out((R, L, 4 * C), BF),
            out((R, L, C), F32),
            out((row_units_b, L, C), BF),
            out((row_units_b, L, C), BF),
        ],
        [vmem((row_units, L, C), BF)] * 2
        + [vmem((col_units, C), F32)] * 2
        + [
            vmem((R + 6, 64, C), F32),
            vmem((R + 4, W, C), F32),
            vmem(((R + 4) * W, 4 * C), F32),
            vmem((3, R + 6, W, C), BF),
            vmem(((R + 4) * W, 9 * C), BF),
            vmem((3, R + 6, 16, C), BF),
            vmem(((R + 4) * 16, 4 * C), F32),
        ],
        scalar=True,
        name="forward",
        limit=30,
        flops=6 * 10**9,
    )
    near_r, far_r = swap_rows(near, far)
    flat_patches = patches.reshape(3 * R * L, 9 * C)
    other_patches = lax.ppermute(flat_patches, "core", CORES)
    (zmain,) = call(
        ahead_back_kernel,
        (g2, recur_weight, near_r, far_r),
        [out((3, R + 2, L, C), F32)],
        [vmem((row_units_b, L, C), BF)] * 2 + [vmem(((R + 4) * L, 4 * C), BF)],
        name="ahead_back",
        flops=2 * 10**9,
    )
    strip = out((col_units_b, C), BF)
    near, far = call(
        cols_b_kernel,
        (g2, q, near_r, far_r),
        [strip] * 2,
        [vmem((row_units_b, L, C), BF)] * 2 + [vmem((col_units_b, C), F32)] * 2,
        name="cols_b",
    )
    near_c, far_c = swap_cols(near, far)
    g1, g0, _, cell_grad, near_c_rows, far_c_rows, mine, theirs = call(
        backward_kernel,
        (frame_count, hidden_cot, recur_weight, zmain, m1, m0, t1, g2, q, near_r, far_r, near_c, far_c),
        [out((R, L, 4 * C), BF), out((R, L, 4 * C), BF), out((1, R, L, C), F32), out((1, R, L, C), F32),
         out((4, L, C), BF), out((4, L, C), BF), out((512, 3 * C), BF), out((512, 3 * C), BF)],
        [vmem((row_units_b, L, C), BF)] * 2
        + [vmem((col_units_b, C), F32)] * 2
        + [vmem(((R + 4) * W, 4 * C), BF), vmem((R + 2, W, C), F32), vmem((3, R + 2, 64, C), F32), vmem((4 * C, 3 * C), BF), vmem(((R + 4) * 16, 4 * C), BF)],
        {1: (1, 1, R, L, C)},
        scalar=True,
        name="backward",
        limit=24,
        flops=4 * 10**9,
    )
    _, col_units_c = col_offsets(ROWS_C)
    near_r, far_r = swap_rows(near_c_rows, far_c_rows)
    got = lax.ppermute(theirs, "core", CORES)
    (own_sum,) = call(own_sum_kernel, (mine, flat_patches), [out((512, 9 * C), F32)], [], name="own_sum", flops=2 * 10**9)
    got, near_r, far_r = lax.optimization_barrier((got, near_r, far_r))
    sent = call(
        chip_sum_kernel,
        (got, other_patches, own_sum),
        [out((256, HALF), BF)] * 4,
        [],
        name="chip_sum",
        flops=2 * 10**9,
    )
    strip = out((col_units_c, C), BF)
    near, far = call(
        cols_c_kernel,
        (g0, near_r, far_r),
        [strip] * 2,
        [vmem((4, L, C), BF)] * 2 + [vmem((col_units_c, C), F32)] * 2,
        name="cols_c",
    )
    near_c, far_c = swap_cols(near, far)
    came = first_partner(sent[1], "dp"), first_partner(sent[3], "x")
    *came, near_c, far_c = lax.optimization_barrier((*came, near_c, far_c))
    sent = call(halve_kernel, (sent[0], came[0], sent[2], came[1]), [out((128, HALF), BF)] * 4, [], name="halve")
    came = first_partner(sent[1], "x"), first_partner(sent[3], "dp")
    (hidden_grad,) = call(
        last_kernel,
        (g0, recur_weight, near_r, far_r, near_c, far_c),
        [out((1, R, L, C), BF)],
        [vmem((4, L, C), BF)] * 2
        + [vmem((col_units_c, C), F32)] * 2
        + [vmem(((R + 2) * W, 4 * C), BF), vmem((3, R, 64, C), F32)],
        name="last",
        flops=2 * 10**9,
    )
    *came, hidden_grad = lax.optimization_barrier((*came, hidden_grad))
    (blocks,) = call(
        quarter_kernel, (sent[0], came[0], sent[2], came[1]), [out((128, 9 * C), BF)], [], name="quarter"
    )
    parts = lax.all_to_all(blocks, AXES, 0, 0, tiled=True, axis_index_groups=owner_groups())
    (total,) = call(total_kernel, (parts.reshape(16, 8, 9 * C),), [out((8, 9 * C), F32)], [], name="total")
    weight_grad = total.T
    gate_grad = jnp.stack([g0, g1, g2])[None]
    return (hidden_seq, weight_grad, gate_grad, hidden_grad, cell_grad)


def solution(mesh):
    split = Mesh(mesh.devices.reshape(4, 4, 2, 4), ("dp", "x", "core", "sx"))
    sy = ("x", "core")
    step = jax.shard_map(
        body,
        mesh=split,
        in_specs=(
            P("dp", None, sy, "sx", None),
            P(),
            P("dp", sy, "sx", None),
            P("dp", sy, "sx", None),
            P("dp", None, sy, "sx", None),
            P("dp"),
        ),
        out_specs=(
            P("dp", None, sy, "sx", None),
            P(None, ("dp", "x", "core", "sx")),
            P("dp", None, sy, "sx", None),
            P("dp", sy, "sx", None),
            P("dp", sy, "sx", None),
        ),
        check_vma=False,
    )
    return step
```

```python
import functools

import jax
import jax.numpy as jnp
from jax import lax
from jax.experimental import pallas as pl
from jax.experimental.pallas import tpu as pltpu
from jax.sharding import Mesh, PartitionSpec as P


def ring_pairs(size, phase):
    pairs = [(i, (i + 1) % size) for i in range(phase, size, 2)]
    return [edge for a, b in pairs for edge in ((a, b), (b, a))]


CORES = [(0, 1), (1, 0)]
AXES = ("dp", "x", "core", "sx")
HALF = 1152
BF = jnp.bfloat16
F32 = jnp.float32
R, L, C = 8, 32, 256
W = 48
ROWS_A = (("h", 3, 1), ("c", 2, 1), ("x0", 2, 4), ("x1", 1, 4), ("t1", 1, 1))
ROWS_B = (("g", 2, 4), ("q", 1, 1))
ROWS_C = (("g", 1, 4),)


def row_offsets(spec):
    table, at = {}, 0
    for name, width, parts in spec:
        for row in range(width):
            for part in range(parts):
                table[name, row, part] = at
                at += 1
    return table, at


def col_offsets(spec):
    table, at = {}, 0
    for name, width, parts in spec:
        for part in range(parts):
            for row in range(R + 2 * width):
                table[name, row, part] = at
                at += width
    return table, -(-at // 16) * 16


def quarter(part):
    return slice(part * C, (part + 1) * C)


def parities():
    return lax.axis_index("core"), lax.axis_index("sx") % 2


def arranged(odd, near, far, before, after):
    @pl.when(odd == 1)
    def _():
        before[...] = near[...]
        after[...] = far[...]

    @pl.when(odd == 0)
    def _():
        before[...] = far[...]
        after[...] = near[...]


def pack_columns(spec, own, above, below, odd, near, far, left, right):
    rows, _ = row_offsets(spec)
    cols, _ = col_offsets(spec)
    for name, width, parts in spec:
        for row in range(R + 2 * width):
            for part in range(parts):
                at = cols[name, row, part]
                if row < width:
                    unit = rows[name, row, part]
                    first, last = above[unit, 0:8, :], above[unit, 24:32, :]
                elif row >= R + width:
                    unit = rows[name, row - R - width, part]
                    first, last = below[unit, 0:8, :], below[unit, 24:32, :]
                else:
                    first, last = own(name, row - width, slice(0, 8), part), own(name, row - width, slice(24, 32), part)
                left[at : at + width, :] = first.astype(F32)[0:width]
                right[at : at + width, :] = last.astype(F32)[8 - width : 8]

    @pl.when(odd == 1)
    def _():
        near[...] = left[...].astype(BF)
        far[...] = right[...].astype(BF)

    @pl.when(odd == 0)
    def _():
        near[...] = right[...].astype(BF)
        far[...] = left[...].astype(BF)


def rows_a_kernel(h_ref, c_ref, x_ref, t_ref, near, far, cells, sems):
    odd, _ = parities()
    rows, _ = row_offsets(ROWS_A)
    copies = []

    def start(source, target):
        copy = pltpu.make_async_copy(source, target, sems.at[len(copies)])
        copy.start()
        copies.append(copy)

    for side, out in enumerate((near, far)):
        top = odd == 1 if side == 0 else odd == 0
        for name, width, parts in ROWS_A:
            first = jnp.where(top, 0, R - width)
            at = pl.ds(first, width)
            unit = rows[name, 0, 0]
            if name == "h":
                start(h_ref.at[0, at], out.at[unit : unit + width])
            elif name == "c":
                start(c_ref.at[0, at], cells.at[side])
            elif name == "t1":
                start(t_ref.at[0, 1, at], out.at[unit : unit + width])
            else:
                for row in range(width):
                    for part in range(parts):
                        start(x_ref.at[0, int(name[1]), first + row, :, quarter(part)], out.at[rows[name, row, part]])
    for copy in copies:
        copy.wait()
    for side, out in enumerate((near, far)):
        for row in range(2):
            out[rows["c", row, 0]] = cells[side, row].astype(BF)


def cols_a_kernel(h_ref, c_ref, x_ref, t_ref, near_r, far_r, near, far, above, below, left, right):
    row_odd, col_odd = parities()
    arranged(row_odd, near_r, far_r, above, below)

    def own(name, row, cells, part):
        if name == "h":
            return h_ref[0, row, cells]
        if name == "c":
            return c_ref[0, row, cells]
        if name == "t1":
            return t_ref[0, 1, row, cells]
        return x_ref[0, int(name[1]), row, cells, quarter(part)]

    pack_columns(ROWS_A, own, above, below, col_odd, near, far, left, right)


def cols_b_kernel(g_ref, q_ref, near_r, far_r, near, far, above, below, left, right):
    row_odd, col_odd = parities()
    arranged(row_odd, near_r, far_r, above, below)

    def own(name, row, cells, part):
        if name == "q":
            return q_ref[row, cells]
        return g_ref[row, cells, quarter(part)]

    pack_columns(ROWS_B, own, above, below, col_odd, near, far, left, right)


def cols_c_kernel(g_ref, near_r, far_r, near, far, above, below, left, right):
    row_odd, col_odd = parities()
    arranged(row_odd, near_r, far_r, above, below)

    def own(name, row, cells, part):
        return g_ref[row, cells, quarter(part)]

    pack_columns(ROWS_C, own, above, below, col_odd, near, far, left, right)


def unpack_columns(odd, near, far, left, right):
    @pl.when(odd == 1)
    def _():
        left[...] = near[...].astype(F32)
        right[...] = far[...].astype(F32)

    @pl.when(odd == 0)
    def _():
        left[...] = far[...].astype(F32)
        right[...] = near[...].astype(F32)


def border(at, width, left, right):
    cell = lax.broadcasted_iota(jnp.int32, (16, C), 0)
    out = jnp.zeros((16, C), F32)
    for i in range(width):
        out = jnp.where(cell == i, jnp.broadcast_to(right[at + i : at + i + 1, :], (16, C)), out)
        out = jnp.where(cell == 16 - width + i, jnp.broadcast_to(left[at + i : at + i + 1, :], (16, C)), out)
    return out


def widened_grads(spec, width, g_ref, above, below, left, right, gw):
    rows, _ = row_offsets(spec)
    cols, _ = col_offsets(spec)
    for row in range(R + 2 * width):
        fits = inside(width, row)
        for part in range(4):
            if row < width:
                mid = above[rows["g", row, part]]
            elif row >= R + width:
                mid = below[rows["g", row - R - width, part]]
            else:
                mid = g_ref[row - width, :, quarter(part)]
            full = jnp.concatenate([mid.astype(F32), border(cols["g", row, part], width, left, right)], axis=0)
            gw[row * W : (row + 1) * W, quarter(part)] = jnp.where(fits, full, 0.0).astype(BF)


def wrapped(n, z):
    def wrap(row, carry):
        z[0, row, 56:57, :] = z[0, row, 8:9, :]
        z[2, row, 7:8, :] = z[2, row, 55:56, :]
        return carry

    lax.fori_loop(0, n, wrap, 0)


def back(n, gw, w_ref, z):
    for side in range(3):
        z[side, 0:n, 8:56, :] = products(gw, w_ref, side, n, W).reshape(n, W, C)
    wrapped(n, z)


def summed(z, row, cells):
    return z[0, row, 9 : 9 + cells, :] + z[1, row, 8 : 8 + cells, :] + z[2, row, 7 : 7 + cells, :]


def last_kernel(g_ref, w_ref, near_r, far_r, near_c, far_c, dh_ref, above, below, left, right, gw, z):
    row_odd, col_odd = parities()
    arranged(row_odd, near_r, far_r, above, below)
    unpack_columns(col_odd, near_c, far_c, left, right)
    widened_grads(ROWS_C, 1, g_ref, above, below, left, right, gw)
    back(R, gw, w_ref, z)

    def one(row, carry):
        dh_ref[0, row] = summed(z, row, L).astype(BF)
        return carry

    lax.fori_loop(0, R, one, 0)


def set_member(core, place, half, j):
    near = jnp.where((place == 1) | (place == 2), 1, 0)
    kind = jnp.where(core == 0, near, place // 2)
    kind = jnp.where(half == 1, 1 - kind, kind)
    return jnp.where(core == 0, kind + j * (3 - 2 * kind), 2 * kind + j)


def turn(grads, turned, mine_ref, theirs_ref):
    core = lax.axis_index("core")
    for frame, g_ref in enumerate(grads):
        flat = g_ref[...].reshape(R * L, 4 * C).astype(F32)
        turned[:, quarter(frame)] = jnp.transpose(flat).astype(BF)

    place = {axis: lax.axis_index(axis) for axis in ("dp", "x")}

    def pick(block, carry):
        at = pl.ds(pl.multiple_of(block * 32, 32), 32)
        outer, inner = block // 4, block % 4
        for who, out in ((core, mine_ref), (1 - core, theirs_ref)):
            d = set_member(who, place["dp"], outer // 2, outer % 2)
            x = set_member(who, place["x"], inner // 2, inner % 2)
            out[at, :] = turned[pl.ds(pl.multiple_of(((d * 4 + x) * 2 + who) * 32, 32), 32), :]
        return carry

    lax.fori_loop(0, 16, pick, 0)


def own_sum_kernel(mine_ref, p_ref, out_ref):
    def one(n, carry):
        at = pl.ds(pl.multiple_of(n * 3 * C, C), 3 * C)
        out_ref[:, at] = jnp.dot(mine_ref[...], p_ref[:, at], preferred_element_type=F32)
        return carry

    lax.fori_loop(0, 3, one, 0)


def parted(rows, total, keep, send):
    for block in range(keep.shape[0] // rows):
        src = block * 2 * rows
        keep[block * rows : (block + 1) * rows, :] = total[src : src + rows].astype(BF)
        send[block * rows : (block + 1) * rows, :] = total[src + rows : src + 2 * rows].astype(BF)


def chip_sum_kernel(got_ref, p_ref, own_ref, keep0, send0, keep1, send1):
    for color, (rows, keep, send) in enumerate(((256, keep0, send0), (64, keep1, send1))):
        at = slice(color * HALF, (color + 1) * HALF)
        total = own_ref[:, at] + jnp.dot(got_ref[...], p_ref[:, at], preferred_element_type=F32)
        parted(rows, total, keep, send)


def halve_kernel(kept0, came0, kept1, came1, keep0, send0, keep1, send1):
    parted(64, kept0[...].astype(F32) + came0[...].astype(F32), keep0, send0)
    parted(128, kept1[...].astype(F32) + came1[...].astype(F32), keep1, send1)


def quarter_kernel(kept0, came0, kept1, came1, out_ref):
    out_ref[:, 0:HALF] = (kept0[...].astype(F32) + came0[...].astype(F32)).astype(BF)
    out_ref[:, HALF:] = (kept1[...].astype(F32) + came1[...].astype(F32)).astype(BF)


def total_kernel(parts_ref, out_ref):
    def one(i, carry):
        out_ref[...] = out_ref[...] + parts_ref[i].astype(F32)
        return carry

    out_ref[...] = jnp.zeros_like(out_ref)
    lax.fori_loop(0, 16, one, 0)


def inside(by, row):
    at_row = (lax.axis_index("x") * 2 + lax.axis_index("core")) * R + row - by
    cell = lax.broadcasted_iota(jnp.int32, (W, C), 0)
    column = jnp.where(cell < 40, cell, cell - W) + lax.axis_index("sx") * L
    fits = (column >= 0) & (column < 4 * L)
    return fits & jnp.broadcast_to((at_row >= 0) & (at_row < 8 * R), (W, C))


def sigmoid(value):
    return 0.5 * jnp.tanh(0.5 * value) + 0.5


def load_kernel(w_hbm, w_ref, sems):
    copies = [
        pltpu.make_async_copy(w_hbm.at[quarter(i)], w_ref.at[quarter(i)], sems.at[i]) for i in range(9)
    ]
    for copy in copies:
        copy.start()
    for copy in copies:
        copy.wait()


def ahead_kernel(h_ref, w_ref, near_r, far_r, out_ref, above, below, hs, shifted, wide):
    row_odd, _ = parities()
    arranged(row_odd, near_r, far_r, above, below)
    rows, _ = row_offsets(ROWS_A)
    n = R + 4
    hs[...] = jnp.zeros_like(hs)
    for row in range(R + 6):
        if row < 3:
            mid = above[rows["h", row, 0]]
        elif row >= R + 3:
            mid = below[rows["h", row - R - 3, 0]]
        else:
            mid = h_ref[0, row - 3]
        hs[row, 8:40, :] = jnp.where(inside(3, row)[0:L], mid.astype(F32), 0.0)
        for side in range(3):
            shifted[side, row] = hs[row, 7 + side : 39 + side, :].astype(BF)
    for k in range(9):
        up, side = k // 3, k % 3
        wide[:, quarter(k)] = shifted[side, up : up + n].reshape(n * L, C)

    def one(at_n, carry):
        at = pl.ds(pl.multiple_of(at_n * 2 * C, C), 2 * C)
        out_ref[:, at] = jnp.dot(wide[...], w_ref[:, at], preferred_element_type=F32)
        return carry

    lax.fori_loop(0, 2, one, 0)


def forward_kernel(count_ref, h_ref, c_ref, x_ref, t_ref, w_ref, main_ref, near_r, far_r, near_c, far_c,
                   seq_ref, patch_ref, m1_ref, m0_ref, t1_ref, g2_ref, q_ref, near_out, far_out,
                   above, below, left, right, hs, cs, gates, shifted, wide, edge, edge_gates):
    row_odd, col_odd = parities()
    count = count_ref[0]
    arranged(row_odd, near_r, far_r, above, below)

    unpack_columns(col_odd, near_c, far_c, left, right)

    rows, _ = row_offsets(ROWS_A)
    cols, _ = col_offsets(ROWS_A)
    widths = {name: width for name, width, _ in ROWS_A}

    def main(name, row, part):
        width = widths[name]
        if row < width:
            return above[rows[name, row, part]].astype(F32)
        if row >= R + width:
            return below[rows[name, row - R - width, part]].astype(F32)
        row -= width
        if name == "h":
            return h_ref[0, row].astype(F32)
        if name == "c":
            return c_ref[0, row]
        if name == "t1":
            return t_ref[0, 1, row].astype(F32)
        return x_ref[0, int(name[1]), row, :, quarter(part)].astype(F32)

    def sides(name, row, part):
        width = widths[name]
        at = cols[name, row, part]
        return right[at : at + width, :], left[at : at + width, :]

    zero16 = jnp.zeros((16, C), F32)
    hs[...] = jnp.zeros_like(hs)
    for row in range(R + 6):
        hs[row, 8:40, :] = main("h", row, 0)
        after, before = sides("h", row, 0)
        hs[row, 40:43, :] = after
        hs[row, 53:56, :] = before
        hs[row, 8:56, :] = jnp.where(inside(3, row), hs[row, 8:56, :], 0.0)
    for row in range(R + 4):
        cs[row, 0:32, :] = main("c", row, 0)
        cs[row, 32:48, :] = zero16
        after, before = sides("c", row, 0)
        cs[row, 32:34, :] = after
        cs[row, 46:48, :] = before

    def load_gates(name, by):
        for row in range(R + 2 * by):
            for part in range(4):
                at = row * W
                gates[at : at + 32, quarter(part)] = main(name, row, part)
                gates[at + 32 : at + W, quarter(part)] = zero16
                after, before = sides(name, row, part)
                gates[at + 32 : at + 32 + by, quarter(part)] = after
                gates[at + W - by : at + W, quarter(part)] = before

    def shift(n_rows):
        def one(row, carry):
            hs[row, 7:8, :] = hs[row, 55:56, :]
            hs[row, 56:58, :] = hs[row, 8:10, :]
            for side in range(3):
                shifted[side, row] = hs[row, 7 + side : 55 + side, :].astype(BF)
            return carry

        lax.fori_loop(0, n_rows, one, 0)

    def own_patches(frame, by):
        for k in range(9):
            up, side = k // 3, k % 3
            patch_ref[frame, :, quarter(k)] = shifted[side, by + up : by + up + R, 0:32, :].reshape(R * L, C)

    def merge(row, carry):
        cell = lax.broadcasted_iota(jnp.int32, (16, C), 0)
        at = pl.multiple_of(row * W, 16)
        for part in range(4):
            main = main_ref[pl.ds(pl.multiple_of(row * L, 16), L), quarter(part)]
            side = edge_gates[pl.ds(pl.multiple_of(row * 16, 16), 16), quarter(part)]

            def put(value, slot, source):
                return jnp.where(cell == slot, jnp.broadcast_to(side[source : source + 1], (16, C)), value)

            low = put(main[0:16], 0, 15)
            high = put(main[16:32], 15, 0)
            out = jnp.zeros((16, C), F32)
            for slot, source in ((0, 1), (1, 2), (14, 13), (15, 14)):
                out = put(out, slot, source)
            for i, value in enumerate((low, high, out)):
                cells = pl.ds(at + 16 * i, 16)
                gates[cells, quarter(part)] = gates[cells, quarter(part)] + value
        return carry

    for frame in range(3):
        by = 2 - frame
        n = R + 2 * by
        cells = n * W if by else R * L
        valid = frame < count
        wcols = W if by else L
        shift(n + 2)
        own_patches(frame, by)
        if frame == 0:
            load_gates("x0", by)
            for row in range(n + 2):
                for side in range(3):
                    near = hs[row, 38 + side : 46 + side, :]
                    far = hs[row, 48 + side : 56 + side, :]
                    edge[side, row] = jnp.concatenate([near, far], axis=0).astype(BF)
            for k in range(9):
                up, side = k // 3, k % 3
                wide[0 : n * 16, quarter(k)] = edge[side, up : up + n].reshape(n * 16, C)

            def one(at_n, carry):
                at = pl.ds(pl.multiple_of(at_n * 2 * C, C), 2 * C)
                edge_gates[:, at] = jnp.dot(wide[0 : 12 * 16, :], w_ref[:, at], preferred_element_type=F32)
                return carry

        elif by:
            load_gates("x1", by)
            for k in range(9):
                up, side = k // 3, k % 3
                wide[0:cells, quarter(k)] = shifted[side, up : up + n].reshape(cells, C)

            def one(at_n, carry, cells=cells):
                at = pl.ds(pl.multiple_of(at_n * 2 * C, C), 2 * C)
                gates[0:cells, at] = gates[0:cells, at] + jnp.dot(
                    wide[0:cells, :], w_ref[:, at], preferred_element_type=F32
                )
                return carry
        else:

            def one(at_n, carry):
                at = pl.ds(pl.multiple_of(at_n * 2 * C, C), 2 * C)
                gates[0 : R * L, at] = x_ref[0, 2, :, :, at].reshape(R * L, 2 * C).astype(F32) + jnp.dot(
                    patch_ref[2], w_ref[:, at], preferred_element_type=F32
                )
                return carry

        lax.fori_loop(0, 2, one, 0)
        if frame == 0:
            lax.fori_loop(0, n, merge, 0)

        def gating(row, carry, frame=frame, by=by, wcols=wcols, valid=valid):
            start = pl.multiple_of(row * wcols, 16)
            g = gates[pl.ds(start, wcols), :]
            si = sigmoid(g[:, 0:C])
            sf = sigmoid(g[:, C : 2 * C])
            tg = jnp.tanh(g[:, 2 * C : 3 * C])
            so = sigmoid(g[:, 3 * C :])
            cell = cs[row + (0 if frame == 0 else frame), 0:wcols, :]
            cell_new = sf * cell + si * tg
            tc = jnp.tanh(cell_new)
            h_new = (so * tc).astype(BF).astype(F32)
            factors = (
                so * (1.0 - tc * tc),
                tg * si * (1.0 - si),
                cell * sf * (1.0 - sf),
                si * (1.0 - tg * tg),
                tc * so * (1.0 - so),
                sf,
            )
            h_old = hs[row + 1, 8 : 8 + wcols, :]
            keep = jnp.broadcast_to(valid, h_new.shape)
            h_next = jnp.where(keep, h_new, h_old)
            cs[row + frame, 0:wcols, :] = jnp.where(keep, cell_new, cell)
            if by:
                hs[row, 8:56, :] = jnp.where(inside(by, row), h_next, 0.0)
            if frame == 0:

                @pl.when((row >= 2) & (row < 2 + R))
                def _():
                    seq_ref[0, 0, row - 2] = h_next[0:L].astype(BF)
                    for i, factor in enumerate(factors):
                        m0_ref[i, row - 2] = factor[0:L].astype(BF)
            elif frame == 1:
                for i, factor in enumerate(factors):
                    m1_ref[i, row] = factor.astype(BF)

                @pl.when((row >= 1) & (row < 1 + R))
                def _():
                    seq_ref[0, 1, row - 1] = h_next[0:L].astype(BF)
            else:
                seq_ref[0, 2, row] = h_next.astype(BF)
                a, bi, bfg, bg, bo, _ = factors
                grad_h = t_ref[0, 2, row].astype(F32)
                dc_new = grad_h * a
                for part, value in enumerate((dc_new * bi, dc_new * bfg, dc_new * bg, grad_h * bo)):
                    g2_ref[row, :, quarter(part)] = jnp.where(keep, value, 0.0).astype(BF)
                q_ref[row] = jnp.where(keep, dc_new * sf, grad_h)
            return carry

        lax.fori_loop(0, n, gating, 0)
    for row in range(R + 2):
        t1_ref[row, 0:32, :] = main("t1", row, 0).astype(BF)
        after, before = sides("t1", row, 0)
        cell = lax.broadcasted_iota(jnp.int32, (16, C), 0)
        pad = jnp.where(cell == 0, jnp.broadcast_to(after, (16, C)), jnp.where(cell == 15, jnp.broadcast_to(before, (16, C)), 0.0))
        t1_ref[row, 32:48, :] = pad.astype(BF)
    rows_b, _ = row_offsets(ROWS_B)
    for name, width, parts in ROWS_B:
        first = jnp.where(row_odd == 1, 0, R - width)
        last = jnp.where(row_odd == 1, R - width, 0)
        for row in range(width):
            for part in range(parts):
                unit = rows_b[name, row, part]
                for start, out in ((first, near_out), (last, far_out)):
                    if name == "q":
                        out[unit] = q_ref[start + row].astype(BF)
                    else:
                        out[unit] = g2_ref[start + row, :, quarter(part)]


def ahead_back_kernel(g_ref, w_ref, near_r, far_r, z_ref, above, below, gm):
    row_odd, _ = parities()
    arranged(row_odd, near_r, far_r, above, below)
    rows, _ = row_offsets(ROWS_B)
    for row in range(R + 4):
        fits = inside(2, row)[0:L]
        for part in range(4):
            if row < 2:
                mid = above[rows["g", row, part]]
            elif row >= R + 2:
                mid = below[rows["g", row - R - 2, part]]
            else:
                mid = g_ref[row - 2, :, quarter(part)]
            gm[row * L : (row + 1) * L, quarter(part)] = jnp.where(fits, mid.astype(F32), 0.0).astype(BF)
    n = R + 2
    for side in range(3):
        z_ref[side] = products(gm, w_ref, side, n, L).reshape(n, L, C)


def products(grads, w_ref, side, n, cells):
    total = None
    for up in range(3):
        k = up * 3 + side
        term = lax.dot_general(
            grads[(2 - up) * cells : (2 - up + n) * cells, :],
            w_ref[k * C : (k + 1) * C, :],
            (((1,), (1,)), ((), ())),
            preferred_element_type=F32,
        )
        total = term if total is None else total + term
    return total


def backward_kernel(count_ref, t0_ref, w_ref, zmain_ref, m1_ref, m0_ref, t1_ref, g2_ref, q_ref, near_r, far_r, near_c, far_c,
                    g1_ref, g0_ref, dh_ref, dc_ref, near_out, far_out, mine_ref, theirs_ref, above, below, left, right, gw, qs, z, turned, gb):
    row_odd, col_odd = parities()
    count = count_ref[0]
    arranged(row_odd, near_r, far_r, above, below)

    unpack_columns(col_odd, near_c, far_c, left, right)

    rows, _ = row_offsets(ROWS_B)
    cols, _ = col_offsets(ROWS_B)
    valid2, valid1 = 2 < count, 1 < count
    for row in range(R + 4):
        fits = inside(2, row)[L:W]
        for part in range(4):
            value = border(cols["g", row, part], 2, left, right)
            gb[row * 16 : (row + 1) * 16, quarter(part)] = jnp.where(fits, value, 0.0).astype(BF)
    for row in range(R + 2):
        if row < 1:
            mid = above[rows["q", 0, 0]].astype(F32)
        elif row >= R + 1:
            mid = below[rows["q", 0, 0]].astype(F32)
        else:
            mid = q_ref[row - 1]
        qs[row, 0:32, :] = mid
        qs[row, 32:48, :] = border(cols["q", row, 0], 1, left, right)

    for side in range(3):
        z[side, 0 : R + 2, 8:40, :] = zmain_ref[side]
        z[side, 0 : R + 2, 40:56, :] = products(gb, w_ref, side, R + 2, 16).reshape(R + 2, 16, C)
    wrapped(R + 2, z)

    def first(row, carry):
        keep2 = jnp.broadcast_to(valid2, (W, C))
        keep1 = jnp.broadcast_to(valid1, (W, C))
        q = qs[row]
        grad_h = jnp.where(keep2, summed(z, row, W), q) + t1_ref[row].astype(F32)
        grad_c = jnp.where(keep2, q, 0.0)
        a, bi, bfg, bg, bo, sf = (m1_ref[i, row].astype(F32) for i in range(6))
        dc_new = grad_c + grad_h * a
        keep = keep1 & inside(1, row)
        at = pl.ds(pl.multiple_of(row * W, W), W)
        for part, value in enumerate((dc_new * bi, dc_new * bfg, dc_new * bg, grad_h * bo)):
            gw[at, quarter(part)] = jnp.where(keep, value, 0.0).astype(BF)

        @pl.when((row >= 1) & (row < 1 + R))
        def _():
            dc_ref[0, row - 1] = jnp.where(keep1, dc_new * sf, grad_c)[0:L]
            dh_ref[0, row - 1] = grad_h[0:L]
            for part in range(4):
                g1_ref[row - 1, :, quarter(part)] = gw[pl.ds(pl.multiple_of(row * W, W), L), quarter(part)]

        return carry

    lax.fori_loop(0, R + 2, first, 0)
    back(R, gw, w_ref, z)

    def second(row, carry):
        keep1 = jnp.broadcast_to(valid1, (L, C))
        grad_h = jnp.where(keep1, summed(z, row, L), dh_ref[0, row]) + t0_ref[0, 0, row].astype(F32)
        a, bi, bfg, bg, bo, sf = (m0_ref[i, row].astype(F32) for i in range(6))
        dc_new = dc_ref[0, row] + grad_h * a
        for part, value in enumerate((dc_new * bi, dc_new * bfg, dc_new * bg, grad_h * bo)):
            g0_ref[row, :, quarter(part)] = value.astype(BF)
        dc_ref[0, row] = dc_new * sf
        return carry

    lax.fori_loop(0, R, second, 0)
    first_row = jnp.where(row_odd == 1, 0, R - 1)
    last_row = jnp.where(row_odd == 1, R - 1, 0)
    for part in range(4):
        near_out[part] = g0_ref[first_row, :, quarter(part)]
        far_out[part] = g0_ref[last_row, :, quarter(part)]
    turn((g0_ref, g1_ref, g2_ref), turned, mine_ref, theirs_ref)


def whole(shape):
    return pl.BlockSpec(shape, lambda _: (0,) * len(shape))


def call(kernel, inputs, outs, scratch, blocks=None, scalar=False, name=None, flops=0, limit=16, outside=()):
    blocks = blocks or {}
    specs = [whole(blocks.get(i, value.shape)) for i, value in enumerate(inputs)]
    inputs = list(inputs)
    for i in outside:
        specs[i] = pl.BlockSpec(memory_space=pltpu.HBM)
        inputs[i] = pltpu.with_memory_space_constraint(inputs[i], pltpu.HBM)
    if scalar:
        specs[0] = pl.BlockSpec(memory_space=pltpu.SMEM)
    size = sum(value.size * value.dtype.itemsize for value in inputs)
    return pl.pallas_call(
        kernel,
        grid=(1,),
        in_specs=specs,
        out_specs=[whole(out.shape) for out in outs],
        out_shape=outs,
        scratch_shapes=scratch,
        name=name,
        compiler_params=pltpu.CompilerParams(vmem_limit_bytes=limit << 20),
        cost_estimate=pl.CostEstimate(flops=flops, bytes_accessed=size, transcendentals=0),
    )(*inputs)


def swap_rows(near, far):
    axis = ("x", "core")
    return lax.ppermute(near, axis, ring_pairs(8, 0)), lax.ppermute(far, axis, ring_pairs(8, 1))


def swap_cols(near, far):
    return lax.ppermute(near, "sx", ring_pairs(4, 0)), lax.ppermute(far, "sx", ring_pairs(4, 1))


def first_partner(value, axis):
    flips = (1, 3)
    pairs = [(i * 2 + c, (i ^ flips[c]) * 2 + c) for i in range(4) for c in range(2)]
    return lax.ppermute(value, (axis, "core"), pairs)


def owner_groups():
    sets = (((0, 3), (1, 2)), ((0, 1), (2, 3)))
    return [
        [((d * 4 + x) * 2 + core) * 4 + y for d in ds for x in xs for y in range(4)]
        for core in range(2)
        for ds in sets[core]
        for xs in sets[core]
    ]


def body(input_gates, recur_weight, hidden_init, cell_init, hidden_cot, frame_count):
    width = C
    out = jax.ShapeDtypeStruct
    vmem = pltpu.VMEM
    _, row_units = row_offsets(ROWS_A)
    _, col_units = col_offsets(ROWS_A)
    first_two = {2: (1, 2, R, L, 4 * C)}
    border = out((row_units, L, C), BF)
    near, far = call(
        rows_a_kernel,
        (hidden_init, cell_init, input_gates, hidden_cot),
        [border] * 2,
        [vmem((2, 2, L, C), F32), pltpu.SemaphoreType.DMA((30,))],
        name="rows_a",
        outside=(0, 1, 2, 3),
    )
    near_r, far_r = swap_rows(near, far)
    weight_in, _ = lax.optimization_barrier((recur_weight, near))
    (recur_weight,) = call(
        load_kernel,
        (weight_in,),
        [out((9 * C, 4 * C), BF)],
        [pltpu.SemaphoreType.DMA((9,))],
        name="load",
        outside=(0,),
    )
    (own_gates,) = call(
        ahead_kernel,
        (hidden_init, recur_weight, near_r, far_r),
        [out(((R + 4) * L, 4 * C), F32)],
        [vmem((row_units, L, C), BF)] * 2
        + [vmem((R + 6, 64, C), F32), vmem((3, R + 6, L, C), BF), vmem(((R + 4) * L, 9 * C), BF)],
        name="ahead",
        flops=2 * 10**9,
    )
    strip = out((col_units, C), BF)
    near, far = call(
        cols_a_kernel,
        (hidden_init, cell_init, input_gates, hidden_cot, near_r, far_r),
        [strip] * 2,
        [vmem((row_units, L, C), BF)] * 2 + [vmem((col_units, C), F32)] * 2,
        first_two,
        name="cols_a",
    )
    near_c, far_c = swap_cols(near, far)
    _, row_units_b = row_offsets(ROWS_B)
    _, col_units_b = col_offsets(ROWS_B)
    hidden_seq, patches, m1, m0, t1, g2, q, near, far = call(
        forward_kernel,
        (frame_count, hidden_init, cell_init, input_gates, hidden_cot, recur_weight, own_gates, near_r, far_r, near_c, far_c),
        [
            out((1, 3, R, L, C), BF),
            out((3, R * L, 9 * C), BF),
            out((6, R + 2, W, C), BF),
            out((6, R, L, C), BF),
            out((R + 2, W, C), BF),
            out((R, L, 4 * C), BF),
            out((R, L, C), F32),
            out((row_units_b, L, C), BF),
            out((row_units_b, L, C), BF),
        ],
        [vmem((row_units, L, C), BF)] * 2
        + [vmem((col_units, C), F32)] * 2
        + [
            vmem((R + 6, 64, C), F32),
            vmem((R + 4, W, C), F32),
            vmem(((R + 4) * W, 4 * C), F32),
            vmem((3, R + 6, W, C), BF),
            vmem(((R + 4) * W, 9 * C), BF),
            vmem((3, R + 6, 16, C), BF),
            vmem(((R + 4) * 16, 4 * C), F32),
        ],
        scalar=True,
        name="forward",
        limit=30,
        flops=6 * 10**9,
    )
    near_r, far_r = swap_rows(near, far)
    flat_patches = patches.reshape(3 * R * L, 9 * C)
    other_patches = lax.ppermute(flat_patches, "core", CORES)
    (zmain,) = call(
        ahead_back_kernel,
        (g2, recur_weight, near_r, far_r),
        [out((3, R + 2, L, C), F32)],
        [vmem((row_units_b, L, C), BF)] * 2 + [vmem(((R + 4) * L, 4 * C), BF)],
        name="ahead_back",
        flops=2 * 10**9,
    )
    strip = out((col_units_b, C), BF)
    near, far = call(
        cols_b_kernel,
        (g2, q, near_r, far_r),
        [strip] * 2,
        [vmem((row_units_b, L, C), BF)] * 2 + [vmem((col_units_b, C), F32)] * 2,
        name="cols_b",
    )
    near_c, far_c = swap_cols(near, far)
    g1, g0, _, cell_grad, near_c_rows, far_c_rows, mine, theirs = call(
        backward_kernel,
        (frame_count, hidden_cot, recur_weight, zmain, m1, m0, t1, g2, q, near_r, far_r, near_c, far_c),
        [out((R, L, 4 * C), BF), out((R, L, 4 * C), BF), out((1, R, L, C), F32), out((1, R, L, C), F32),
         out((4, L, C), BF), out((4, L, C), BF), out((512, 3 * C), BF), out((512, 3 * C), BF)],
        [vmem((row_units_b, L, C), BF)] * 2
        + [vmem((col_units_b, C), F32)] * 2
        + [vmem(((R + 4) * W, 4 * C), BF), vmem((R + 2, W, C), F32), vmem((3, R + 2, 64, C), F32), vmem((4 * C, 3 * C), BF), vmem(((R + 4) * 16, 4 * C), BF)],
        {1: (1, 1, R, L, C)},
        scalar=True,
        name="backward",
        limit=24,
        flops=4 * 10**9,
    )
    _, col_units_c = col_offsets(ROWS_C)
    near_r, far_r = swap_rows(near_c_rows, far_c_rows)
    got = lax.ppermute(theirs, "core", CORES)
    (own_sum,) = call(own_sum_kernel, (mine, flat_patches), [out((512, 9 * C), F32)], [], name="own_sum", flops=2 * 10**9)
    sent = call(
        chip_sum_kernel,
        (got, other_patches, own_sum),
        [out((256, HALF), BF)] * 4,
        [],
        name="chip_sum",
        flops=2 * 10**9,
    )
    strip = out((col_units_c, C), BF)
    near, far = call(
        cols_c_kernel,
        (g0, near_r, far_r),
        [strip] * 2,
        [vmem((4, L, C), BF)] * 2 + [vmem((col_units_c, C), F32)] * 2,
        name="cols_c",
    )
    came = first_partner(sent[1], "dp"), first_partner(sent[3], "x")
    near, far, *came = lax.optimization_barrier((near, far, *came))
    sent = call(halve_kernel, (sent[0], came[0], sent[2], came[1]), [out((128, HALF), BF)] * 4, [], name="halve")
    came = first_partner(sent[1], "x"), first_partner(sent[3], "dp")
    near_c, far_c = swap_cols(near, far)
    *came, near_c, far_c = lax.optimization_barrier((*came, near_c, far_c))
    (blocks,) = call(
        quarter_kernel, (sent[0], came[0], sent[2], came[1]), [out((128, 9 * C), BF)], [], name="quarter"
    )
    (hidden_grad,) = call(
        last_kernel,
        (g0, recur_weight, near_r, far_r, near_c, far_c),
        [out((1, R, L, C), BF)],
        [vmem((4, L, C), BF)] * 2
        + [vmem((col_units_c, C), F32)] * 2
        + [vmem(((R + 2) * W, 4 * C), BF), vmem((3, R, 64, C), F32)],
        name="last",
        flops=2 * 10**9,
    )
    parts = lax.all_to_all(blocks, AXES, 0, 0, tiled=True, axis_index_groups=owner_groups())
    (total,) = call(total_kernel, (parts.reshape(16, 8, 9 * C),), [out((8, 9 * C), F32)], [], name="total")
    weight_grad = total.T
    gate_grad = jnp.stack([g0, g1, g2])[None]
    return (hidden_seq, weight_grad, gate_grad, hidden_grad, cell_grad)


def solution(mesh):
    split = Mesh(mesh.devices.reshape(4, 4, 2, 4), ("dp", "x", "core", "sx"))
    sy = ("x", "core")
    step = jax.shard_map(
        body,
        mesh=split,
        in_specs=(
            P("dp", None, sy, "sx", None),
            P(),
            P("dp", sy, "sx", None),
            P("dp", sy, "sx", None),
            P("dp", None, sy, "sx", None),
            P("dp"),
        ),
        out_specs=(
            P("dp", None, sy, "sx", None),
            P(None, ("dp", "x", "core", "sx")),
            P("dp", None, sy, "sx", None),
            P("dp", sy, "sx", None),
            P("dp", sy, "sx", None),
        ),
        check_vma=False,
    )
    return step
```
